128 devices in a mesh: dom: 128 (over x, y, z, core).
Axes of the slice: x: 4, y: 4, z: 4, core: 2. Of those that a mesh axis runs over, the one named last changes fastest.
Arguments:
- traction: float32 [65536, 3, 128], P('dom'), may hold values from -6 to 6
- fluid_coords: float32 [65536, 3, 128], P('dom'), may hold values from 0 to 1
- struct_coords: float32 [3, 32, 16384], P(None, None, 'dom'), may hold values from 0 to 1
- dest: int32 [65536, 1], P('dom'), may hold values from 0 to 127; in each aligned block of 512 rows (0 to 511, 512 to 1023, ...) at most 8 rows name the same one
- target: int32 [65536], P('dom'), may hold values from 0 to 127
- blocks: float32 [3, 96, 96, 16384], P(None, None, None, 'dom'), may hold values from -1 to 7, as said below
- columns: int32 [2, 16384], P(None, 'dom'), may hold values from 0 to 159
- halo_list: int32 [2048], P('dom'), may hold values from 0 to 127
- precond: float32 [96, 96, 16384], P(None, None, 'dom'), may hold values from -1 to 1
Outputs:
- load_field: float32 [96, 16384], P(None, 'dom')
- solution: float32 [96, 16384], P(None, 'dom')
- residual: float32 [96, 16384], P(None, 'dom')
The draws below stay inside these ranges and needn't reach their ends.
Inputs may be any that keep to these rules, and one draw needn't show every extreme that they name: `dest`: among the fluid blocks of one partition no partition is named more than 8 times, a bound that some block reaches. Each diagonal block is its positive diagonal plus small full entries; coupling blocks are small full blocks.
All inputs are finite; a program needn't handle non-finite values.
Results may differ from the reference program's by a relative error of at most 0.0003.
Values sent between devices are 32-bit elements; how exact they have to be, the bound alone decides.
No kernel may reach another device: no remote copies, remote signals or barrier semaphores. Data moves between devices by JAX's collectives and lax.ppermute only.
A program may use at most 128 MiB of HBM per device.

```python
import math
import jax
import jax.numpy as jnp
import numpy as np
from jax import lax

NODES = 128
CLUSTER = 96
SNODE = 32
FB_DEV = 512
SB_DEV = 128
HB = 16
ITERS = 2
PARTS_SIZE = 128
CAP = 8
FBLK = 65536
NBLK = 16384
HALO_ALL = 2048
N_DOM = 128


def draw_blocks(key, part):
    key_jitter, key_scale = jax.random.split(jax.random.fold_in(key, 11))
    random_part = jnp.clip(jax.random.normal(key_jitter, (3, CLUSTER, CLUSTER, NBLK), jnp.float32), -3.0, 3.0)
    random_part = random_part * (0.5 / math.sqrt(3 * CLUSTER))
    scales = jnp.exp(jax.random.uniform(key_scale, (CLUSTER, NBLK), jnp.float32, math.log(2.0), math.log(6.0)))
    identity = jnp.eye(CLUSTER, dtype=jnp.float32)
    diagonal_part = identity[:, :, None] * scales[:, None, :]
    return random_part.at[0].add(diagonal_part)


def draw_precond(key, part):
    key_jitter, key_scale = jax.random.split(jax.random.fold_in(key, 13))
    random_part = jnp.clip(jax.random.normal(key_jitter, (CLUSTER, CLUSTER, NBLK), jnp.float32), -3.0, 3.0)
    random_part = random_part * (0.1 / math.sqrt(CLUSTER))
    scales = jnp.exp(jax.random.uniform(key_scale, (CLUSTER, NBLK), jnp.float32, math.log(0.15), math.log(0.5)))
    identity = jnp.eye(CLUSTER, dtype=jnp.float32)
    return random_part + identity[:, :, None] * scales[:, None, :]


def touch_ends(values, stream_key, low, high):
    place = [jax.random.randint(jax.random.fold_in(stream_key, axis), (), 0, length) for axis, length in enumerate(values.shape)]
    widest = values.shape.index(max(values.shape))
    next_to = place[:widest] + [(place[widest] + 1) % values.shape[widest]] + place[widest + 1:]
    return values.at[tuple(place)].set(low).at[tuple(next_to)].set(high)


def levels(stream_key, extent, cuts, smallest, high):
    loudness, own = 1.0, jax.random.fold_in(stream_key, 6)
    for dim, parts in cuts:
        heights = jnp.exp(jax.random.uniform(jax.random.fold_in(own, dim), (parts,), jnp.float32, smallest / len(cuts), high / len(cuts)))
        loudness = loudness * jnp.repeat(heights, extent[dim] // parts).reshape([-1 if axis == dim else 1 for axis in range(len(extent))])
    return loudness


def deal_out(key, own, number, rows, count, top, most, lean):
    sequence = jax.random.permutation(key, count)
    packed, usual = load_shares(count, rows * top, most, lean, True), load_shares(count, rows * top, most, lean, False)
    places = jnp.arange(count)

    def named(sizes, offset_by):
        used = int((sizes > 0).sum())
        fixed = max(1, used // 4)
        passed = fixed + (places - fixed + offset_by * (used - fixed)) % max(1, count - fixed)
        return jnp.zeros((count,), jnp.int32).at[sequence[jnp.where(places < fixed, places, passed)]].set(jnp.asarray(sizes, jnp.int32))

    sizes = jnp.where(number % 4 == 0, named(packed, number // 4), named(usual, number - number // 4 - 1))
    mixed = jax.random.permutation(jax.random.fold_in(own, 3), count)
    giver, receiver = mixed[0:count // 2 * 2:2], mixed[1:count // 2 * 2:2]
    slack = jnp.minimum(sizes[giver] - 1, most - sizes[receiver]) // 2
    slack = jnp.where((giver == sequence[0]) | (receiver == sequence[0]) | (sizes[receiver] == 0), 0, jnp.maximum(slack, 0))
    passed = jax.random.randint(jax.random.fold_in(own, 4), (count // 2,), 0, 1 << 20) % (slack + 1)
    sizes = sizes.at[giver].add(-passed).at[receiver].add(passed)
    members = jnp.searchsorted(jnp.cumsum(sizes), jnp.arange(rows * top), side="right").astype(jnp.int32)
    listing = members.reshape(top, rows).T
    listing = listing[jax.random.permutation(jax.random.fold_in(own, 1), rows)]
    offset_by = jax.random.randint(jax.random.fold_in(own, 2), (rows, 1), 0, top)
    return jnp.take_along_axis(listing, (jnp.arange(top)[None, :] + offset_by) % top, axis=1)


def load_shares(number_of, total, most, lean, full):
    portions = [(1 << 20) // math.isqrt(rank ** lean) + 1 for rank in range(1, number_of + 1)]
    largest = most if full else min(most, max(-(-total // number_of), total * portions[0] // sum(portions)))
    least = 1 if total - largest >= number_of - 1 else 0
    given, spare = [largest] + [least] * (number_of - 1), total - largest - least * (number_of - 1)
    while spare > 0:
        candidates = [i for i in range(1, number_of) if given[i] < largest] or [i for i in range(1, number_of) if given[i] < most]
        mass, remaining = sum([portions[i] for i in candidates]), spare
        for i in candidates:
            more = min(most - given[i], max(1, remaining * portions[i] // mass), spare)
            given[i] = given[i] + more
            spare = spare - more
    return np.array(given)


def bell_draw(own_key, extent, width, reach, pieces=(), kind=jnp.bfloat16):
    gain = levels(own_key, extent, pieces, -0.22, 0.18) if pieces else 1.0
    values = jax.random.normal(own_key, extent, jnp.float32) * width * gain
    return jnp.minimum(jnp.maximum(values, -reach), reach).astype(kind)


def setup_inputs(seed: int = 0) -> dict:
    streams_of = jax.random.split(jax.random.key(seed), 10)
    traction = bell_draw(streams_of[0], (FBLK, 3, NODES), 1.0, 6.0, ((0, 128),), jnp.float32)
    fluid_coords = jnp.clip(1.0 * jax.random.uniform(streams_of[1], (FBLK, 3, NODES), jnp.float32) ** levels(streams_of[1], (FBLK, 3, NODES), ((0, 128),), -0.2, 0.2), 0.0, 1.0)
    struct_coords = jnp.clip(1.0 * jax.random.uniform(streams_of[2], (3, SNODE, NBLK), jnp.float32) ** levels(streams_of[2], (3, SNODE, NBLK), ((2, 128),), -0.2, 0.2), 0.0, 1.0)
    dest_keys = jax.random.split(jax.random.fold_in(streams_of[3], 1), FBLK // FB_DEV)
    dest_turns = jax.random.permutation(jax.random.fold_in(streams_of[3], 3), FBLK // FB_DEV)
    dest = jax.vmap(lambda own, number: deal_out(jax.random.fold_in(streams_of[3], 2), own, number, FB_DEV, PARTS_SIZE, 1, CAP, 1))(dest_keys, dest_turns).reshape((FBLK, 1))
    target = touch_ends(jax.random.randint(streams_of[4], (FBLK,), 0, SB_DEV), jax.random.fold_in(streams_of[4], 1), 0, SB_DEV - 1).astype(jnp.int32)
    blocks = draw_blocks(jax.random.fold_in(streams_of[9], 71), 0)
    columns = touch_ends(jax.random.randint(streams_of[6], (2, NBLK), 0, SB_DEV + 2 * HB), jax.random.fold_in(streams_of[6], 1), 0, (SB_DEV + 2 * HB) - 1).astype(jnp.int32)
    halo_list = touch_ends(jax.random.randint(streams_of[7], (HALO_ALL,), 0, SB_DEV), jax.random.fold_in(streams_of[7], 1), 0, SB_DEV - 1).astype(jnp.int32)
    precond = draw_precond(jax.random.fold_in(streams_of[9], 71), 0)
    return dict(traction=traction, fluid_coords=fluid_coords, struct_coords=struct_coords, dest=dest, target=target, blocks=blocks, columns=columns, halo_list=halo_list, precond=precond)


support = 0.9

def wendland_map(fluid_pos, force, struct_pos):
    dist_sq = jnp.zeros((fluid_pos.shape[0], struct_pos.shape[2], fluid_pos.shape[2]), jnp.float32)
    for component in range(3):
        dist_sq = dist_sq + (struct_pos[:, component, :, None] - fluid_pos[:, component, None, :]) ** 2
    radius = jnp.sqrt(dist_sq) / support
    weight = jnp.maximum(1.0 - radius, 0.0) ** 4 * (4.0 * radius + 1.0)
    mapped = jnp.einsum('bjn,bcn->bcj', weight, force, precision=lax.Precision.HIGHEST)
    return mapped.reshape(mapped.shape[0], -1)

def precondition(precond, vector):
    return jnp.einsum('abi,bi->ai', precond, vector, precision=lax.Precision.HIGHEST)

def apply_operator(vector, blocks, columns, halo_list):
    per_part = jnp.transpose(vector.reshape(CLUSTER, N_DOM, SB_DEV), (1, 0, 2))
    listed = halo_list.reshape(N_DOM, HB)
    outgoing = jnp.take_along_axis(per_part, listed[:, None, :], axis=2)
    zero_rim = jnp.zeros_like(outgoing[:1])
    from_left = jnp.concatenate([zero_rim, outgoing[:-1]], axis=0)
    from_right = jnp.concatenate([outgoing[1:], zero_rim], axis=0)
    extended = jnp.concatenate([per_part, from_left, from_right], axis=2)
    result = jnp.einsum('abi,bi->ai', blocks[0], vector, precision=lax.Precision.HIGHEST)
    for neighbor in range(2):
        picks = columns[neighbor].reshape(N_DOM, 1, SB_DEV)
        taken = jnp.take_along_axis(extended, picks, axis=2)
        taken = jnp.transpose(taken, (1, 0, 2)).reshape(CLUSTER, NBLK)
        result = result + jnp.einsum('abi,bi->ai', blocks[neighbor + 1], taken, precision=lax.Precision.HIGHEST)
    return result

def reference(traction, fluid_coords, struct_coords, dest, target, blocks, columns, halo_list, precond):
    global_index = (dest[:, 0] * SB_DEV + target).astype(jnp.int32)

    def per_device(device_index):
        start = (device_index * FB_DEV).astype(jnp.int32)
        positions = lax.dynamic_slice_in_dim(fluid_coords, start, FB_DEV, 0)
        forces = lax.dynamic_slice_in_dim(traction, start, FB_DEV, 0)
        picked = lax.dynamic_slice_in_dim(global_index, start, FB_DEV, 0)
        struct_pos = jnp.transpose(jnp.take(struct_coords, picked, axis=2), (2, 0, 1))
        return wendland_map(positions, forces, struct_pos)
    mapped = lax.map(per_device, jnp.arange(N_DOM, dtype=jnp.int32)).reshape(FBLK, CLUSTER)
    load_field = jax.ops.segment_sum(mapped, global_index, num_segments=NBLK).T
    solution = jnp.zeros_like(load_field)
    residual = load_field
    shadow = load_field
    search = load_field
    alignment = jnp.sum(shadow * residual)
    for step in range(ITERS):
        search_pre = precondition(precond, search)
        image = apply_operator(search_pre, blocks, columns, halo_list)
        step_size = alignment / jnp.sum(shadow * image)
        middle = residual - step_size * image
        middle_pre = precondition(precond, middle)
        middle_image = apply_operator(middle_pre, blocks, columns, halo_list)
        smoothing = jnp.sum(middle_image * middle) / jnp.sum(middle_image * middle_image)
        solution = solution + step_size * search_pre + smoothing * middle_pre
        residual = middle - smoothing * middle_image
        new_alignment = jnp.sum(shadow * residual)
        momentum = new_alignment / alignment * (step_size / smoothing)
        search = residual + momentum * (search - smoothing * image)
        alignment = new_alignment
    return (load_field, solution, residual)
```

```python
import jax
import jax.numpy as jnp
from jax import lax
from jax.experimental import pallas as pl
from jax.experimental.pallas import tpu as pltpu
from jax.sharding import Mesh
from jax.sharding import PartitionSpec as P

DOM = ("dom_0", "dom_1", "dom_2", "dom_3")
SUPPORT = 0.9
CAP = 8
LANES = 128
STEPS = 4
F32 = jnp.float32
BF16 = jnp.bfloat16
NN = (((1,), (0,)), ((), ()))
NT = (((1,), (1,)), ((), ()))
TN = (((0,), (0,)), ((), ()))


def iota(shape, dim):
    return lax.broadcasted_iota(jnp.int32, shape, dim)


def flag(mask):
    return jnp.where(mask, 1.0, 0.0).astype(BF16)


def split3(x):
    high = x.astype(BF16)
    rest = x - high.astype(F32)
    mid = rest.astype(BF16)
    low = (rest - mid.astype(F32)).astype(BF16)
    return high, mid, low


def dot(a, b, dims):
    return lax.dot_general(a, b, dims, preferred_element_type=F32)


def pick(x, onehot, dims):
    return sum(dot(part, onehot, dims) for part in reversed(split3(x)))


def pick_from(onehot, x, dims):
    return sum(dot(onehot, part, dims) for part in reversed(split3(x)))


def pad_rows(x, rows):
    if x.shape[0] == rows:
        return x
    return jnp.concatenate([x, jnp.zeros((rows - x.shape[0], x.shape[1]), x.dtype)], axis=0)


def slots_kernel(dest_ref, target_ref, labels_ref, slot_ref):
    dest = dest_ref[...]
    count = dest.shape[1]
    parts = labels_ref.shape[0]
    hits = flag(iota((parts, count), 0) == dest)
    earlier = flag(iota((count, count), 0) < iota((count, count), 1))
    running = dot(hits, earlier, NN)
    before = jnp.sum(running * hits.astype(F32), axis=0, keepdims=True)
    slot_ref[...] = dest * CAP + before.astype(jnp.int32)
    place = iota((LANES, count), 0).astype(F32)
    wanted = jnp.where(place == before, (target_ref[...] + 1).astype(F32), 0.0)
    labels_ref[...] = dot(hits, wanted.astype(BF16), NT)


def slots(dest, target, parts):
    count = dest.shape[1]
    return pl.pallas_call(
        slots_kernel,
        out_shape=(
            jax.ShapeDtypeStruct((parts, LANES), F32),
            jax.ShapeDtypeStruct((1, count), jnp.int32),
        ),
        name="slots",
    )(dest, target)


def answer_kernel(labels_ref, coords_ref, onehot_ref, out_ref):
    rows = out_ref.shape[0]
    parts = labels_ref.shape[0]
    repeat = flag(iota((rows, parts), 0) // CAP == iota((rows, parts), 1))
    spread = dot(repeat, labels_ref[...].astype(BF16), NN)
    own = iota((rows, LANES), 0) % CAP == iota((rows, LANES), 1)
    own_label = jnp.where(own, spread, 0.0).astype(BF16)
    label = dot(own_label, jnp.ones((LANES, LANES), BF16), NN)
    onehot = flag(label == (iota((rows, LANES), 1) + 1).astype(F32))
    onehot_ref[...] = onehot
    out_ref[...] = pick_from(onehot, pad_rows(coords_ref[...], LANES), NT)


def answer(labels, coords):
    rows = labels.shape[0] * CAP
    return pl.pallas_call(
        answer_kernel,
        out_shape=(
            jax.ShapeDtypeStruct((rows, LANES), BF16),
            jax.ShapeDtypeStruct((rows, LANES), F32),
        ),
        name="answer",
    )(labels, coords)


def transfer_kernel(slot_ref, coords_ref, fluid_ref, force_ref, out_ref, turned, struct, mapped):
    rows = coords_ref.shape[0]
    count = slot_ref.shape[1]
    chosen = flag(iota((rows, count), 0) == slot_ref[...])
    struct[...] = pick(coords_ref[...], chosen, TN) * (1.0 / SUPPORT)
    nodes = fluid_ref.shape[2]
    for group in range(count // LANES):
        lanes = pl.ds(group * LANES, LANES)
        for c in range(3):
            turned[c] = fluid_ref[c, lanes, :].T * (1.0 / SUPPORT)
            turned[3 + c] = force_ref[c, lanes, :].T * 4.0
        where = [struct[pl.ds(c * 32, 32), lanes] for c in range(3)]

        def body(step, sums):
            sums = list(sums)
            for k in range(8):
                n = pl.ds(step * 8 + k, 1)
                apart = [where[c] - turned[c, n, :] for c in range(3)]
                square = apart[0] * apart[0] + apart[1] * apart[1] + apart[2] * apart[2]
                square = jnp.maximum(square, 1e-30)
                left = jnp.maximum(1.0 - square * lax.rsqrt(square), 0.0)
                twice = left * left
                quarter = twice * twice * (1.25 - left)
                for c in range(3):
                    sums[c] = sums[c] + quarter * turned[3 + c, n, :]
            return tuple(sums)

        zero = jnp.zeros((32, LANES), F32)
        sums = lax.fori_loop(0, nodes // 8, body, (zero, zero, zero))
        for c in range(3):
            mapped[pl.ds(c * 32, 32), lanes] = sums[c]
    mapped[pl.ds(96, 32), :] = jnp.zeros((32, count), F32)
    out_ref[...] = pick_from(chosen, mapped[...], NT)


def transfer(slot, coords, fluid, force):
    count = slot.shape[1]
    return pl.pallas_call(
        transfer_kernel,
        out_shape=jax.ShapeDtypeStruct(coords.shape, F32),
        scratch_shapes=[
            pltpu.VMEM((6, fluid.shape[2], LANES), F32),
            pltpu.VMEM((LANES, count), F32),
            pltpu.VMEM((LANES, count), F32),
        ],
        name="transfer",
    )(slot, coords, fluid, force)


def times(matrix, vectors, put):
    rows = vectors[0].shape[0]

    def body(step, carry):
        for k in range(8):
            row = step * 8 + k
            total = None
            for index, vector in enumerate(vectors):
                term = matrix(index, row) * vector
                total = term if total is None else total + term
            put(row, jnp.sum(total, axis=0, keepdims=True))
        return carry

    lax.fori_loop(0, rows // 8, body, 0)


def precondition(precond_ref, vector, out_ref):
    def put(row, value):
        out_ref[pl.ds(row, 1), :] = value

    times(lambda _, row: precond_ref[row], [vector], put)


def listed(halo_ref, vector):
    count = halo_ref.shape[0]
    rows = iota((count, LANES), 0)
    column = jnp.zeros((count, LANES), jnp.int32)
    for h in range(count):
        column = jnp.where(rows == h, halo_ref[h], column)
    onehot = flag(column == iota((count, LANES), 1))
    return pick_from(onehot, pad_rows(vector, LANES), NT)


def start_kernel(halo_ref, mapped_ref, onehot_ref, precond_ref, load_ref, pre_ref, send_ref):
    load = pick(mapped_ref[...], onehot_ref[...], TN)[: load_ref.shape[0]]
    load_ref[...] = load
    precondition(precond_ref, load, pre_ref)
    send_ref[...] = listed(halo_ref, pre_ref[...])


SMEM = pl.BlockSpec(memory_space=pltpu.SMEM)
VMEM = pl.BlockSpec(memory_space=pltpu.VMEM)


def start(halo_list, mapped, onehot, precond):
    shape = jax.ShapeDtypeStruct((precond.shape[0], LANES), F32)
    send = jax.ShapeDtypeStruct((halo_list.shape[0], LANES), F32)
    return pl.pallas_call(
        start_kernel,
        out_shape=(shape, shape, send),
        in_specs=[SMEM, VMEM, VMEM, VMEM],
        name="start",
    )(halo_list, mapped, onehot, precond)


def apply(parity_ref, columns_ref, blocks_ref, old, pre, near_ref, far_ref, out_ref):
    size = pre.shape[0]
    count = near_ref.shape[0]
    halo = jnp.concatenate([near_ref[...], far_ref[...]], axis=0)
    flip = (1 - parity_ref[0]) * count
    vectors = [pre]
    for neighbor in range(2):
        column = columns_ref[pl.ds(neighbor, 1), :]
        local = flag(iota((LANES, LANES), 0) == column)
        outside = flag(iota((2 * count, LANES), 0) == ((column - LANES) ^ flip))
        taken = pick(pre, local, NN) + pick(halo, outside, TN)[:size]
        vectors.append(taken)

    def put(row, value):
        out_ref[pl.ds(row, 1), :] = value

    times(lambda index, row: blocks_ref[index, row], vectors, put)
    out_ref[...] = out_ref[...] - old


def step_kernel(
    parity_ref, halo_ref, columns_ref, blocks_ref, precond_ref, old_ref, pre_ref, near_ref, far_ref,
    new_ref, new_pre_ref, send_ref,
):
    apply(parity_ref, columns_ref, blocks_ref, old_ref[...], pre_ref[...], near_ref, far_ref, new_ref)
    precondition(precond_ref, new_ref[...], new_pre_ref)
    send_ref[...] = listed(halo_ref, new_pre_ref[...])


def step(parity, halo_list, columns, blocks, precond, old, pre, near, far):
    shape = jax.ShapeDtypeStruct(old.shape, F32)
    return pl.pallas_call(
        step_kernel,
        out_shape=(shape, shape, jax.ShapeDtypeStruct(near.shape, F32)),
        in_specs=[SMEM, SMEM] + [VMEM] * 7,
        name="step",
    )(parity, halo_list, columns, blocks, precond, old, pre, near, far)


PAIRS = [(i, j) for i in range(STEPS + 1) for j in range(i, STEPS + 1)]


def last_kernel(
    parity_ref, columns_ref, blocks_ref, basis_ref, pre_ref, near_ref, far_ref, new_ref, sums_ref
):
    apply(
        parity_ref, columns_ref, blocks_ref, basis_ref[STEPS - 1], pre_ref[...], near_ref, far_ref, new_ref
    )
    vectors = [basis_ref[j] for j in range(STEPS)] + [new_ref[...]]
    sums = [jnp.sum(vectors[i] * vectors[j], axis=0, keepdims=True) for i, j in PAIRS]
    sums.append(jnp.zeros((LANES - len(sums), LANES), F32))
    ones = jnp.ones((sums_ref.shape[0], LANES), BF16)
    sums_ref[...] = pick_from(ones, jnp.concatenate(sums, axis=0), NT)


def last(parity, columns, blocks, basis, pre, near, far, parts):
    shape = jax.ShapeDtypeStruct(pre.shape, F32)
    return pl.pallas_call(
        last_kernel,
        out_shape=(shape, jax.ShapeDtypeStruct((parts, LANES), F32)),
        in_specs=[SMEM] + [VMEM] * 6,
        name="last",
    )(parity, columns, blocks, basis, pre, near, far)


def plus(x, y):
    return [a + b for a, b in zip(x, y)]


def scaled(scale, x):
    return [scale * a for a in x]


def recurrences(product):
    def inner(x, y):
        return sum(
            a * b * product[min(i, j), max(i, j)]
            for i, a in enumerate(x)
            for j, b in enumerate(y)
        )

    def image_of(x):
        return plus([x[0] * 0.0] + x, x + [x[0] * 0.0])

    one = product[0, 0] * 0.0 + 1.0
    residual = search = shadow = [one]
    answer = []
    alignment = product[0, 0]

    def add(x, y):
        size = max(len(x), len(y))
        zero = one * 0.0
        return plus(x + [zero] * (size - len(x)), y + [zero] * (size - len(y)))

    for iteration in range(2):
        image = image_of(search)
        step_size = alignment / inner(shadow, image)
        middle = add(residual, scaled(-step_size, image))
        middle_image = image_of(middle)
        smoothing = inner(middle_image, middle) / inner(middle_image, middle_image)
        answer = add(answer, add(scaled(step_size, search), scaled(smoothing, middle)))
        residual = add(middle, scaled(-smoothing, middle_image))
        if iteration == 0:
            new_alignment = inner(shadow, residual)
            momentum = new_alignment / alignment * (step_size / smoothing)
            search = add(residual, scaled(momentum, add(search, scaled(-smoothing, image))))
            alignment = new_alignment
    return answer, residual


def finish_kernel(sums_ref, basis_ref, new_ref, pre_ref, solution_ref, residual_ref):
    totals = jnp.sum(sums_ref[...], axis=0, keepdims=True)
    product = {pair: totals[:, k : k + 1] for k, pair in enumerate(PAIRS)}
    answer, residual = recurrences(product)
    vectors = [basis_ref[j] for j in range(STEPS)] + [new_ref[...]]
    solution_ref[...] = sum(a * pre_ref[j] for j, a in enumerate(answer))
    residual_ref[...] = sum(a * v for a, v in zip(residual, vectors))


def finish(sums, basis, new, pre):
    shape = jax.ShapeDtypeStruct(new.shape, F32)
    return pl.pallas_call(finish_kernel, out_shape=(shape, shape), name="finish")(sums, basis, new, pre)


def exchange(send):
    devices = lax.axis_size(DOM)
    near = lax.ppermute(send, DOM, [(i, i ^ 1) for i in range(devices)])
    send, near = lax.optimization_barrier((send, near))
    odd = range(1, devices - 1, 2)
    far = lax.ppermute(send, DOM, [(i, i + 1) for i in odd] + [(i + 1, i) for i in odd])
    return near, far


def to_all(x):
    return lax.all_to_all(x, DOM, split_axis=0, concat_axis=0, tiled=True)


def on_device(
    traction, fluid_coords, struct_coords, dest, target, blocks, columns, halo_list, precond
):
    parts = lax.axis_size(DOM)
    force = jnp.transpose(traction, (1, 0, 2))
    fluid = jnp.transpose(fluid_coords, (1, 0, 2))
    coords = struct_coords.reshape(-1, struct_coords.shape[2])
    labels, slot = slots(dest.reshape(1, -1), target.reshape(1, -1), parts)
    labels = to_all(labels)
    onehot, answered = answer(labels, coords)
    answered = to_all(answered.reshape(parts, CAP, LANES)).reshape(parts * CAP, LANES)
    mapped = transfer(slot, answered, fluid, force)
    mapped = to_all(mapped.reshape(parts, CAP, LANES)).reshape(parts * CAP, LANES)
    load, pre, send = start(halo_list, mapped, onehot, precond)
    parity = lax.axis_index("dom_3").astype(jnp.int32).reshape(1)
    basis, pres = [load], [pre]
    for _ in range(STEPS - 1):
        near, far = exchange(send)
        new, pre, send = step(
            parity, halo_list, columns, blocks, precond, basis[-1], pres[-1], near, far
        )
        basis.append(new)
        pres.append(pre)
    near, far = exchange(send)
    basis = jnp.stack(basis)
    new, sums = last(parity, columns, blocks, basis, pre, near, far, parts)
    solution, residual = finish(to_all(sums), basis, new, jnp.stack(pres))
    return load, solution, residual


def solution(mesh):
    finer = Mesh(mesh.devices.reshape(4, 4, 4, 2), DOM)
    in_specs = (
        P(DOM, None, None),
        P(DOM, None, None),
        P(None, None, DOM),
        P(DOM, None),
        P(DOM),
        P(None, None, None, DOM),
        P(None, DOM),
        P(DOM),
        P(None, None, DOM),
    )
    out_specs = (P(None, DOM), P(None, DOM), P(None, DOM))
    return jax.shard_map(
        on_device, mesh=finer, in_specs=in_specs, out_specs=out_specs, check_vma=False
    )
```

```python
import jax
import jax.numpy as jnp
from jax import lax
from jax.experimental import pallas as pl
from jax.experimental.pallas import tpu as pltpu
from jax.sharding import Mesh
from jax.sharding import PartitionSpec as P

DOM = ("dom_0", "dom_1", "dom_2", "dom_3")
SUPPORT = 0.9
CAP = 8
LANES = 128
STEPS = 4
F32 = jnp.float32
BF16 = jnp.bfloat16
NN = (((1,), (0,)), ((), ()))
NT = (((1,), (1,)), ((), ()))
TN = (((0,), (0,)), ((), ()))


SMEM = pl.BlockSpec(memory_space=pltpu.SMEM)
VMEM = pl.BlockSpec(memory_space=pltpu.VMEM)
ANY = pl.BlockSpec(memory_space=pl.ANY)
MIB = 1 << 20


def limit(mib):
    return pltpu.CompilerParams(vmem_limit_bytes=mib * MIB)


def near_core(*arrays):
    return [pltpu.with_memory_space_constraint(x, pltpu.VMEM) for x in arrays]


def in_hbm(*arrays):
    return [pltpu.with_memory_space_constraint(x, pltpu.HBM) for x in arrays]


def iota(shape, dim):
    return lax.broadcasted_iota(jnp.int32, shape, dim)


def flag(mask):
    return jnp.where(mask, 1.0, 0.0).astype(BF16)


def split3(x):
    high = x.astype(BF16)
    rest = x - high.astype(F32)
    mid = rest.astype(BF16)
    low = (rest - mid.astype(F32)).astype(BF16)
    return high, mid, low


def dot(a, b, dims):
    return lax.dot_general(a, b, dims, preferred_element_type=F32)


def pick(x, onehot, dims):
    return sum(dot(part, onehot, dims) for part in reversed(split3(x)))


def pick_from(onehot, x, dims):
    return sum(dot(onehot, part, dims) for part in reversed(split3(x)))


def pad_rows(x, rows):
    if x.shape[0] == rows:
        return x
    return jnp.concatenate([x, jnp.zeros((rows - x.shape[0], x.shape[1]), x.dtype)], axis=0)


def slots_kernel(dest_ref, target_ref, labels_ref, slot_ref):
    dest = dest_ref[...]
    count = dest.shape[1]
    parts = labels_ref.shape[0]
    hits = flag(iota((parts, count), 0) == dest)
    earlier = flag(iota((count, count), 0) < iota((count, count), 1))
    running = dot(hits, earlier, NN)
    before = jnp.sum(running * hits.astype(F32), axis=0, keepdims=True)
    slot_ref[...] = dest * CAP + before.astype(jnp.int32)
    place = iota((LANES, count), 0).astype(F32)
    wanted = jnp.where(place == before, (target_ref[...] + 1).astype(F32), 0.0)
    labels_ref[...] = dot(hits, wanted.astype(BF16), NT)


def slots(dest, target, parts):
    count = dest.shape[1]
    return pl.pallas_call(
        slots_kernel,
        out_shape=(
            jax.ShapeDtypeStruct((parts, LANES), F32),
            jax.ShapeDtypeStruct((1, count), jnp.int32),
        ),
        compiler_params=limit(2),
        name="slots",
    )(dest, target)


def prepare_kernel(
    halo_ref, parity_ref, columns_ref, after_ref, fluid_ref, force_ref,
    turned_ref, local_ref, outer_ref, listed_ref,
    points, sems,
):
    copies = [
        pltpu.make_async_copy(ref, points.at[k], sems.at[k])
        for k, ref in enumerate((fluid_ref, force_ref))
    ]
    for copy in copies:
        copy.start()
    flip = (1 - parity_ref[0]) * listed_ref.shape[0]
    for neighbor in range(2):
        column = columns_ref[pl.ds(neighbor, 1), :]
        local_ref[neighbor] = flag(iota((LANES, LANES), 0) == column)
        outer_ref[neighbor] = flag(iota(outer_ref.shape[1:], 0) == ((column - LANES) ^ flip))
    rows = iota(listed_ref.shape, 0)
    column = jnp.zeros(listed_ref.shape, jnp.int32)
    for h in range(listed_ref.shape[0]):
        column = jnp.where(rows == h, halo_ref[h], column)
    listed_ref[...] = flag(column == iota(listed_ref.shape, 1))
    for copy in copies:
        copy.wait()
    for group in range(points.shape[2] // LANES):
        lanes = pl.ds(group * LANES, LANES)
        for kind, factor in enumerate((1.0 / SUPPORT, 4.0)):
            for c in range(3):
                turned_ref[group, 3 * kind + c] = points[kind, c, lanes, :].T * factor


def prepare(halo_list, parity, columns, after, fluid, force):
    count, nodes = fluid.shape[1:]
    halo = halo_list.shape[0]
    return pl.pallas_call(
        prepare_kernel,
        out_shape=(
            pltpu.VMEM((count // LANES, 6, nodes, LANES), F32),
            pltpu.VMEM((2, LANES, LANES), BF16),
            pltpu.VMEM((2, 2 * halo, LANES), BF16),
            pltpu.VMEM((halo, LANES), BF16),
        ),
        in_specs=[SMEM, SMEM, VMEM] + [ANY] * 3,
        out_specs=[VMEM] * 4,
        scratch_shapes=[pltpu.VMEM((2, 3, count, nodes), F32), pltpu.SemaphoreType.DMA((2,))],
        compiler_params=limit(4),
        cost_estimate=pl.CostEstimate(flops=0, bytes_accessed=3 * MIB, transcendentals=0),
        name="prepare",
    )(halo_list, parity, columns, *in_hbm(after, fluid, force))


def answer_kernel(labels_ref, coords_ref, after_ref, onehot_ref, out_ref):
    rows = out_ref.shape[0]
    parts = labels_ref.shape[0]
    repeat = flag(iota((rows, parts), 0) // CAP == iota((rows, parts), 1))
    spread = dot(repeat, labels_ref[...].astype(BF16), NN)
    own = iota((rows, LANES), 0) % CAP == iota((rows, LANES), 1)
    own_label = jnp.where(own, spread, 0.0).astype(BF16)
    label = dot(own_label, jnp.ones((LANES, LANES), BF16), NN)
    onehot = flag(label == (iota((rows, LANES), 1) + 1).astype(F32))
    onehot_ref[...] = onehot
    out_ref[...] = pick_from(onehot, pad_rows(coords_ref[...], LANES), NT)


def answer(labels, coords, after):
    rows = labels.shape[0] * CAP
    return pl.pallas_call(
        answer_kernel,
        out_shape=(
            jax.ShapeDtypeStruct((rows, LANES), BF16),
            jax.ShapeDtypeStruct((rows, LANES), F32),
        ),
        in_specs=[VMEM, VMEM, ANY],
        compiler_params=limit(6),
        name="answer",
    )(labels, coords, after)


def transfer_kernel(
    slot_ref, coords_ref, turned_ref, blocks_ref, precond_ref, out_ref, blocks_out, precond_out,
    struct, mapped, sems,
):
    tables = [
        pltpu.make_async_copy(precond_ref, precond_out, sems.at[0]),
        pltpu.make_async_copy(blocks_ref, blocks_out, sems.at[1]),
    ]
    for copy in tables:
        copy.start()
    rows = coords_ref.shape[0]
    count = slot_ref.shape[1]
    chosen = flag(iota((rows, count), 0) == slot_ref[...])
    struct[...] = pick(coords_ref[...], chosen, TN) * (1.0 / SUPPORT)
    nodes = turned_ref.shape[2]
    for group in range(count // LANES):
        lanes = pl.ds(group * LANES, LANES)
        where = [struct[pl.ds(c * 32, 32), lanes] for c in range(3)]

        def body(step, sums):
            sums = list(sums)
            for k in range(8):
                n = pl.ds(step * 8 + k, 1)
                apart = [where[c] - turned_ref[group, c, n, :] for c in range(3)]
                square = apart[0] * apart[0] + apart[1] * apart[1] + apart[2] * apart[2]
                square = jnp.maximum(square, 1e-30)
                left = jnp.maximum(1.0 - square * lax.rsqrt(square), 0.0)
                twice = left * left
                quarter = twice * twice * (1.25 - left)
                for c in range(3):
                    sums[c] = sums[c] + quarter * turned_ref[group, 3 + c, n, :]
            return tuple(sums)

        zero = jnp.zeros((32, LANES), F32)
        sums = lax.fori_loop(0, nodes // 8, body, (zero, zero, zero))
        for c in range(3):
            mapped[pl.ds(c * 32, 32), lanes] = sums[c]
    mapped[pl.ds(96, 32), :] = jnp.zeros((32, count), F32)
    out_ref[...] = pick_from(chosen, mapped[...], NT)
    for copy in tables:
        copy.wait()


def transfer(slot, coords, turned, blocks, precond):
    count = slot.shape[1]
    return pl.pallas_call(
        transfer_kernel,
        out_shape=(
            jax.ShapeDtypeStruct(coords.shape, F32),
            pltpu.VMEM(blocks.shape, F32),
            pltpu.VMEM(precond.shape, F32),
        ),
        in_specs=[VMEM] * 3 + [ANY] * 2,
        out_specs=[VMEM] * 3,
        scratch_shapes=[
            pltpu.VMEM((LANES, count), F32),
            pltpu.VMEM((LANES, count), F32),
            pltpu.SemaphoreType.DMA((2,)),
        ],
        compiler_params=limit(10),
        name="transfer",
    )(slot, coords, *near_core(turned), *in_hbm(blocks, precond))


def times(matrices, vectors, put):
    rows = vectors[0].shape[0]

    def body(step, carry):
        for k in range(8):
            row = step * 8 + k
            total = None
            for matrix, vector in zip(matrices, vectors):
                term = matrix[row] * vector
                total = term if total is None else total + term
            put(row, jnp.sum(total, axis=0, keepdims=True))
        return carry

    lax.fori_loop(0, rows // 8, body, 0)


def precondition(precond_ref, listed_ref, vector, out_ref, send_ref):
    def put(row, value):
        out_ref[pl.ds(row, 1), :] = value

    times([precond_ref], [vector], put)
    send_ref[...] = pick_from(listed_ref[...], pad_rows(out_ref[...], LANES), NT)


def start_kernel(mapped_ref, onehot_ref, precond_ref, listed_ref, load_ref, pre_ref, send_ref):
    load = pick(mapped_ref[...], onehot_ref[...], TN)[: load_ref.shape[0]]
    load_ref[...] = load
    precondition(precond_ref, listed_ref, load, pre_ref, send_ref)


def start(mapped, onehot, precond, listed):
    shape = pltpu.VMEM((precond.shape[0], LANES), F32)
    return pl.pallas_call(
        start_kernel,
        out_shape=(shape, shape, pltpu.VMEM(listed.shape, F32)),
        in_specs=[VMEM] * 4,
        out_specs=[VMEM] * 3,
        compiler_params=limit(6),
        name="start",
    )(mapped, onehot, *near_core(precond, listed))


def inside_kernel(blocks_ref, local_ref, outer_ref, old_ref, pre_ref, near_ref, part_ref, taken_ref):
    pre = pre_ref[...]
    size = pre.shape[0]
    count = near_ref.shape[0]

    def put(row, value):
        part_ref[pl.ds(row, 1), :] = value - old_ref[pl.ds(row, 1), :]

    times([blocks_ref.at[0]], [pre], put)
    for neighbor in range(2):
        taken = pick(pre, local_ref[neighbor], NN)
        taken_ref[neighbor] = taken + pick(near_ref[...], outer_ref[neighbor, :count, :], TN)[:size]


def inside(blocks, local, outer, old, pre, near):
    size = old.shape[0]
    return pl.pallas_call(
        inside_kernel,
        out_shape=(pltpu.VMEM(old.shape, F32), pltpu.VMEM((2, size, LANES), F32)),
        in_specs=[VMEM] * 6,
        out_specs=[VMEM] * 2,
        compiler_params=limit(6),
        cost_estimate=pl.CostEstimate(flops=0, bytes_accessed=2 * MIB, transcendentals=0),
        name="inside",
    )(*near_core(blocks, local, outer, old, pre, near))


def outside(blocks_ref, outer_ref, part_ref, taken_ref, far_ref, new_ref):
    size = part_ref.shape[0]
    count = far_ref.shape[0]
    vectors = [
        taken_ref[neighbor] + pick(far_ref[...], outer_ref[neighbor, count:, :], TN)[:size]
        for neighbor in range(2)
    ]

    def put(row, value):
        new_ref[pl.ds(row, 1), :] = value + part_ref[pl.ds(row, 1), :]

    times([blocks_ref.at[1], blocks_ref.at[2]], vectors, put)


def step_kernel(
    blocks_ref, precond_ref, outer_ref, listed_ref, part_ref, taken_ref, far_ref,
    new_ref, new_pre_ref, send_ref,
):
    outside(blocks_ref, outer_ref, part_ref, taken_ref, far_ref, new_ref)
    precondition(precond_ref, listed_ref, new_ref[...], new_pre_ref, send_ref)


def step(blocks, precond, outer, listed, part, taken, far):
    shape = pltpu.VMEM(part.shape, F32)
    return pl.pallas_call(
        step_kernel,
        out_shape=(shape, shape, pltpu.VMEM(far.shape, F32)),
        in_specs=[VMEM] * 7,
        out_specs=[VMEM] * 3,
        compiler_params=limit(6),
        name="step",
    )(*near_core(blocks, precond, outer, listed, part, taken, far))


PAIRS = [(i, j) for i in range(STEPS + 1) for j in range(i, STEPS + 1)]


def last_kernel(
    blocks_ref, outer_ref, part_ref, taken_ref, far_ref, b0_ref, b1_ref, b2_ref, b3_ref,
    new_ref, sums_ref,
):
    outside(blocks_ref, outer_ref, part_ref, taken_ref, far_ref, new_ref)
    vectors = [ref[...] for ref in (b0_ref, b1_ref, b2_ref, b3_ref, new_ref)]
    sums = [jnp.sum(vectors[i] * vectors[j], axis=0, keepdims=True) for i, j in PAIRS]
    sums.append(jnp.zeros((LANES - len(sums), LANES), F32))
    ones = jnp.ones((sums_ref.shape[0], LANES), BF16)
    sums_ref[...] = pick_from(ones, jnp.concatenate(sums, axis=0), NT)


def last(blocks, outer, part, taken, far, basis, parts):
    return pl.pallas_call(
        last_kernel,
        out_shape=(pltpu.VMEM(part.shape, F32), pltpu.VMEM((parts, LANES), F32)),
        in_specs=[VMEM] * 9,
        out_specs=[VMEM] * 2,
        compiler_params=limit(6),
        name="last",
    )(*near_core(blocks, outer, part, taken, far, *basis))


def plus(x, y):
    return [a + b for a, b in zip(x, y)]


def scaled(scale, x):
    return [scale * a for a in x]


def recurrences(product):
    def inner(x, y):
        return sum(
            a * b * product[min(i, j), max(i, j)]
            for i, a in enumerate(x)
            for j, b in enumerate(y)
        )

    def image_of(x):
        return plus([x[0] * 0.0] + x, x + [x[0] * 0.0])

    one = product[0, 0] * 0.0 + 1.0
    residual = search = shadow = [one]
    answer = []
    alignment = product[0, 0]

    def add(x, y):
        size = max(len(x), len(y))
        zero = one * 0.0
        return plus(x + [zero] * (size - len(x)), y + [zero] * (size - len(y)))

    for iteration in range(2):
        image = image_of(search)
        step_size = alignment / inner(shadow, image)
        middle = add(residual, scaled(-step_size, image))
        middle_image = image_of(middle)
        smoothing = inner(middle_image, middle) / inner(middle_image, middle_image)
        answer = add(answer, add(scaled(step_size, search), scaled(smoothing, middle)))
        residual = add(middle, scaled(-smoothing, middle_image))
        if iteration == 0:
            new_alignment = inner(shadow, residual)
            momentum = new_alignment / alignment * (step_size / smoothing)
            search = add(residual, scaled(momentum, add(search, scaled(-smoothing, image))))
            alignment = new_alignment
    return answer, residual


def finish_kernel(sums_ref, *refs):
    basis, pres, (solution_ref, residual_ref) = refs[:5], refs[5:9], refs[9:]
    totals = jnp.sum(sums_ref[...], axis=0, keepdims=True)
    product = {pair: totals[:, k : k + 1] for k, pair in enumerate(PAIRS)}
    answer, residual = recurrences(product)
    solution_ref[...] = sum(a * ref[...] for a, ref in zip(answer, pres))
    residual_ref[...] = sum(a * ref[...] for a, ref in zip(residual, basis))


def finish(sums, basis, pres):
    shape = jax.ShapeDtypeStruct(pres[0].shape, F32)
    return pl.pallas_call(
        finish_kernel,
        out_shape=(shape, shape),
        in_specs=[VMEM] * 10,
        compiler_params=limit(4),
        name="finish",
    )(*near_core(sums, *basis, *pres))


def to_near(send):
    devices = lax.axis_size(DOM)
    return lax.ppermute(send, DOM, [(i, i ^ 1) for i in range(devices)])


def to_far(send):
    odd = range(1, lax.axis_size(DOM) - 1, 2)
    return lax.ppermute(send, DOM, [(i, i + 1) for i in odd] + [(i + 1, i) for i in odd])


def to_all(x):
    return lax.all_to_all(x, DOM, split_axis=0, concat_axis=0, tiled=True)


def on_device(
    traction, fluid_coords, struct_coords, dest, target, blocks, columns, halo_list, precond
):
    parts = lax.axis_size(DOM)
    parity = lax.axis_index("dom_3").astype(jnp.int32).reshape(1)
    force = jnp.transpose(traction, (1, 0, 2))
    fluid = jnp.transpose(fluid_coords, (1, 0, 2))
    coords = struct_coords.reshape(-1, struct_coords.shape[2])
    wanted, slot = slots(dest.reshape(1, -1), target.reshape(1, -1), parts)
    turned, local, outer, listed = prepare(halo_list, parity, columns, wanted, fluid, force)
    onehot, answered = answer(to_all(wanted), coords, listed)
    answered = to_all(answered.reshape(parts, CAP, LANES)).reshape(parts * CAP, LANES)
    mapped, blocks, precond = transfer(slot, answered, turned, blocks, precond)
    mapped = to_all(mapped.reshape(parts, CAP, LANES)).reshape(parts * CAP, LANES)
    load, pre, send = start(mapped, onehot, precond, listed)
    basis, pres = [load], [pre]
    for j in range(STEPS):
        near = to_near(send)
        send, near = lax.optimization_barrier((send, near))
        far = to_far(send)
        part, taken = inside(blocks, local, outer, basis[-1], pres[-1], near)
        if j < STEPS - 1:
            new, pre, send = step(blocks, precond, outer, listed, part, taken, far)
            pres.append(pre)
        else:
            new, sums = last(blocks, outer, part, taken, far, basis, parts)
        basis.append(new)
    solution, residual = finish(to_all(sums), basis, pres)
    return load, solution, residual


def solution(mesh):
    finer = Mesh(mesh.devices.reshape(4, 4, 4, 2), DOM)
    in_specs = (
        P(DOM, None, None),
        P(DOM, None, None),
        P(None, None, DOM),
        P(DOM, None),
        P(DOM),
        P(None, None, None, DOM),
        P(None, DOM),
        P(DOM),
        P(None, None, DOM),
    )
    out_specs = (P(None, DOM), P(None, DOM), P(None, DOM))
    return jax.shard_map(
        on_device, mesh=finer, in_specs=in_specs, out_specs=out_specs, check_vma=False
    )
```

```python
import jax
import jax.numpy as jnp
from jax import lax
from jax.experimental import pallas as pl
from jax.experimental.pallas import tpu as pltpu
from jax.sharding import Mesh
from jax.sharding import PartitionSpec as P

DOM = ("dom_0", "dom_1", "dom_2", "dom_3")
SUPPORT = 0.9
CAP = 8
LANES = 128
STEPS = 4
F32 = jnp.float32
BF16 = jnp.bfloat16
NN = (((1,), (0,)), ((), ()))
NT = (((1,), (1,)), ((), ()))
TN = (((0,), (0,)), ((), ()))


SMEM = pl.BlockSpec(memory_space=pltpu.SMEM)
VMEM = pl.BlockSpec(memory_space=pltpu.VMEM)
ANY = pl.BlockSpec(memory_space=pl.ANY)
MIB = 1 << 20


def limit(mib):
    return pltpu.CompilerParams(vmem_limit_bytes=mib * MIB)


def near_core(*arrays):
    return [pltpu.with_memory_space_constraint(x, pltpu.VMEM) for x in arrays]


def in_hbm(*arrays):
    return [pltpu.with_memory_space_constraint(x, pltpu.HBM) for x in arrays]


def iota(shape, dim):
    return lax.broadcasted_iota(jnp.int32, shape, dim)


def flag(mask):
    return jnp.where(mask, 1.0, 0.0).astype(BF16)


def split3(x):
    high = x.astype(BF16)
    rest = x - high.astype(F32)
    mid = rest.astype(BF16)
    low = (rest - mid.astype(F32)).astype(BF16)
    return high, mid, low


def dot(a, b, dims):
    return lax.dot_general(a, b, dims, preferred_element_type=F32)


def pick(x, onehot, dims):
    return sum(dot(part, onehot, dims) for part in reversed(split3(x)))


def pick_from(onehot, x, dims):
    return sum(dot(onehot, part, dims) for part in reversed(split3(x)))


def pad_rows(x, rows):
    if x.shape[0] == rows:
        return x
    return jnp.concatenate([x, jnp.zeros((rows - x.shape[0], x.shape[1]), x.dtype)], axis=0)


def slots_kernel(dest_ref, target_ref, labels_ref, slot_ref):
    dest = dest_ref[...]
    count = dest.shape[1]
    parts = labels_ref.shape[0]
    hits = flag(iota((parts, count), 0) == dest)
    earlier = flag(iota((count, count), 0) < iota((count, count), 1))
    running = dot(hits, earlier, NN)
    before = jnp.sum(running * hits.astype(F32), axis=0, keepdims=True)
    slot_ref[...] = dest * CAP + before.astype(jnp.int32)
    place = iota((LANES, count), 0).astype(F32)
    wanted = jnp.where(place == before, (target_ref[...] + 1).astype(F32), 0.0)
    labels_ref[...] = dot(hits, wanted.astype(BF16), NT)


def slots(dest, target, parts):
    count = dest.shape[1]
    return pl.pallas_call(
        slots_kernel,
        out_shape=(
            jax.ShapeDtypeStruct((parts, LANES), F32),
            jax.ShapeDtypeStruct((1, count), jnp.int32),
        ),
        compiler_params=limit(2),
        name="slots",
    )(*in_hbm(dest, target))


def prepare_kernel(
    halo_ref, parity_ref, columns_ref, coords_ref, after_ref, fluid_ref, force_ref,
    turned_ref, coords_out, local_ref, outer_ref, listed_ref,
    points, sems,
):
    copies = [
        pltpu.make_async_copy(ref, points.at[k], sems.at[k])
        for k, ref in enumerate((fluid_ref, force_ref))
    ]
    for copy in copies:
        copy.start()
    coords_out[...] = pad_rows(coords_ref[...], LANES)
    flip = (1 - parity_ref[0]) * listed_ref.shape[0]
    for neighbor in range(2):
        column = columns_ref[pl.ds(neighbor, 1), :]
        local_ref[neighbor] = flag(iota((LANES, LANES), 0) == column)
        outer_ref[neighbor] = flag(iota(outer_ref.shape[1:], 0) == ((column - LANES) ^ flip))
    rows = iota(listed_ref.shape, 0)
    column = jnp.zeros(listed_ref.shape, jnp.int32)
    for h in range(listed_ref.shape[0]):
        column = jnp.where(rows == h, halo_ref[h], column)
    listed_ref[...] = flag(column == iota(listed_ref.shape, 1))
    for copy in copies:
        copy.wait()
    for group in range(points.shape[2] // LANES):
        lanes = pl.ds(group * LANES, LANES)
        for kind, factor in enumerate((1.0 / SUPPORT, 4.0)):
            for c in range(3):
                turned_ref[group, 3 * kind + c] = points[kind, c, lanes, :].T * factor


def prepare(halo_list, parity, columns, coords, after, fluid, force):
    count, nodes = fluid.shape[1:]
    halo = halo_list.shape[0]
    return pl.pallas_call(
        prepare_kernel,
        out_shape=(
            pltpu.VMEM((count // LANES, 6, nodes, LANES), F32),
            pltpu.VMEM((LANES, LANES), F32),
            pltpu.VMEM((2, LANES, LANES), BF16),
            pltpu.VMEM((2, 2 * halo, LANES), BF16),
            pltpu.VMEM((halo, LANES), BF16),
        ),
        in_specs=[SMEM, SMEM, VMEM, VMEM] + [ANY] * 3,
        out_specs=[VMEM] * 5,
        scratch_shapes=[pltpu.VMEM((2, 3, count, nodes), F32), pltpu.SemaphoreType.DMA((2,))],
        compiler_params=limit(4),
        cost_estimate=pl.CostEstimate(flops=0, bytes_accessed=3 * MIB, transcendentals=0),
        name="prepare",
    )(*in_hbm(halo_list, parity, columns, coords, after, fluid, force))


def answer_kernel(labels_ref, coords_ref, onehot_ref, out_ref):
    rows = out_ref.shape[0]
    parts = labels_ref.shape[0]
    repeat = flag(iota((rows, parts), 0) // CAP == iota((rows, parts), 1))
    spread = dot(repeat, labels_ref[...].astype(BF16), NN)
    own = iota((rows, LANES), 0) % CAP == iota((rows, LANES), 1)
    own_label = jnp.where(own, spread, 0.0).astype(BF16)
    label = dot(own_label, jnp.ones((LANES, LANES), BF16), NN)
    onehot = flag(label == (iota((rows, LANES), 1) + 1).astype(F32))
    onehot_ref[...] = onehot
    out_ref[...] = pick_from(onehot, coords_ref[...], NT)


def answer(labels, coords):
    rows = labels.shape[0] * CAP
    return pl.pallas_call(
        answer_kernel,
        out_shape=(
            jax.ShapeDtypeStruct((rows, LANES), BF16),
            jax.ShapeDtypeStruct((rows, LANES), F32),
        ),
        in_specs=[VMEM, VMEM],
        compiler_params=limit(6),
        name="answer",
    )(labels, *near_core(coords))


def transfer_kernel(
    slot_ref, coords_ref, turned_ref, blocks_ref, precond_ref, out_ref, blocks_out, precond_out,
    struct, mapped, sems,
):
    tables = [
        pltpu.make_async_copy(precond_ref, precond_out, sems.at[0]),
        pltpu.make_async_copy(blocks_ref, blocks_out, sems.at[1]),
    ]
    for copy in tables:
        copy.start()
    rows = coords_ref.shape[0]
    count = slot_ref.shape[1]
    chosen = flag(iota((rows, count), 0) == slot_ref[...])
    struct[...] = pick(coords_ref[...], chosen, TN) * (1.0 / SUPPORT)
    nodes = turned_ref.shape[2]
    for group in range(count // LANES):
        lanes = pl.ds(group * LANES, LANES)
        where = [struct[pl.ds(c * 32, 32), lanes] for c in range(3)]

        def body(step, sums):
            sums = list(sums)
            for k in range(8):
                n = pl.ds(step * 8 + k, 1)
                apart = [where[c] - turned_ref[group, c, n, :] for c in range(3)]
                square = apart[0] * apart[0] + apart[1] * apart[1] + apart[2] * apart[2]
                square = jnp.maximum(square, 1e-30)
                left = jnp.maximum(1.0 - square * lax.rsqrt(square), 0.0)
                twice = left * left
                quarter = twice * twice * (1.25 - left)
                for c in range(3):
                    sums[c] = sums[c] + quarter * turned_ref[group, 3 + c, n, :]
            return tuple(sums)

        zero = jnp.zeros((32, LANES), F32)
        sums = lax.fori_loop(0, nodes // 8, body, (zero, zero, zero))
        for c in range(3):
            mapped[pl.ds(c * 32, 32), lanes] = sums[c]
    mapped[pl.ds(96, 32), :] = jnp.zeros((32, count), F32)
    out_ref[...] = pick_from(chosen, mapped[...], NT)
    for copy in tables:
        copy.wait()


def transfer(slot, coords, turned, blocks, precond):
    count = slot.shape[1]
    return pl.pallas_call(
        transfer_kernel,
        out_shape=(
            jax.ShapeDtypeStruct(coords.shape, F32),
            pltpu.VMEM(blocks.shape, F32),
            pltpu.VMEM(precond.shape, F32),
        ),
        in_specs=[VMEM] * 3 + [ANY] * 2,
        out_specs=[VMEM] * 3,
        scratch_shapes=[
            pltpu.VMEM((LANES, count), F32),
            pltpu.VMEM((LANES, count), F32),
            pltpu.SemaphoreType.DMA((2,)),
        ],
        compiler_params=limit(10),
        name="transfer",
    )(slot, coords, *near_core(turned), *in_hbm(blocks, precond))


def times(matrices, vectors, put):
    rows = vectors[0].shape[0]

    def body(step, carry):
        for k in range(8):
            row = step * 8 + k
            total = None
            for matrix, vector in zip(matrices, vectors):
                term = matrix[row] * vector
                total = term if total is None else total + term
            put(row, jnp.sum(total, axis=0, keepdims=True))
        return carry

    lax.fori_loop(0, rows // 8, body, 0)


def precondition(precond_ref, listed_ref, vector, out_ref, send_ref):
    def put(row, value):
        out_ref[pl.ds(row, 1), :] = value

    times([precond_ref], [vector], put)
    send_ref[...] = pick_from(listed_ref[...], pad_rows(out_ref[...], LANES), NT)


def start_kernel(mapped_ref, onehot_ref, precond_ref, listed_ref, load_ref, pre_ref, send_ref):
    load = pick(mapped_ref[...], onehot_ref[...], TN)[: load_ref.shape[0]]
    load_ref[...] = load
    precondition(precond_ref, listed_ref, load, pre_ref, send_ref)


def start(mapped, onehot, precond, listed):
    shape = pltpu.VMEM((precond.shape[0], LANES), F32)
    return pl.pallas_call(
        start_kernel,
        out_shape=(shape, shape, pltpu.VMEM(listed.shape, F32)),
        in_specs=[VMEM] * 4,
        out_specs=[VMEM] * 3,
        compiler_params=limit(6),
        name="start",
    )(mapped, onehot, *near_core(precond, listed))


def inside_kernel(blocks_ref, local_ref, outer_ref, old_ref, pre_ref, near_ref, part_ref, taken_ref):
    pre = pre_ref[...]
    size = pre.shape[0]
    count = near_ref.shape[0]

    def put(row, value):
        part_ref[pl.ds(row, 1), :] = value - old_ref[pl.ds(row, 1), :]

    times([blocks_ref.at[0]], [pre], put)
    for neighbor in range(2):
        taken = pick(pre, local_ref[neighbor], NN)
        taken_ref[neighbor] = taken + pick(near_ref[...], outer_ref[neighbor, :count, :], TN)[:size]


def inside(blocks, local, outer, old, pre, near):
    size = old.shape[0]
    return pl.pallas_call(
        inside_kernel,
        out_shape=(pltpu.VMEM(old.shape, F32), pltpu.VMEM((2, size, LANES), F32)),
        in_specs=[VMEM] * 6,
        out_specs=[VMEM] * 2,
        compiler_params=limit(6),
        cost_estimate=pl.CostEstimate(flops=0, bytes_accessed=2 * MIB, transcendentals=0),
        name="inside",
    )(*near_core(blocks, local, outer, old, pre, near))


def outside(blocks_ref, outer_ref, part_ref, taken_ref, far_ref, new_ref):
    size = part_ref.shape[0]
    count = far_ref.shape[0]
    vectors = [
        taken_ref[neighbor] + pick(far_ref[...], outer_ref[neighbor, count:, :], TN)[:size]
        for neighbor in range(2)
    ]

    def put(row, value):
        new_ref[pl.ds(row, 1), :] = value + part_ref[pl.ds(row, 1), :]

    times([blocks_ref.at[1], blocks_ref.at[2]], vectors, put)


def step_kernel(
    blocks_ref, precond_ref, outer_ref, listed_ref, part_ref, taken_ref, far_ref,
    new_ref, new_pre_ref, send_ref,
):
    outside(blocks_ref, outer_ref, part_ref, taken_ref, far_ref, new_ref)
    precondition(precond_ref, listed_ref, new_ref[...], new_pre_ref, send_ref)


def step(blocks, precond, outer, listed, part, taken, far):
    shape = pltpu.VMEM(part.shape, F32)
    return pl.pallas_call(
        step_kernel,
        out_shape=(shape, shape, pltpu.VMEM(far.shape, F32)),
        in_specs=[VMEM] * 7,
        out_specs=[VMEM] * 3,
        compiler_params=limit(6),
        name="step",
    )(*near_core(blocks, precond, outer, listed, part, taken, far))


PAIRS = [(i, j) for i in range(STEPS + 1) for j in range(i, STEPS + 1)]


def last_kernel(
    blocks_ref, outer_ref, part_ref, taken_ref, far_ref, b0_ref, b1_ref, b2_ref, b3_ref,
    new_ref, sums_ref,
):
    outside(blocks_ref, outer_ref, part_ref, taken_ref, far_ref, new_ref)
    vectors = [ref[...] for ref in (b0_ref, b1_ref, b2_ref, b3_ref, new_ref)]
    sums = [jnp.sum(vectors[i] * vectors[j], axis=0, keepdims=True) for i, j in PAIRS]
    sums.append(jnp.zeros((LANES - len(sums), LANES), F32))
    ones = jnp.ones((sums_ref.shape[0], LANES), BF16)
    sums_ref[...] = pick_from(ones, jnp.concatenate(sums, axis=0), NT)


def last(blocks, outer, part, taken, far, basis, parts):
    return pl.pallas_call(
        last_kernel,
        out_shape=(pltpu.VMEM(part.shape, F32), pltpu.VMEM((parts, LANES), F32)),
        in_specs=[VMEM] * 9,
        out_specs=[VMEM] * 2,
        compiler_params=limit(6),
        name="last",
    )(*near_core(blocks, outer, part, taken, far, *basis))


def plus(x, y):
    return [a + b for a, b in zip(x, y)]


def scaled(scale, x):
    return [scale * a for a in x]


def recurrences(product):
    def inner(x, y):
        return sum(
            a * b * product[min(i, j), max(i, j)]
            for i, a in enumerate(x)
            for j, b in enumerate(y)
        )

    def image_of(x):
        return plus([x[0] * 0.0] + x, x + [x[0] * 0.0])

    one = product[0, 0] * 0.0 + 1.0
    residual = search = shadow = [one]
    answer = []
    alignment = product[0, 0]

    def add(x, y):
        size = max(len(x), len(y))
        zero = one * 0.0
        return plus(x + [zero] * (size - len(x)), y + [zero] * (size - len(y)))

    for iteration in range(2):
        image = image_of(search)
        step_size = alignment / inner(shadow, image)
        middle = add(residual, scaled(-step_size, image))
        middle_image = image_of(middle)
        smoothing = inner(middle_image, middle) / inner(middle_image, middle_image)
        answer = add(answer, add(scaled(step_size, search), scaled(smoothing, middle)))
        residual = add(middle, scaled(-smoothing, middle_image))
        if iteration == 0:
            new_alignment = inner(shadow, residual)
            momentum = new_alignment / alignment * (step_size / smoothing)
            search = add(residual, scaled(momentum, add(search, scaled(-smoothing, image))))
            alignment = new_alignment
    return answer, residual


def finish_kernel(sums_ref, *refs):
    basis, pres, (solution_ref, residual_ref) = refs[:5], refs[5:9], refs[9:]
    totals = jnp.sum(sums_ref[...], axis=0, keepdims=True)
    product = {pair: totals[:, k : k + 1] for k, pair in enumerate(PAIRS)}
    answer, residual = recurrences(product)
    solution_ref[...] = sum(a * ref[...] for a, ref in zip(answer, pres))
    residual_ref[...] = sum(a * ref[...] for a, ref in zip(residual, basis))


def finish(sums, basis, pres):
    shape = jax.ShapeDtypeStruct(pres[0].shape, F32)
    return pl.pallas_call(
        finish_kernel,
        out_shape=(shape, shape),
        in_specs=[VMEM] * 10,
        compiler_params=limit(4),
        name="finish",
    )(*near_core(sums, *basis, *pres))


def to_near(send):
    devices = lax.axis_size(DOM)
    return lax.ppermute(send, DOM, [(i, i ^ 1) for i in range(devices)])


def to_far(send):
    odd = range(1, lax.axis_size(DOM) - 1, 2)
    return lax.ppermute(send, DOM, [(i, i + 1) for i in odd] + [(i + 1, i) for i in odd])


def to_all(x):
    return lax.all_to_all(x, DOM, split_axis=0, concat_axis=0, tiled=True)


def on_device(
    traction, fluid_coords, struct_coords, dest, target, blocks, columns, halo_list, precond
):
    parts = lax.axis_size(DOM)
    parity = lax.axis_index("dom_3").astype(jnp.int32).reshape(1)
    force = jnp.transpose(traction, (1, 0, 2))
    fluid = jnp.transpose(fluid_coords, (1, 0, 2))
    coords = struct_coords.reshape(-1, struct_coords.shape[2])
    wanted, slot = slots(dest.reshape(1, -1), target.reshape(1, -1), parts)
    turned, coords, local, outer, listed = prepare(
        halo_list, parity, columns, coords, wanted, fluid, force
    )
    onehot, answered = answer(to_all(wanted), coords)
    answered = to_all(answered.reshape(parts, CAP, LANES)).reshape(parts * CAP, LANES)
    mapped, blocks, precond = transfer(slot, answered, turned, blocks, precond)
    mapped = to_all(mapped.reshape(parts, CAP, LANES)).reshape(parts * CAP, LANES)
    load, pre, send = start(mapped, onehot, precond, listed)
    basis, pres = [load], [pre]
    for j in range(STEPS):
        far = to_far(send)
        near = to_near(send)
        part, taken = inside(blocks, local, outer, basis[-1], pres[-1], near)
        if j < STEPS - 1:
            new, pre, send = step(blocks, precond, outer, listed, part, taken, far)
            pres.append(pre)
        else:
            new, sums = last(blocks, outer, part, taken, far, basis, parts)
        basis.append(new)
    solution, residual = finish(to_all(sums), basis, pres)
    return load, solution, residual


def solution(mesh):
    finer = Mesh(mesh.devices.reshape(4, 4, 4, 2), DOM)
    in_specs = (
        P(DOM, None, None),
        P(DOM, None, None),
        P(None, None, DOM),
        P(DOM, None),
        P(DOM),
        P(None, None, None, DOM),
        P(None, DOM),
        P(DOM),
        P(None, None, DOM),
    )
    out_specs = (P(None, DOM), P(None, DOM), P(None, DOM))
    return jax.shard_map(
        on_device, mesh=finer, in_specs=in_specs, out_specs=out_specs, check_vma=False
    )
```

```python
import functools

import jax
import jax.numpy as jnp
from jax import lax
from jax.experimental import pallas as pl
from jax.experimental.pallas import tpu as pltpu
from jax.sharding import PartitionSpec as P

DOM = "dom"
SUPPORT = 0.9
CAP = 8
LANES = 128
STEPS = 4
F32 = jnp.float32
BF16 = jnp.bfloat16
NN = (((1,), (0,)), ((), ()))
NT = (((1,), (1,)), ((), ()))
TN = (((0,), (0,)), ((), ()))


SMEM = pl.BlockSpec(memory_space=pltpu.SMEM)
VMEM = pl.BlockSpec(memory_space=pltpu.VMEM)
ANY = pl.BlockSpec(memory_space=pl.ANY)
MIB = 1 << 20


def limit(mib):
    return pltpu.CompilerParams(vmem_limit_bytes=mib * MIB)


def near_core(*arrays):
    return [pltpu.with_memory_space_constraint(x, pltpu.VMEM) for x in arrays]


def in_hbm(*arrays):
    return [pltpu.with_memory_space_constraint(x, pltpu.HBM) for x in arrays]


def iota(shape, dim):
    return lax.broadcasted_iota(jnp.int32, shape, dim)


def flag(mask):
    return jnp.where(mask, 1.0, 0.0).astype(BF16)


def split3(x):
    high = x.astype(BF16)
    rest = x - high.astype(F32)
    mid = rest.astype(BF16)
    low = (rest - mid.astype(F32)).astype(BF16)
    return high, mid, low


def dot(a, b, dims):
    return lax.dot_general(a, b, dims, preferred_element_type=F32)


def pick(x, onehot, dims):
    return sum(dot(part, onehot, dims) for part in reversed(split3(x)))


def pick_from(onehot, x, dims):
    return sum(dot(onehot, part, dims) for part in reversed(split3(x)))


def pad_rows(x, rows):
    if x.shape[0] == rows:
        return x
    return jnp.concatenate([x, jnp.zeros((rows - x.shape[0], x.shape[1]), x.dtype)], axis=0)


def slots_kernel(dest_ref, target_ref, labels_ref, slot_ref):
    dest = dest_ref[...]
    count = dest.shape[1]
    parts = labels_ref.shape[0]
    hits = flag(iota((parts, count), 0) == dest)
    earlier = flag(iota((count, count), 0) < iota((count, count), 1))
    running = dot(hits, earlier, NN)
    before = jnp.sum(running * hits.astype(F32), axis=0, keepdims=True)
    slot_ref[...] = dest * CAP + before.astype(jnp.int32)
    place = iota((LANES, count), 0).astype(F32)
    wanted = jnp.where(place == before, (target_ref[...] + 1).astype(F32), 0.0)
    labels_ref[...] = dot(hits, wanted.astype(BF16), NT)


def slots(dest, target, parts):
    count = dest.shape[1]
    return pl.pallas_call(
        slots_kernel,
        out_shape=(
            jax.ShapeDtypeStruct((parts, LANES), F32),
            jax.ShapeDtypeStruct((1, count), jnp.int32),
        ),
        compiler_params=limit(2),
        name="slots",
    )(*in_hbm(dest, target))


def prepare_kernel(
    parts, halo_ref, place_ref, columns_ref, coords_ref, after_ref, fluid_ref, force_ref,
    turned_ref, coords_out, local_ref, outer_ref, listed_ref,
    points, sems,
):
    copies = [
        pltpu.make_async_copy(ref, points.at[k], sems.at[k])
        for k, ref in enumerate((fluid_ref, force_ref))
    ]
    for copy in copies:
        copy.start()
    coords_out[...] = pad_rows(coords_ref[...], LANES)
    halo = listed_ref.shape[0]
    core = place_ref[0] % 2
    at_end = jnp.logical_or(place_ref[0] == 0, place_ref[0] == parts - 1)
    held = jnp.where(at_end, halo, 2 * halo)
    for neighbor in range(2):
        column = columns_ref[pl.ds(neighbor, 1), :]
        local_ref[neighbor] = flag(iota((LANES, LANES), 0) == column)
        outer = (column - LANES) ^ ((1 - core) * halo)
        outer = jnp.where(outer < held, outer, -1)
        outer_ref[neighbor] = flag(iota(outer_ref.shape[1:], 0) == outer)
    rows = iota(listed_ref.shape, 0)
    column = jnp.zeros(listed_ref.shape, jnp.int32)
    for h in range(listed_ref.shape[0]):
        column = jnp.where(rows == h, halo_ref[h], column)
    listed_ref[...] = flag(column == iota(listed_ref.shape, 1))
    for copy in copies:
        copy.wait()
    for group in range(points.shape[2] // LANES):
        lanes = pl.ds(group * LANES, LANES)
        for kind, factor in enumerate((1.0 / SUPPORT, 4.0)):
            for c in range(3):
                turned_ref[group, 3 * kind + c] = points[kind, c, lanes, :].T * factor


def prepare(halo_list, place, columns, coords, after, fluid, force):
    count, nodes = fluid.shape[1:]
    halo = halo_list.shape[0]
    return pl.pallas_call(
        functools.partial(prepare_kernel, after.shape[0]),
        out_shape=(
            pltpu.VMEM((count // LANES, 6, nodes, LANES), F32),
            pltpu.VMEM((LANES, LANES), F32),
            pltpu.VMEM((2, LANES, LANES), BF16),
            pltpu.VMEM((2, 2 * halo, LANES), BF16),
            pltpu.VMEM((halo, LANES), BF16),
        ),
        in_specs=[SMEM, SMEM, VMEM, VMEM] + [ANY] * 3,
        out_specs=[VMEM] * 5,
        scratch_shapes=[pltpu.VMEM((2, 3, count, nodes), F32), pltpu.SemaphoreType.DMA((2,))],
        compiler_params=limit(4),
        cost_estimate=pl.CostEstimate(flops=0, bytes_accessed=3 * MIB, transcendentals=0),
        name="prepare",
    )(*in_hbm(halo_list, place, columns, coords, after, fluid, force))


def answer_kernel(labels_ref, coords_ref, onehot_ref, out_ref):
    rows = out_ref.shape[0]
    parts = labels_ref.shape[0]
    repeat = flag(iota((rows, parts), 0) // CAP == iota((rows, parts), 1))
    spread = dot(repeat, labels_ref[...].astype(BF16), NN)
    own = iota((rows, LANES), 0) % CAP == iota((rows, LANES), 1)
    own_label = jnp.where(own, spread, 0.0).astype(BF16)
    label = dot(own_label, jnp.ones((LANES, LANES), BF16), NN)
    onehot = flag(label == (iota((rows, LANES), 1) + 1).astype(F32))
    onehot_ref[...] = onehot
    out_ref[...] = pick_from(onehot, coords_ref[...], NT)


def answer(labels, coords):
    rows = labels.shape[0] * CAP
    return pl.pallas_call(
        answer_kernel,
        out_shape=(
            jax.ShapeDtypeStruct((rows, LANES), BF16),
            jax.ShapeDtypeStruct((rows, LANES), F32),
        ),
        in_specs=[VMEM, VMEM],
        compiler_params=limit(6),
        name="answer",
    )(labels, *near_core(coords))


def transfer_kernel(
    slot_ref, coords_ref, turned_ref, blocks_ref, precond_ref, out_ref, blocks_out, precond_out,
    struct, mapped, sems,
):
    tables = [
        pltpu.make_async_copy(precond_ref, precond_out, sems.at[0]),
        pltpu.make_async_copy(blocks_ref, blocks_out, sems.at[1]),
    ]
    for copy in tables:
        copy.start()
    rows = coords_ref.shape[0]
    count = slot_ref.shape[1]
    chosen = flag(iota((rows, count), 0) == slot_ref[...])
    struct[...] = pick(coords_ref[...], chosen, TN) * (1.0 / SUPPORT)
    nodes = turned_ref.shape[2]
    for group in range(count // LANES):
        lanes = pl.ds(group * LANES, LANES)
        where = [struct[pl.ds(c * 32, 32), lanes] for c in range(3)]

        def body(step, sums):
            sums = list(sums)
            for k in range(8):
                n = pl.ds(step * 8 + k, 1)
                apart = [where[c] - turned_ref[group, c, n, :] for c in range(3)]
                square = apart[0] * apart[0] + apart[1] * apart[1] + apart[2] * apart[2]
                square = jnp.maximum(square, 1e-30)
                left = jnp.maximum(1.0 - square * lax.rsqrt(square), 0.0)
                twice = left * left
                quarter = twice * twice * (1.25 - left)
                for c in range(3):
                    sums[c] = sums[c] + quarter * turned_ref[group, 3 + c, n, :]
            return tuple(sums)

        zero = jnp.zeros((32, LANES), F32)
        sums = lax.fori_loop(0, nodes // 8, body, (zero, zero, zero))
        for c in range(3):
            mapped[pl.ds(c * 32, 32), lanes] = sums[c]
    mapped[pl.ds(96, 32), :] = jnp.zeros((32, count), F32)
    out_ref[...] = pick_from(chosen, mapped[...], NT)
    for copy in tables:
        copy.wait()


def transfer(slot, coords, turned, blocks, precond):
    count = slot.shape[1]
    return pl.pallas_call(
        transfer_kernel,
        out_shape=(
            jax.ShapeDtypeStruct(coords.shape, F32),
            pltpu.VMEM(blocks.shape, F32),
            pltpu.VMEM(precond.shape, F32),
        ),
        in_specs=[VMEM] * 3 + [ANY] * 2,
        out_specs=[VMEM] * 3,
        scratch_shapes=[
            pltpu.VMEM((LANES, count), F32),
            pltpu.VMEM((LANES, count), F32),
            pltpu.SemaphoreType.DMA((2,)),
        ],
        compiler_params=limit(10),
        name="transfer",
    )(slot, coords, *near_core(turned), *in_hbm(blocks, precond))


def times(matrices, vectors, put):
    rows = vectors[0].shape[0]

    def body(step, carry):
        for k in range(8):
            row = step * 8 + k
            total = None
            for matrix, vector in zip(matrices, vectors):
                term = matrix[row] * vector
                total = term if total is None else total + term
            put(row, jnp.sum(total, axis=0, keepdims=True))
        return carry

    lax.fori_loop(0, rows // 8, body, 0)


def precondition(precond_ref, listed_ref, vector, out_ref, send_ref):
    def put(row, value):
        out_ref[pl.ds(row, 1), :] = value

    times([precond_ref], [vector], put)
    send_ref[...] = pick_from(listed_ref[...], pad_rows(out_ref[...], LANES), NT)


def start_kernel(mapped_ref, onehot_ref, precond_ref, listed_ref, load_ref, pre_ref, send_ref):
    load = pick(mapped_ref[...], onehot_ref[...], TN)[: load_ref.shape[0]]
    load_ref[...] = load
    precondition(precond_ref, listed_ref, load, pre_ref, send_ref)


def start(mapped, onehot, precond, listed):
    shape = pltpu.VMEM((precond.shape[0], LANES), F32)
    return pl.pallas_call(
        start_kernel,
        out_shape=(shape, shape, pltpu.VMEM(listed.shape, F32)),
        in_specs=[VMEM] * 4,
        out_specs=[VMEM] * 3,
        compiler_params=limit(6),
        name="start",
    )(mapped, onehot, *near_core(precond, listed))


def inside_kernel(blocks_ref, local_ref, outer_ref, old_ref, pre_ref, near_ref, part_ref, taken_ref):
    pre = pre_ref[...]
    size = pre.shape[0]
    count = near_ref.shape[0]

    def put(row, value):
        part_ref[pl.ds(row, 1), :] = value - old_ref[pl.ds(row, 1), :]

    times([blocks_ref.at[0]], [pre], put)
    for neighbor in range(2):
        taken = pick(pre, local_ref[neighbor], NN)
        taken_ref[neighbor] = taken + pick(near_ref[...], outer_ref[neighbor, :count, :], TN)[:size]


def inside(blocks, local, outer, old, pre, near):
    size = old.shape[0]
    return pl.pallas_call(
        inside_kernel,
        out_shape=(pltpu.VMEM(old.shape, F32), pltpu.VMEM((2, size, LANES), F32)),
        in_specs=[VMEM] * 6,
        out_specs=[VMEM] * 2,
        compiler_params=limit(6),
        cost_estimate=pl.CostEstimate(flops=0, bytes_accessed=2 * MIB, transcendentals=0),
        name="inside",
    )(*near_core(blocks, local, outer, old, pre, near))


def outside(blocks_ref, outer_ref, part_ref, taken_ref, far_ref, new_ref):
    size = part_ref.shape[0]
    count = far_ref.shape[0]
    vectors = [
        taken_ref[neighbor] + pick(far_ref[...], outer_ref[neighbor, count:, :], TN)[:size]
        for neighbor in range(2)
    ]

    def put(row, value):
        new_ref[pl.ds(row, 1), :] = value + part_ref[pl.ds(row, 1), :]

    times([blocks_ref.at[1], blocks_ref.at[2]], vectors, put)


def step_kernel(
    blocks_ref, precond_ref, outer_ref, listed_ref, part_ref, taken_ref, far_ref,
    new_ref, new_pre_ref, send_ref,
):
    outside(blocks_ref, outer_ref, part_ref, taken_ref, far_ref, new_ref)
    precondition(precond_ref, listed_ref, new_ref[...], new_pre_ref, send_ref)


def step(blocks, precond, outer, listed, part, taken, far):
    shape = pltpu.VMEM(part.shape, F32)
    return pl.pallas_call(
        step_kernel,
        out_shape=(shape, shape, pltpu.VMEM(far.shape, F32)),
        in_specs=[VMEM] * 7,
        out_specs=[VMEM] * 3,
        compiler_params=limit(6),
        name="step",
    )(*near_core(blocks, precond, outer, listed, part, taken, far))


PAIRS = [(i, j) for i in range(STEPS + 1) for j in range(i, STEPS + 1)]


def last_kernel(
    blocks_ref, outer_ref, part_ref, taken_ref, far_ref, b0_ref, b1_ref, b2_ref, b3_ref,
    new_ref, sums_ref,
):
    outside(blocks_ref, outer_ref, part_ref, taken_ref, far_ref, new_ref)
    vectors = [ref[...] for ref in (b0_ref, b1_ref, b2_ref, b3_ref, new_ref)]
    sums = [jnp.sum(vectors[i] * vectors[j], axis=0, keepdims=True) for i, j in PAIRS]
    sums.append(jnp.zeros((LANES - len(sums), LANES), F32))
    ones = jnp.ones((sums_ref.shape[0], LANES), BF16)
    sums_ref[...] = pick_from(ones, jnp.concatenate(sums, axis=0), NT)


def last(blocks, outer, part, taken, far, basis, parts):
    return pl.pallas_call(
        last_kernel,
        out_shape=(pltpu.VMEM(part.shape, F32), pltpu.VMEM((parts, LANES), F32)),
        in_specs=[VMEM] * 9,
        out_specs=[VMEM] * 2,
        compiler_params=limit(6),
        name="last",
    )(*near_core(blocks, outer, part, taken, far, *basis))


def plus(x, y):
    return [a + b for a, b in zip(x, y)]


def scaled(scale, x):
    return [scale * a for a in x]


def recurrences(product):
    def inner(x, y):
        return sum(
            a * b * product[min(i, j), max(i, j)]
            for i, a in enumerate(x)
            for j, b in enumerate(y)
        )

    def image_of(x):
        return plus([x[0] * 0.0] + x, x + [x[0] * 0.0])

    one = product[0, 0] * 0.0 + 1.0
    residual = search = shadow = [one]
    answer = []
    alignment = product[0, 0]

    def add(x, y):
        size = max(len(x), len(y))
        zero = one * 0.0
        return plus(x + [zero] * (size - len(x)), y + [zero] * (size - len(y)))

    for iteration in range(2):
        image = image_of(search)
        step_size = alignment / inner(shadow, image)
        middle = add(residual, scaled(-step_size, image))
        middle_image = image_of(middle)
        smoothing = inner(middle_image, middle) / inner(middle_image, middle_image)
        answer = add(answer, add(scaled(step_size, search), scaled(smoothing, middle)))
        residual = add(middle, scaled(-smoothing, middle_image))
        if iteration == 0:
            new_alignment = inner(shadow, residual)
            momentum = new_alignment / alignment * (step_size / smoothing)
            search = add(residual, scaled(momentum, add(search, scaled(-smoothing, image))))
            alignment = new_alignment
    return answer, residual


def finish_kernel(sums_ref, *refs):
    basis, pres, (solution_ref, residual_ref) = refs[:5], refs[5:9], refs[9:]
    totals = jnp.sum(sums_ref[...], axis=0, keepdims=True)
    product = {pair: totals[:, k : k + 1] for k, pair in enumerate(PAIRS)}
    answer, residual = recurrences(product)
    solution_ref[...] = sum(a * ref[...] for a, ref in zip(answer, pres))
    residual_ref[...] = sum(a * ref[...] for a, ref in zip(residual, basis))


def finish(sums, basis, pres):
    shape = jax.ShapeDtypeStruct(pres[0].shape, F32)
    return pl.pallas_call(
        finish_kernel,
        out_shape=(shape, shape),
        in_specs=[VMEM] * 10,
        compiler_params=limit(4),
        name="finish",
    )(*near_core(sums, *basis, *pres))


def to_near(send):
    devices = lax.axis_size(DOM)
    return lax.ppermute(send, DOM, [(i, i ^ 1) for i in range(devices)])


def to_far(send):
    devices = lax.axis_size(DOM)
    pairs = [(i, (i + 1) % devices) for i in range(1, devices, 2)]
    return lax.ppermute(send, DOM, pairs + [(j, i) for i, j in pairs])


def to_all(x):
    return lax.all_to_all(x, DOM, split_axis=0, concat_axis=0, tiled=True)


def on_device(
    traction, fluid_coords, struct_coords, dest, target, blocks, columns, halo_list, precond
):
    parts = lax.axis_size(DOM)
    place = lax.axis_index(DOM).astype(jnp.int32).reshape(1)
    force = jnp.transpose(traction, (1, 0, 2))
    fluid = jnp.transpose(fluid_coords, (1, 0, 2))
    coords = struct_coords.reshape(-1, struct_coords.shape[2])
    wanted, slot = slots(dest.reshape(1, -1), target.reshape(1, -1), parts)
    turned, coords, local, outer, listed = prepare(
        halo_list, place, columns, coords, wanted, fluid, force
    )
    onehot, answered = answer(to_all(wanted), coords)
    answered = to_all(answered.reshape(parts, CAP, LANES)).reshape(parts * CAP, LANES)
    mapped, blocks, precond = transfer(slot, answered, turned, blocks, precond)
    mapped = to_all(mapped.reshape(parts, CAP, LANES)).reshape(parts * CAP, LANES)
    load, pre, send = start(mapped, onehot, precond, listed)
    basis, pres = [load], [pre]
    for j in range(STEPS):
        far = to_far(send)
        near = to_near(send)
        part, taken = inside(blocks, local, outer, basis[-1], pres[-1], near)
        if j < STEPS - 1:
            new, pre, send = step(blocks, precond, outer, listed, part, taken, far)
            pres.append(pre)
        else:
            new, sums = last(blocks, outer, part, taken, far, basis, parts)
        basis.append(new)
    solution, residual = finish(to_all(sums), basis, pres)
    return load, solution, residual


def solution(mesh):
    in_specs = (
        P(DOM, None, None),
        P(DOM, None, None),
        P(None, None, DOM),
        P(DOM, None),
        P(DOM),
        P(None, None, None, DOM),
        P(None, DOM),
        P(DOM),
        P(None, None, DOM),
    )
    out_specs = (P(None, DOM), P(None, DOM), P(None, DOM))
    return jax.shard_map(
        on_device, mesh=mesh, in_specs=in_specs, out_specs=out_specs, check_vma=False
    )
```

```python
import functools

import jax
import jax.numpy as jnp
from jax import lax
from jax.experimental import pallas as pl
from jax.experimental.pallas import tpu as pltpu
from jax.sharding import PartitionSpec as P

DOM = "dom"
SUPPORT = 0.9
CAP = 8
LANES = 128
STEPS = 4
F32 = jnp.float32
BF16 = jnp.bfloat16
NN = (((1,), (0,)), ((), ()))
NT = (((1,), (1,)), ((), ()))
TN = (((0,), (0,)), ((), ()))


SMEM = pl.BlockSpec(memory_space=pltpu.SMEM)
VMEM = pl.BlockSpec(memory_space=pltpu.VMEM)
ANY = pl.BlockSpec(memory_space=pl.ANY)
MIB = 1 << 20


def limit(mib):
    return pltpu.CompilerParams(vmem_limit_bytes=mib * MIB)


def near_core(*arrays):
    return [pltpu.with_memory_space_constraint(x, pltpu.VMEM) for x in arrays]


def in_hbm(*arrays):
    return [pltpu.with_memory_space_constraint(x, pltpu.HBM) for x in arrays]


def iota(shape, dim):
    return lax.broadcasted_iota(jnp.int32, shape, dim)


def flag(mask):
    return jnp.where(mask, 1.0, 0.0).astype(BF16)


def split3(x):
    high = x.astype(BF16)
    rest = x - high.astype(F32)
    mid = rest.astype(BF16)
    low = (rest - mid.astype(F32)).astype(BF16)
    return high, mid, low


def dot(a, b, dims):
    return lax.dot_general(a, b, dims, preferred_element_type=F32)


def three(product, size, axis):
    parts = [lax.slice_in_dim(product, k * size, (k + 1) * size, axis=axis) for k in range(3)]
    return parts[0] + (parts[1] + parts[2])


def pick(x, onehot, dims):
    free = 0 if dims == NN else 1
    stacked = jnp.concatenate(split3(x), axis=free)
    return three(dot(stacked, onehot, dims), x.shape[free], 0)


def pick_from(onehot, x):
    return three(dot(onehot, jnp.concatenate(split3(x), axis=0), NT), x.shape[0], 1)


def pad_rows(x, rows):
    if x.shape[0] == rows:
        return x
    return jnp.concatenate([x, jnp.zeros((rows - x.shape[0], x.shape[1]), x.dtype)], axis=0)


def slots_kernel(dest_ref, target_ref, labels_ref, slot_ref):
    dest = dest_ref[...]
    count = dest.shape[1]
    parts = labels_ref.shape[0]
    hits = flag(iota((parts, count), 0) == dest)
    earlier = flag(iota((count, count), 0) < iota((count, count), 1))
    running = dot(hits, earlier, NN)
    before = jnp.sum(running * hits.astype(F32), axis=0, keepdims=True)
    slot_ref[...] = dest * CAP + before.astype(jnp.int32)
    place = iota((LANES, count), 0).astype(F32)
    wanted = jnp.where(place == before, (target_ref[...] + 1).astype(F32), 0.0)
    labels_ref[...] = dot(hits, wanted.astype(BF16), NT)


def slots(dest, target, parts):
    count = dest.shape[1]
    return pl.pallas_call(
        slots_kernel,
        out_shape=(
            jax.ShapeDtypeStruct((parts, LANES), F32),
            jax.ShapeDtypeStruct((1, count), jnp.int32),
        ),
        compiler_params=limit(2),
        name="slots",
    )(*in_hbm(dest, target))


def prepare_kernel(
    parts, halo_ref, place_ref, columns_ref, coords_ref, after_ref, fluid_ref, force_ref,
    turned_ref, coords_out, local_ref, outer_ref, listed_ref,
    points, sems,
):
    copies = [
        pltpu.make_async_copy(ref, points.at[k], sems.at[k])
        for k, ref in enumerate((fluid_ref, force_ref))
    ]
    for copy in copies:
        copy.start()
    coords_out[...] = pad_rows(coords_ref[...], LANES)
    halo = listed_ref.shape[0]
    core = place_ref[0] % 2
    at_end = jnp.logical_or(place_ref[0] == 0, place_ref[0] == parts - 1)
    held = jnp.where(at_end, halo, 2 * halo)
    for neighbor in range(2):
        column = columns_ref[pl.ds(neighbor, 1), :]
        local_ref[neighbor] = flag(iota((LANES, LANES), 0) == column)
        outer = (column - LANES) ^ ((1 - core) * halo)
        outer = jnp.where(outer < held, outer, -1)
        outer_ref[neighbor] = flag(iota(outer_ref.shape[1:], 0) == outer)
    rows = iota(listed_ref.shape, 0)
    column = jnp.zeros(listed_ref.shape, jnp.int32)
    for h in range(listed_ref.shape[0]):
        column = jnp.where(rows == h, halo_ref[h], column)
    listed_ref[...] = flag(column == iota(listed_ref.shape, 1))
    for copy in copies:
        copy.wait()
    for group in range(points.shape[2] // LANES):
        lanes = pl.ds(group * LANES, LANES)
        length = jnp.zeros(turned_ref.shape[2:], F32)
        for c in range(3):
            position = points[0, c, lanes, :].T * (1.0 / SUPPORT)
            length = length + position * position
            turned_ref[group, c] = position * -2.0
            turned_ref[group, 3 + c] = points[1, c, lanes, :].T * 4.0
        turned_ref[group, 6] = length


def prepare(halo_list, place, columns, coords, after, fluid, force):
    count, nodes = fluid.shape[1:]
    halo = halo_list.shape[0]
    return pl.pallas_call(
        functools.partial(prepare_kernel, after.shape[0]),
        out_shape=(
            pltpu.VMEM((count // LANES, 7, nodes, LANES), F32),
            pltpu.VMEM((LANES, LANES), F32),
            pltpu.VMEM((2, LANES, LANES), BF16),
            pltpu.VMEM((2, 2 * halo, LANES), BF16),
            pltpu.VMEM((halo, LANES), BF16),
        ),
        in_specs=[SMEM, SMEM, VMEM, VMEM] + [ANY] * 3,
        out_specs=[VMEM] * 5,
        scratch_shapes=[pltpu.VMEM((2, 3, count, nodes), F32), pltpu.SemaphoreType.DMA((2,))],
        compiler_params=limit(4),
        cost_estimate=pl.CostEstimate(flops=0, bytes_accessed=3 * MIB, transcendentals=0),
        name="prepare",
    )(*in_hbm(halo_list, place, columns, coords, after, fluid, force))


def answer_kernel(labels_ref, coords_ref, onehot_ref, out_ref):
    rows = out_ref.shape[0]
    parts = labels_ref.shape[0]
    repeat = flag(iota((rows, parts), 0) // CAP == iota((rows, parts), 1))
    spread = dot(repeat, labels_ref[...].astype(BF16), NN)
    own = iota((rows, LANES), 0) % CAP == iota((rows, LANES), 1)
    own_label = jnp.where(own, spread, 0.0).astype(BF16)
    label = dot(own_label, jnp.ones((LANES, LANES), BF16), NN)
    onehot = flag(label == (iota((rows, LANES), 1) + 1).astype(F32))
    onehot_ref[...] = onehot
    out_ref[...] = pick_from(onehot, coords_ref[...])


def answer(labels, coords):
    rows = labels.shape[0] * CAP
    return pl.pallas_call(
        answer_kernel,
        out_shape=(
            jax.ShapeDtypeStruct((rows, LANES), BF16),
            jax.ShapeDtypeStruct((rows, LANES), F32),
        ),
        in_specs=[VMEM, VMEM],
        compiler_params=limit(6),
        name="answer",
    )(labels, *near_core(coords))


def transfer_kernel(
    slot_ref, coords_ref, turned_ref, blocks_ref, precond_ref, out_ref, blocks_out, precond_out,
    struct, mapped, sems,
):
    tables = [
        pltpu.make_async_copy(precond_ref, precond_out, sems.at[0]),
        pltpu.make_async_copy(blocks_ref, blocks_out, sems.at[1]),
    ]
    for copy in tables:
        copy.start()
    rows = coords_ref.shape[0]
    count = slot_ref.shape[1]
    chosen = flag(iota((rows, count), 0) == slot_ref[...])
    struct[...] = pick(coords_ref[...], chosen, TN) * (1.0 / SUPPORT)
    nodes = turned_ref.shape[2]
    for group in range(count // LANES):
        lanes = pl.ds(group * LANES, LANES)
        where = [struct[pl.ds(c * 32, 32), lanes] for c in range(3)]
        length = where[0] * where[0] + where[1] * where[1] + where[2] * where[2]

        def body(step, sums):
            sums = list(sums)
            for k in range(8):
                n = pl.ds(step * 8 + k, 1)
                square = length + turned_ref[group, 6, n, :]
                for c in range(3):
                    square = square + where[c] * turned_ref[group, c, n, :]
                square = jnp.maximum(square, 1e-30)
                left = jnp.maximum(1.0 - square * lax.rsqrt(square), 0.0)
                twice = left * left
                quarter = twice * twice * (1.25 - left)
                for c in range(3):
                    sums[c] = sums[c] + quarter * turned_ref[group, 3 + c, n, :]
            return tuple(sums)

        zero = jnp.zeros((32, LANES), F32)
        sums = lax.fori_loop(0, nodes // 8, body, (zero, zero, zero))
        for c in range(3):
            mapped[pl.ds(c * 32, 32), lanes] = sums[c]
    mapped[pl.ds(96, 32), :] = jnp.zeros((32, count), F32)
    out_ref[...] = pick_from(chosen, mapped[...])
    for copy in tables:
        copy.wait()


def transfer(slot, coords, turned, blocks, precond):
    count = slot.shape[1]
    return pl.pallas_call(
        transfer_kernel,
        out_shape=(
            jax.ShapeDtypeStruct(coords.shape, F32),
            pltpu.VMEM(blocks.shape, F32),
            pltpu.VMEM(precond.shape, F32),
        ),
        in_specs=[VMEM] * 3 + [ANY] * 2,
        out_specs=[VMEM] * 3,
        scratch_shapes=[
            pltpu.VMEM((LANES, count), F32),
            pltpu.VMEM((LANES, count), F32),
            pltpu.SemaphoreType.DMA((2,)),
        ],
        compiler_params=limit(10),
        name="transfer",
    )(slot, coords, *near_core(turned), *in_hbm(blocks, precond))


def times(matrices, vectors, put):
    rows = vectors[0].shape[0]

    def body(step, carry):
        for k in range(8):
            row = step * 8 + k
            total = None
            for matrix, vector in zip(matrices, vectors):
                term = matrix[row] * vector
                total = term if total is None else total + term
            put(row, jnp.sum(total, axis=0, keepdims=True))
        return carry

    lax.fori_loop(0, rows // 8, body, 0)


def precondition(precond_ref, listed_ref, vector, out_ref, send_ref):
    def put(row, value):
        out_ref[pl.ds(row, 1), :] = value

    times([precond_ref], [vector], put)
    send_ref[...] = pick_from(listed_ref[...], pad_rows(out_ref[...], LANES))


def start_kernel(mapped_ref, onehot_ref, precond_ref, listed_ref, load_ref, pre_ref, send_ref):
    load = pick(mapped_ref[...], onehot_ref[...], TN)[: load_ref.shape[0]]
    load_ref[...] = load
    precondition(precond_ref, listed_ref, load, pre_ref, send_ref)


def start(mapped, onehot, precond, listed):
    shape = pltpu.VMEM((precond.shape[0], LANES), F32)
    return pl.pallas_call(
        start_kernel,
        out_shape=(shape, shape, pltpu.VMEM(listed.shape, F32)),
        in_specs=[VMEM] * 4,
        out_specs=[VMEM] * 3,
        compiler_params=limit(6),
        name="start",
    )(mapped, onehot, *near_core(precond, listed))


def inside_kernel(blocks_ref, local_ref, outer_ref, old_ref, pre_ref, near_ref, part_ref, taken_ref):
    pre = pre_ref[...]
    size = pre.shape[0]
    count = near_ref.shape[0]

    def put(row, value):
        part_ref[pl.ds(row, 1), :] = value - old_ref[pl.ds(row, 1), :]

    times([blocks_ref.at[0]], [pre], put)
    for neighbor in range(2):
        taken = pick(pre, local_ref[neighbor], NN)
        taken_ref[neighbor] = taken + pick(near_ref[...], outer_ref[neighbor, :count, :], TN)[:size]


def inside(blocks, local, outer, old, pre, near):
    size = old.shape[0]
    return pl.pallas_call(
        inside_kernel,
        out_shape=(pltpu.VMEM(old.shape, F32), pltpu.VMEM((2, size, LANES), F32)),
        in_specs=[VMEM] * 6,
        out_specs=[VMEM] * 2,
        compiler_params=limit(6),
        cost_estimate=pl.CostEstimate(flops=0, bytes_accessed=2 * MIB, transcendentals=0),
        name="inside",
    )(*near_core(blocks, local, outer, old, pre, near))


def outside(blocks_ref, outer_ref, part_ref, taken_ref, far_ref, new_ref):
    size = part_ref.shape[0]
    count = far_ref.shape[0]
    vectors = [
        taken_ref[neighbor] + pick(far_ref[...], outer_ref[neighbor, count:, :], TN)[:size]
        for neighbor in range(2)
    ]

    def put(row, value):
        new_ref[pl.ds(row, 1), :] = value + part_ref[pl.ds(row, 1), :]

    times([blocks_ref.at[1], blocks_ref.at[2]], vectors, put)


def step_kernel(
    blocks_ref, precond_ref, outer_ref, listed_ref, part_ref, taken_ref, far_ref,
    new_ref, new_pre_ref, send_ref,
):
    outside(blocks_ref, outer_ref, part_ref, taken_ref, far_ref, new_ref)
    precondition(precond_ref, listed_ref, new_ref[...], new_pre_ref, send_ref)


def step(blocks, precond, outer, listed, part, taken, far):
    shape = pltpu.VMEM(part.shape, F32)
    return pl.pallas_call(
        step_kernel,
        out_shape=(shape, shape, pltpu.VMEM(far.shape, F32)),
        in_specs=[VMEM] * 7,
        out_specs=[VMEM] * 3,
        compiler_params=limit(6),
        name="step",
    )(*near_core(blocks, precond, outer, listed, part, taken, far))


PAIRS = [(i, j) for i in range(STEPS + 1) for j in range(i, STEPS + 1)]


def last_kernel(
    blocks_ref, outer_ref, part_ref, taken_ref, far_ref, b0_ref, b1_ref, b2_ref, b3_ref,
    new_ref, sums_ref,
):
    outside(blocks_ref, outer_ref, part_ref, taken_ref, far_ref, new_ref)
    vectors = [ref[...] for ref in (b0_ref, b1_ref, b2_ref, b3_ref, new_ref)]
    sums = [jnp.sum(vectors[i] * vectors[j], axis=0, keepdims=True) for i, j in PAIRS]
    sums.append(jnp.zeros((LANES - len(sums), LANES), F32))
    ones = jnp.ones((sums_ref.shape[0], LANES), BF16)
    sums_ref[...] = pick_from(ones, jnp.concatenate(sums, axis=0))


def last(blocks, outer, part, taken, far, basis, parts):
    return pl.pallas_call(
        last_kernel,
        out_shape=(pltpu.VMEM(part.shape, F32), pltpu.VMEM((parts, LANES), F32)),
        in_specs=[VMEM] * 9,
        out_specs=[VMEM] * 2,
        compiler_params=limit(6),
        name="last",
    )(*near_core(blocks, outer, part, taken, far, *basis))


def plus(x, y):
    return [a + b for a, b in zip(x, y)]


def scaled(scale, x):
    return [scale * a for a in x]


def recurrences(product):
    def inner(x, y):
        return sum(
            a * b * product[min(i, j), max(i, j)]
            for i, a in enumerate(x)
            for j, b in enumerate(y)
        )

    def image_of(x):
        return plus([x[0] * 0.0] + x, x + [x[0] * 0.0])

    one = product[0, 0] * 0.0 + 1.0
    residual = search = shadow = [one]
    answer = []
    alignment = product[0, 0]

    def add(x, y):
        size = max(len(x), len(y))
        zero = one * 0.0
        return plus(x + [zero] * (size - len(x)), y + [zero] * (size - len(y)))

    for iteration in range(2):
        image = image_of(search)
        step_size = alignment / inner(shadow, image)
        middle = add(residual, scaled(-step_size, image))
        middle_image = image_of(middle)
        smoothing = inner(middle_image, middle) / inner(middle_image, middle_image)
        answer = add(answer, add(scaled(step_size, search), scaled(smoothing, middle)))
        residual = add(middle, scaled(-smoothing, middle_image))
        if iteration == 0:
            new_alignment = inner(shadow, residual)
            momentum = new_alignment / alignment * (step_size / smoothing)
            search = add(residual, scaled(momentum, add(search, scaled(-smoothing, image))))
            alignment = new_alignment
    return answer, residual


def finish_kernel(sums_ref, *refs):
    basis, pres, (solution_ref, residual_ref) = refs[:5], refs[5:9], refs[9:]
    totals = jnp.sum(sums_ref[...], axis=0, keepdims=True)
    product = {pair: totals[:, k : k + 1] for k, pair in enumerate(PAIRS)}
    answer, residual = recurrences(product)
    solution_ref[...] = sum(a * ref[...] for a, ref in zip(answer, pres))
    residual_ref[...] = sum(a * ref[...] for a, ref in zip(residual, basis))


def finish(sums, basis, pres):
    shape = jax.ShapeDtypeStruct(pres[0].shape, F32)
    return pl.pallas_call(
        finish_kernel,
        out_shape=(shape, shape),
        in_specs=[VMEM] * 10,
        compiler_params=limit(4),
        name="finish",
    )(*near_core(sums, *basis, *pres))


def to_near(send):
    devices = lax.axis_size(DOM)
    return lax.ppermute(send, DOM, [(i, i ^ 1) for i in range(devices)])


def to_far(send, closed):
    devices = lax.axis_size(DOM)
    pairs = [(i, (i + 1) % devices) for i in range(1, devices if closed else devices - 1, 2)]
    return lax.ppermute(send, DOM, pairs + [(j, i) for i, j in pairs])


def to_all(x):
    return lax.all_to_all(x, DOM, split_axis=0, concat_axis=0, tiled=True)


def on_device(
    traction, fluid_coords, struct_coords, dest, target, blocks, columns, halo_list, precond
):
    parts = lax.axis_size(DOM)
    place = lax.axis_index(DOM).astype(jnp.int32).reshape(1)
    force = jnp.transpose(traction, (1, 0, 2))
    fluid = jnp.transpose(fluid_coords, (1, 0, 2))
    coords = struct_coords.reshape(-1, struct_coords.shape[2])
    wanted, slot = slots(dest.reshape(1, -1), target.reshape(1, -1), parts)
    turned, coords, local, outer, listed = prepare(
        halo_list, place, columns, coords, wanted, fluid, force
    )
    onehot, answered = answer(to_all(wanted), coords)
    answered = to_all(answered.reshape(parts, CAP, LANES)).reshape(parts * CAP, LANES)
    mapped, blocks, precond = transfer(slot, answered, turned, blocks, precond)
    mapped = to_all(mapped.reshape(parts, CAP, LANES)).reshape(parts * CAP, LANES)
    load, pre, send = start(mapped, onehot, precond, listed)
    basis, pres = [load], [pre]
    for j in range(STEPS):
        far = to_far(send, j > 0)
        near = to_near(send)
        part, taken = inside(blocks, local, outer, basis[-1], pres[-1], near)
        if j < STEPS - 1:
            new, pre, send = step(blocks, precond, outer, listed, part, taken, far)
            pres.append(pre)
        else:
            new, sums = last(blocks, outer, part, taken, far, basis, parts)
        basis.append(new)
    solution, residual = finish(to_all(sums), basis, pres)
    return load, solution, residual


def solution(mesh):
    in_specs = (
        P(DOM, None, None),
        P(DOM, None, None),
        P(None, None, DOM),
        P(DOM, None),
        P(DOM),
        P(None, None, None, DOM),
        P(None, DOM),
        P(DOM),
        P(None, None, DOM),
    )
    out_specs = (P(None, DOM), P(None, DOM), P(None, DOM))
    return jax.shard_map(
        on_device, mesh=mesh, in_specs=in_specs, out_specs=out_specs, check_vma=False
    )
```

```python
import functools

import jax
import jax.numpy as jnp
from jax import lax
from jax.experimental import pallas as pl
from jax.experimental.pallas import tpu as pltpu
from jax.sharding import PartitionSpec as P

DOM = "dom"
SUPPORT = 0.9
CAP = 8
LANES = 128
STEPS = 4
F32 = jnp.float32
BF16 = jnp.bfloat16
NN = (((1,), (0,)), ((), ()))
NT = (((1,), (1,)), ((), ()))
TN = (((0,), (0,)), ((), ()))


SMEM = pl.BlockSpec(memory_space=pltpu.SMEM)
VMEM = pl.BlockSpec(memory_space=pltpu.VMEM)
ANY = pl.BlockSpec(memory_space=pl.ANY)
MIB = 1 << 20


def limit(mib):
    return pltpu.CompilerParams(vmem_limit_bytes=mib * MIB)


def near_core(*arrays):
    return [pltpu.with_memory_space_constraint(x, pltpu.VMEM) for x in arrays]


def in_hbm(*arrays):
    return [pltpu.with_memory_space_constraint(x, pltpu.HBM) for x in arrays]


def iota(shape, dim):
    return lax.broadcasted_iota(jnp.int32, shape, dim)


def flag(mask):
    return jnp.where(mask, 1.0, 0.0).astype(BF16)


def split3(x):
    high = x.astype(BF16)
    rest = x - high.astype(F32)
    mid = rest.astype(BF16)
    low = (rest - mid.astype(F32)).astype(BF16)
    return high, mid, low


def dot(a, b, dims):
    return lax.dot_general(a, b, dims, preferred_element_type=F32)


def three(product, size, axis):
    parts = [lax.slice_in_dim(product, k * size, (k + 1) * size, axis=axis) for k in range(3)]
    return parts[0] + (parts[1] + parts[2])


def pick(x, onehot, dims):
    free = 0 if dims == NN else 1
    stacked = jnp.concatenate(split3(x), axis=free)
    return three(dot(stacked, onehot, dims), x.shape[free], 0)


def pick_from(onehot, x):
    return three(dot(onehot, jnp.concatenate(split3(x), axis=0), NT), x.shape[0], 1)


def pad_rows(x, rows):
    if x.shape[0] == rows:
        return x
    return jnp.concatenate([x, jnp.zeros((rows - x.shape[0], x.shape[1]), x.dtype)], axis=0)


def pack(wide_ref, out_ref):
    parts = wide_ref.shape[0] // CAP
    free = iota((parts, LANES), 1) >= 96
    spare = [wide_ref[pl.ds(6 + k, parts, CAP), :] for k in range(2)]
    for r in range(6):
        own = wide_ref[pl.ds(r, parts, CAP), :]
        extra = pltpu.roll(spare[r // 3], 96 - 32 * (r % 3), axis=1)
        out_ref[pl.ds(r, parts, 6), :] = jnp.where(free, extra, own)


def unpack(packed_ref, wide_ref):
    parts = wide_ref.shape[0] // CAP
    lane = iota((parts, LANES), 1)
    rows = [packed_ref[pl.ds(r, parts, 6), :] for r in range(6)]
    for r in range(6):
        wide_ref[pl.ds(r, parts, CAP), :] = rows[r]
    for k in range(2):
        first, second, third = [pltpu.roll(rows[3 * k + c], 32 * c + 32, axis=1) for c in range(3)]
        value = jnp.where(lane < 32, first, jnp.where(lane < 64, second, third))
        wide_ref[pl.ds(6 + k, parts, CAP), :] = value


def slots_kernel(dest_ref, target_ref, labels_ref, slot_ref):
    dest = dest_ref[...]
    count = dest.shape[1]
    parts = labels_ref.shape[0]
    hits = flag(iota((parts, count), 0) == dest)
    earlier = flag(iota((count, count), 0) < iota((count, count), 1))
    running = dot(hits, earlier, NN)
    before = jnp.sum(running * hits.astype(F32), axis=0, keepdims=True)
    slot_ref[...] = dest * CAP + before.astype(jnp.int32)
    place = iota((LANES, count), 0).astype(F32)
    wanted = jnp.where(place == before, (target_ref[...] + 1).astype(F32), 0.0)
    labels_ref[...] = dot(hits, wanted.astype(BF16), NT)


def slots(dest, target, parts):
    count = dest.shape[1]
    return pl.pallas_call(
        slots_kernel,
        out_shape=(
            jax.ShapeDtypeStruct((parts, LANES), F32),
            jax.ShapeDtypeStruct((1, count), jnp.int32),
        ),
        compiler_params=limit(2),
        name="slots",
    )(*in_hbm(dest, target))


def prepare_kernel(
    parts, halo_ref, place_ref, columns_ref, coords_ref, after_ref, fluid_ref, force_ref,
    turned_ref, coords_out, local_ref, outer_ref, listed_ref,
    points, sems,
):
    copies = [
        pltpu.make_async_copy(ref, points.at[k], sems.at[k])
        for k, ref in enumerate((fluid_ref, force_ref))
    ]
    for copy in copies:
        copy.start()
    coords_out[...] = pad_rows(coords_ref[...], LANES)
    halo = listed_ref.shape[0]
    core = place_ref[0] % 2
    at_end = jnp.logical_or(place_ref[0] == 0, place_ref[0] == parts - 1)
    held = jnp.where(at_end, halo, 2 * halo)
    for neighbor in range(2):
        column = columns_ref[pl.ds(neighbor, 1), :]
        local_ref[neighbor] = flag(iota((LANES, LANES), 0) == column)
        outer = (column - LANES) ^ ((1 - core) * halo)
        outer = jnp.where(outer < held, outer, -1)
        outer_ref[neighbor] = flag(iota(outer_ref.shape[1:], 0) == outer)
    rows = iota(listed_ref.shape, 0)
    column = jnp.zeros(listed_ref.shape, jnp.int32)
    for h in range(listed_ref.shape[0]):
        column = jnp.where(rows == h, halo_ref[h], column)
    listed_ref[...] = flag(column == iota(listed_ref.shape, 1))
    for copy in copies:
        copy.wait()
    for group in range(points.shape[2] // LANES):
        lanes = pl.ds(group * LANES, LANES)
        length = jnp.zeros(turned_ref.shape[2:], F32)
        for c in range(3):
            position = points[0, c, lanes, :].T * (1.0 / SUPPORT)
            length = length + position * position
            turned_ref[group, c] = position * -2.0
            turned_ref[group, 3 + c] = points[1, c, lanes, :].T * 4.0
        turned_ref[group, 6] = length


def prepare(halo_list, place, columns, coords, after, fluid, force):
    count, nodes = fluid.shape[1:]
    halo = halo_list.shape[0]
    return pl.pallas_call(
        functools.partial(prepare_kernel, after.shape[0]),
        out_shape=(
            pltpu.VMEM((count // LANES, 7, nodes, LANES), F32),
            pltpu.VMEM((LANES, LANES), F32),
            pltpu.VMEM((2, LANES, LANES), BF16),
            pltpu.VMEM((2, 2 * halo, LANES), BF16),
            pltpu.VMEM((halo, LANES), BF16),
        ),
        in_specs=[SMEM, SMEM, VMEM, VMEM] + [ANY] * 3,
        out_specs=[VMEM] * 5,
        scratch_shapes=[pltpu.VMEM((2, 3, count, nodes), F32), pltpu.SemaphoreType.DMA((2,))],
        compiler_params=limit(4),
        cost_estimate=pl.CostEstimate(flops=0, bytes_accessed=3 * MIB, transcendentals=0),
        name="prepare",
    )(*in_hbm(halo_list, place, columns, coords, after, fluid, force))


def answer_kernel(labels_ref, coords_ref, onehot_ref, out_ref, wide):
    rows = onehot_ref.shape[0]
    parts = labels_ref.shape[0]
    repeat = flag(iota((rows, parts), 0) // CAP == iota((rows, parts), 1))
    spread = dot(repeat, labels_ref[...].astype(BF16), NN)
    own = iota((rows, LANES), 0) % CAP == iota((rows, LANES), 1)
    own_label = jnp.where(own, spread, 0.0).astype(BF16)
    label = dot(own_label, jnp.ones((LANES, LANES), BF16), NN)
    onehot = flag(label == (iota((rows, LANES), 1) + 1).astype(F32))
    onehot_ref[...] = onehot
    wide[...] = pick_from(onehot, coords_ref[...])
    pack(wide, out_ref)


def answer(labels, coords):
    rows = labels.shape[0] * CAP
    return pl.pallas_call(
        answer_kernel,
        out_shape=(
            jax.ShapeDtypeStruct((rows, LANES), BF16),
            jax.ShapeDtypeStruct((rows * 3 // 4, LANES), F32),
        ),
        in_specs=[VMEM, VMEM],
        scratch_shapes=[pltpu.VMEM((rows, LANES), F32)],
        compiler_params=limit(6),
        name="answer",
    )(labels, *near_core(coords))


def transfer_kernel(
    slot_ref, coords_ref, turned_ref, blocks_ref, precond_ref, out_ref, blocks_out, precond_out,
    wide, struct, mapped, sems,
):
    tables = [
        pltpu.make_async_copy(precond_ref, precond_out, sems.at[0]),
        pltpu.make_async_copy(blocks_ref, blocks_out, sems.at[1]),
    ]
    for copy in tables:
        copy.start()
    rows = wide.shape[0]
    count = slot_ref.shape[1]
    unpack(coords_ref, wide)
    chosen = flag(iota((rows, count), 0) == slot_ref[...])
    struct[...] = pick(wide[...], chosen, TN) * (1.0 / SUPPORT)
    nodes = turned_ref.shape[2]
    for group in range(count // LANES):
        lanes = pl.ds(group * LANES, LANES)
        where = [struct[pl.ds(c * 32, 32), lanes] for c in range(3)]
        length = where[0] * where[0] + where[1] * where[1] + where[2] * where[2]

        def body(step, sums):
            sums = list(sums)
            for k in range(8):
                n = pl.ds(step * 8 + k, 1)
                square = length + turned_ref[group, 6, n, :]
                for c in range(3):
                    square = square + where[c] * turned_ref[group, c, n, :]
                square = jnp.maximum(square, 1e-30)
                left = jnp.maximum(1.0 - square * lax.rsqrt(square), 0.0)
                twice = left * left
                quarter = twice * twice * (1.25 - left)
                for c in range(3):
                    sums[c] = sums[c] + quarter * turned_ref[group, 3 + c, n, :]
            return tuple(sums)

        zero = jnp.zeros((32, LANES), F32)
        sums = lax.fori_loop(0, nodes // 8, body, (zero, zero, zero))
        for c in range(3):
            mapped[pl.ds(c * 32, 32), lanes] = sums[c]
    mapped[pl.ds(96, 32), :] = jnp.zeros((32, count), F32)
    wide[...] = pick_from(chosen, mapped[...])
    pack(wide, out_ref)
    for copy in tables:
        copy.wait()


def transfer(slot, coords, turned, blocks, precond):
    count = slot.shape[1]
    return pl.pallas_call(
        transfer_kernel,
        out_shape=(
            jax.ShapeDtypeStruct(coords.shape, F32),
            pltpu.VMEM(blocks.shape, F32),
            pltpu.VMEM(precond.shape, F32),
        ),
        in_specs=[VMEM] * 3 + [ANY] * 2,
        out_specs=[VMEM] * 3,
        scratch_shapes=[
            pltpu.VMEM((coords.shape[0] * 4 // 3, LANES), F32),
            pltpu.VMEM((LANES, count), F32),
            pltpu.VMEM((LANES, count), F32),
            pltpu.SemaphoreType.DMA((2,)),
        ],
        compiler_params=limit(10),
        name="transfer",
    )(slot, coords, *near_core(turned), *in_hbm(blocks, precond))


def times(matrices, vectors, put):
    rows = vectors[0].shape[0]

    def body(step, carry):
        for k in range(8):
            row = step * 8 + k
            total = None
            for matrix, vector in zip(matrices, vectors):
                term = matrix[row] * vector
                total = term if total is None else total + term
            put(row, jnp.sum(total, axis=0, keepdims=True))
        return carry

    lax.fori_loop(0, rows // 8, body, 0)


def precondition(precond_ref, listed_ref, vector, out_ref, send_ref):
    def put(row, value):
        out_ref[pl.ds(row, 1), :] = value

    times([precond_ref], [vector], put)
    send_ref[...] = pick_from(listed_ref[...], pad_rows(out_ref[...], LANES))


def start_kernel(
    mapped_ref, onehot_ref, precond_ref, listed_ref, load_ref, pre_ref, send_ref, wide
):
    unpack(mapped_ref, wide)
    load = pick(wide[...], onehot_ref[...], TN)[: load_ref.shape[0]]
    load_ref[...] = load
    precondition(precond_ref, listed_ref, load, pre_ref, send_ref)


def start(mapped, onehot, precond, listed):
    shape = pltpu.VMEM((precond.shape[0], LANES), F32)
    return pl.pallas_call(
        start_kernel,
        out_shape=(shape, shape, pltpu.VMEM(listed.shape, F32)),
        in_specs=[VMEM] * 4,
        out_specs=[VMEM] * 3,
        scratch_shapes=[pltpu.VMEM(onehot.shape, F32)],
        compiler_params=limit(6),
        name="start",
    )(mapped, onehot, *near_core(precond, listed))


def inside_kernel(blocks_ref, local_ref, outer_ref, old_ref, pre_ref, near_ref, part_ref, taken_ref):
    pre = pre_ref[...]
    size = pre.shape[0]
    count = near_ref.shape[0]

    def put(row, value):
        part_ref[pl.ds(row, 1), :] = value - old_ref[pl.ds(row, 1), :]

    times([blocks_ref.at[0]], [pre], put)
    for neighbor in range(2):
        taken = pick(pre, local_ref[neighbor], NN)
        taken_ref[neighbor] = taken + pick(near_ref[...], outer_ref[neighbor, :count, :], TN)[:size]


def inside(blocks, local, outer, old, pre, near):
    size = old.shape[0]
    return pl.pallas_call(
        inside_kernel,
        out_shape=(pltpu.VMEM(old.shape, F32), pltpu.VMEM((2, size, LANES), F32)),
        in_specs=[VMEM] * 6,
        out_specs=[VMEM] * 2,
        compiler_params=limit(6),
        cost_estimate=pl.CostEstimate(flops=0, bytes_accessed=2 * MIB, transcendentals=0),
        name="inside",
    )(*near_core(blocks, local, outer, old, pre, near))


def outside(blocks_ref, outer_ref, part_ref, taken_ref, far_ref, new_ref):
    size = part_ref.shape[0]
    count = far_ref.shape[0]
    vectors = [
        taken_ref[neighbor] + pick(far_ref[...], outer_ref[neighbor, count:, :], TN)[:size]
        for neighbor in range(2)
    ]

    def put(row, value):
        new_ref[pl.ds(row, 1), :] = value + part_ref[pl.ds(row, 1), :]

    times([blocks_ref.at[1], blocks_ref.at[2]], vectors, put)


def step_kernel(
    blocks_ref, precond_ref, outer_ref, listed_ref, part_ref, taken_ref, far_ref,
    new_ref, new_pre_ref, send_ref,
):
    outside(blocks_ref, outer_ref, part_ref, taken_ref, far_ref, new_ref)
    precondition(precond_ref, listed_ref, new_ref[...], new_pre_ref, send_ref)


def step(blocks, precond, outer, listed, part, taken, far):
    shape = pltpu.VMEM(part.shape, F32)
    return pl.pallas_call(
        step_kernel,
        out_shape=(shape, shape, pltpu.VMEM(far.shape, F32)),
        in_specs=[VMEM] * 7,
        out_specs=[VMEM] * 3,
        compiler_params=limit(6),
        name="step",
    )(*near_core(blocks, precond, outer, listed, part, taken, far))


PAIRS = [(i, j) for i in range(STEPS + 1) for j in range(i, STEPS + 1)]


def last_kernel(
    blocks_ref, outer_ref, part_ref, taken_ref, far_ref, b0_ref, b1_ref, b2_ref, b3_ref,
    new_ref, sums_ref,
):
    outside(blocks_ref, outer_ref, part_ref, taken_ref, far_ref, new_ref)
    vectors = [ref[...] for ref in (b0_ref, b1_ref, b2_ref, b3_ref, new_ref)]
    sums = [jnp.sum(vectors[i] * vectors[j], axis=0, keepdims=True) for i, j in PAIRS]
    sums.append(jnp.zeros((LANES - len(sums), LANES), F32))
    ones = jnp.ones((sums_ref.shape[0], LANES), BF16)
    sums_ref[...] = pick_from(ones, jnp.concatenate(sums, axis=0))


def last(blocks, outer, part, taken, far, basis, parts):
    return pl.pallas_call(
        last_kernel,
        out_shape=(pltpu.VMEM(part.shape, F32), pltpu.VMEM((parts, LANES), F32)),
        in_specs=[VMEM] * 9,
        out_specs=[VMEM] * 2,
        compiler_params=limit(6),
        name="last",
    )(*near_core(blocks, outer, part, taken, far, *basis))


def plus(x, y):
    return [a + b for a, b in zip(x, y)]


def scaled(scale, x):
    return [scale * a for a in x]


def recurrences(product):
    def inner(x, y):
        return sum(
            a * b * product[min(i, j), max(i, j)]
            for i, a in enumerate(x)
            for j, b in enumerate(y)
        )

    def image_of(x):
        return plus([x[0] * 0.0] + x, x + [x[0] * 0.0])

    one = product[0, 0] * 0.0 + 1.0
    residual = search = shadow = [one]
    answer = []
    alignment = product[0, 0]

    def add(x, y):
        size = max(len(x), len(y))
        zero = one * 0.0
        return plus(x + [zero] * (size - len(x)), y + [zero] * (size - len(y)))

    for iteration in range(2):
        image = image_of(search)
        step_size = alignment / inner(shadow, image)
        middle = add(residual, scaled(-step_size, image))
        middle_image = image_of(middle)
        smoothing = inner(middle_image, middle) / inner(middle_image, middle_image)
        answer = add(answer, add(scaled(step_size, search), scaled(smoothing, middle)))
        residual = add(middle, scaled(-smoothing, middle_image))
        if iteration == 0:
            new_alignment = inner(shadow, residual)
            momentum = new_alignment / alignment * (step_size / smoothing)
            search = add(residual, scaled(momentum, add(search, scaled(-smoothing, image))))
            alignment = new_alignment
    return answer, residual


def finish_kernel(sums_ref, *refs):
    basis, pres, (solution_ref, residual_ref) = refs[:5], refs[5:9], refs[9:]
    totals = jnp.sum(sums_ref[...], axis=0, keepdims=True)
    product = {pair: totals[:, k : k + 1] for k, pair in enumerate(PAIRS)}
    answer, residual = recurrences(product)
    solution_ref[...] = sum(a * ref[...] for a, ref in zip(answer, pres))
    residual_ref[...] = sum(a * ref[...] for a, ref in zip(residual, basis))


def finish(sums, basis, pres):
    shape = jax.ShapeDtypeStruct(pres[0].shape, F32)
    return pl.pallas_call(
        finish_kernel,
        out_shape=(shape, shape),
        in_specs=[VMEM] * 10,
        compiler_params=limit(4),
        name="finish",
    )(*near_core(sums, *basis, *pres))


def to_near(send):
    devices = lax.axis_size(DOM)
    return lax.ppermute(send, DOM, [(i, i ^ 1) for i in range(devices)])


def to_far(send, closed):
    devices = lax.axis_size(DOM)
    pairs = [(i, (i + 1) % devices) for i in range(1, devices if closed else devices - 1, 2)]
    return lax.ppermute(send, DOM, pairs + [(j, i) for i, j in pairs])


def to_all(x):
    return lax.all_to_all(x, DOM, split_axis=0, concat_axis=0, tiled=True)


def on_device(
    traction, fluid_coords, struct_coords, dest, target, blocks, columns, halo_list, precond
):
    parts = lax.axis_size(DOM)
    place = lax.axis_index(DOM).astype(jnp.int32).reshape(1)
    force = jnp.transpose(traction, (1, 0, 2))
    fluid = jnp.transpose(fluid_coords, (1, 0, 2))
    coords = struct_coords.reshape(-1, struct_coords.shape[2])
    wanted, slot = slots(dest.reshape(1, -1), target.reshape(1, -1), parts)
    turned, coords, local, outer, listed = prepare(
        halo_list, place, columns, coords, wanted, fluid, force
    )
    onehot, answered = answer(to_all(wanted), coords)
    answered = to_all(answered.reshape(parts, 1, -1)).reshape(answered.shape)
    mapped, blocks, precond = transfer(slot, answered, turned, blocks, precond)
    mapped = to_all(mapped.reshape(parts, 1, -1)).reshape(mapped.shape)
    load, pre, send = start(mapped, onehot, precond, listed)
    basis, pres = [load], [pre]
    for j in range(STEPS):
        far = to_far(send, j > 0)
        near = to_near(send)
        part, taken = inside(blocks, local, outer, basis[-1], pres[-1], near)
        if j < STEPS - 1:
            new, pre, send = step(blocks, precond, outer, listed, part, taken, far)
            pres.append(pre)
        else:
            new, sums = last(blocks, outer, part, taken, far, basis, parts)
        basis.append(new)
    solution, residual = finish(to_all(sums), basis, pres)
    return load, solution, residual


def solution(mesh):
    in_specs = (
        P(DOM, None, None),
        P(DOM, None, None),
        P(None, None, DOM),
        P(DOM, None),
        P(DOM),
        P(None, None, None, DOM),
        P(None, DOM),
        P(DOM),
        P(None, None, DOM),
    )
    out_specs = (P(None, DOM), P(None, DOM), P(None, DOM))
    return jax.shard_map(
        on_device, mesh=mesh, in_specs=in_specs, out_specs=out_specs, check_vma=False
    )
```

```python
import functools

import jax
import jax.numpy as jnp
from jax import lax
from jax.experimental import pallas as pl
from jax.experimental.pallas import tpu as pltpu
from jax.sharding import PartitionSpec as P

DOM = "dom"
SUPPORT = 0.9
CAP = 8
LANES = 128
STEPS = 4
KNOWN = [(i, j) for j in range(STEPS) for i in range(j + 1)]
HELD = 16
F32 = jnp.float32
BF16 = jnp.bfloat16
NN = (((1,), (0,)), ((), ()))
NT = (((1,), (1,)), ((), ()))
TN = (((0,), (0,)), ((), ()))


SMEM = pl.BlockSpec(memory_space=pltpu.SMEM)
VMEM = pl.BlockSpec(memory_space=pltpu.VMEM)
ANY = pl.BlockSpec(memory_space=pl.ANY)
MIB = 1 << 20


def limit(mib):
    return pltpu.CompilerParams(vmem_limit_bytes=mib * MIB)


def near_core(*arrays):
    return [pltpu.with_memory_space_constraint(x, pltpu.VMEM) for x in arrays]


def in_hbm(*arrays):
    return [pltpu.with_memory_space_constraint(x, pltpu.HBM) for x in arrays]


def iota(shape, dim):
    return lax.broadcasted_iota(jnp.int32, shape, dim)


def flag(mask):
    return jnp.where(mask, 1.0, 0.0).astype(BF16)


def split3(x):
    high = x.astype(BF16)
    rest = x - high.astype(F32)
    mid = rest.astype(BF16)
    low = (rest - mid.astype(F32)).astype(BF16)
    return high, mid, low


def dot(a, b, dims):
    return lax.dot_general(a, b, dims, preferred_element_type=F32)


def three(product, size, axis):
    parts = [lax.slice_in_dim(product, k * size, (k + 1) * size, axis=axis) for k in range(3)]
    return parts[0] + (parts[1] + parts[2])


def pick(x, onehot, dims):
    free = 0 if dims == NN else 1
    stacked = jnp.concatenate(split3(x), axis=free)
    return three(dot(stacked, onehot, dims), x.shape[free], 0)


def pick_from(onehot, x):
    return three(dot(onehot, jnp.concatenate(split3(x), axis=0), NT), x.shape[0], 1)


def pad_rows(x, rows):
    if x.shape[0] == rows:
        return x
    return jnp.concatenate([x, jnp.zeros((rows - x.shape[0], x.shape[1]), x.dtype)], axis=0)


def pack(wide_ref, out_ref):
    parts = wide_ref.shape[0] // CAP
    free = iota((parts, LANES), 1) >= 96
    spare = [wide_ref[pl.ds(6 + k, parts, CAP), :] for k in range(2)]
    for r in range(6):
        own = wide_ref[pl.ds(r, parts, CAP), :]
        extra = pltpu.roll(spare[r // 3], 96 - 32 * (r % 3), axis=1)
        out_ref[pl.ds(r, parts, 6), :] = jnp.where(free, extra, own)


def unpack(packed_ref, wide_ref):
    parts = wide_ref.shape[0] // CAP
    lane = iota((parts, LANES), 1)
    rows = [packed_ref[pl.ds(r, parts, 6), :] for r in range(6)]
    for r in range(6):
        wide_ref[pl.ds(r, parts, CAP), :] = rows[r]
    for k in range(2):
        first, second, third = [pltpu.roll(rows[3 * k + c], 32 * c + 32, axis=1) for c in range(3)]
        value = jnp.where(lane < 32, first, jnp.where(lane < 64, second, third))
        wide_ref[pl.ds(6 + k, parts, CAP), :] = value


def slots_kernel(dest_ref, target_ref, labels_ref, slot_ref):
    dest = dest_ref[...]
    count = dest.shape[1]
    parts = labels_ref.shape[0]
    hits = flag(iota((parts, count), 0) == dest)
    earlier = flag(iota((count, count), 0) < iota((count, count), 1))
    running = dot(hits, earlier, NN)
    before = jnp.sum(running * hits.astype(F32), axis=0, keepdims=True)
    slot_ref[...] = dest * CAP + before.astype(jnp.int32)
    place = iota((LANES, count), 0).astype(F32)
    wanted = jnp.where(place == before, (target_ref[...] + 1).astype(F32), 0.0)
    labels_ref[...] = dot(hits, wanted.astype(BF16), NT)


def slots(dest, target, parts):
    count = dest.shape[1]
    return pl.pallas_call(
        slots_kernel,
        out_shape=(
            jax.ShapeDtypeStruct((parts, LANES), F32),
            jax.ShapeDtypeStruct((1, count), jnp.int32),
        ),
        compiler_params=limit(2),
        name="slots",
    )(*in_hbm(dest, target))


def prepare_kernel(
    parts, halo_ref, place_ref, columns_ref, coords_ref, after_ref, fluid_ref, force_ref,
    turned_ref, coords_out, local_ref, outer_ref, listed_ref,
    points, sems,
):
    copies = [
        pltpu.make_async_copy(ref, points.at[k], sems.at[k])
        for k, ref in enumerate((fluid_ref, force_ref))
    ]
    for copy in copies:
        copy.start()
    coords_out[...] = pad_rows(coords_ref[...], LANES)
    halo = listed_ref.shape[0]
    core = place_ref[0] % 2
    at_end = jnp.logical_or(place_ref[0] == 0, place_ref[0] == parts - 1)
    held = jnp.where(at_end, halo, 2 * halo)
    for neighbor in range(2):
        column = columns_ref[pl.ds(neighbor, 1), :]
        local_ref[neighbor] = flag(iota((LANES, LANES), 0) == column)
        outer = (column - LANES) ^ ((1 - core) * halo)
        outer = jnp.where(outer < held, outer, -1)
        outer_ref[neighbor] = flag(iota(outer_ref.shape[1:], 0) == outer)
    rows = iota(listed_ref.shape, 0)
    column = jnp.zeros(listed_ref.shape, jnp.int32)
    for h in range(listed_ref.shape[0]):
        column = jnp.where(rows == h, halo_ref[h], column)
    listed_ref[...] = flag(column == iota(listed_ref.shape, 1))
    for copy in copies:
        copy.wait()
    for group in range(points.shape[2] // LANES):
        lanes = pl.ds(group * LANES, LANES)
        length = jnp.zeros(turned_ref.shape[2:], F32)
        for c in range(3):
            position = points[0, c, lanes, :].T * (1.0 / SUPPORT)
            length = length + position * position
            turned_ref[group, c] = position * -2.0
            turned_ref[group, 3 + c] = points[1, c, lanes, :].T * 4.0
        turned_ref[group, 6] = length


def prepare(halo_list, place, columns, coords, after, fluid, force):
    count, nodes = fluid.shape[1:]
    halo = halo_list.shape[0]
    return pl.pallas_call(
        functools.partial(prepare_kernel, after.shape[0]),
        out_shape=(
            pltpu.VMEM((count // LANES, 7, nodes, LANES), F32),
            pltpu.VMEM((LANES, LANES), F32),
            pltpu.VMEM((2, LANES, LANES), BF16),
            pltpu.VMEM((2, 2 * halo, LANES), BF16),
            pltpu.VMEM((halo, LANES), BF16),
        ),
        in_specs=[SMEM, SMEM, VMEM, VMEM] + [ANY] * 3,
        out_specs=[VMEM] * 5,
        scratch_shapes=[pltpu.VMEM((2, 3, count, nodes), F32), pltpu.SemaphoreType.DMA((2,))],
        compiler_params=limit(4),
        cost_estimate=pl.CostEstimate(flops=0, bytes_accessed=3 * MIB, transcendentals=0),
        name="prepare",
    )(*in_hbm(halo_list, place, columns, coords, after, fluid, force))


def answer_kernel(labels_ref, coords_ref, onehot_ref, out_ref, wide):
    rows = onehot_ref.shape[0]
    parts = labels_ref.shape[0]
    repeat = flag(iota((rows, parts), 0) // CAP == iota((rows, parts), 1))
    spread = dot(repeat, labels_ref[...].astype(BF16), NN)
    own = iota((rows, LANES), 0) % CAP == iota((rows, LANES), 1)
    own_label = jnp.where(own, spread, 0.0).astype(BF16)
    label = dot(own_label, jnp.ones((LANES, LANES), BF16), NN)
    onehot = flag(label == (iota((rows, LANES), 1) + 1).astype(F32))
    onehot_ref[...] = onehot
    wide[...] = pick_from(onehot, coords_ref[...])
    pack(wide, out_ref)


def answer(labels, coords):
    rows = labels.shape[0] * CAP
    return pl.pallas_call(
        answer_kernel,
        out_shape=(
            jax.ShapeDtypeStruct((rows, LANES), BF16),
            jax.ShapeDtypeStruct((rows * 3 // 4, LANES), F32),
        ),
        in_specs=[VMEM, VMEM],
        scratch_shapes=[pltpu.VMEM((rows, LANES), F32)],
        compiler_params=limit(6),
        name="answer",
    )(labels, *near_core(coords))


def transfer_kernel(
    slot_ref, coords_ref, turned_ref, blocks_ref, precond_ref, out_ref, blocks_out, precond_out,
    wide, struct, mapped, sems,
):
    tables = [
        pltpu.make_async_copy(precond_ref, precond_out, sems.at[0]),
        pltpu.make_async_copy(blocks_ref, blocks_out, sems.at[1]),
    ]
    for copy in tables:
        copy.start()
    rows = wide.shape[0]
    count = slot_ref.shape[1]
    unpack(coords_ref, wide)
    chosen = flag(iota((rows, count), 0) == slot_ref[...])
    struct[...] = pick(wide[...], chosen, TN) * (1.0 / SUPPORT)
    nodes = turned_ref.shape[2]
    for group in range(count // LANES):
        lanes = pl.ds(group * LANES, LANES)
        where = [struct[pl.ds(c * 32, 32), lanes] for c in range(3)]
        length = where[0] * where[0] + where[1] * where[1] + where[2] * where[2]

        def body(step, sums):
            sums = list(sums)
            for k in range(8):
                n = pl.ds(step * 8 + k, 1)
                square = length + turned_ref[group, 6, n, :]
                for c in range(3):
                    square = square + where[c] * turned_ref[group, c, n, :]
                square = jnp.maximum(square, 1e-30)
                left = jnp.maximum(1.0 - square * lax.rsqrt(square), 0.0)
                twice = left * left
                quarter = twice * twice * (1.25 - left)
                for c in range(3):
                    sums[c] = sums[c] + quarter * turned_ref[group, 3 + c, n, :]
            return tuple(sums)

        zero = jnp.zeros((32, LANES), F32)
        sums = lax.fori_loop(0, nodes // 8, body, (zero, zero, zero))
        for c in range(3):
            mapped[pl.ds(c * 32, 32), lanes] = sums[c]
    mapped[pl.ds(96, 32), :] = jnp.zeros((32, count), F32)
    wide[...] = pick_from(chosen, mapped[...])
    pack(wide, out_ref)
    for copy in tables:
        copy.wait()


def transfer(slot, coords, turned, blocks, precond):
    count = slot.shape[1]
    return pl.pallas_call(
        transfer_kernel,
        out_shape=(
            jax.ShapeDtypeStruct(coords.shape, F32),
            pltpu.VMEM(blocks.shape, F32),
            pltpu.VMEM(precond.shape, F32),
        ),
        in_specs=[VMEM] * 3 + [ANY] * 2,
        out_specs=[VMEM] * 3,
        scratch_shapes=[
            pltpu.VMEM((coords.shape[0] * 4 // 3, LANES), F32),
            pltpu.VMEM((LANES, count), F32),
            pltpu.VMEM((LANES, count), F32),
            pltpu.SemaphoreType.DMA((2,)),
        ],
        compiler_params=limit(10),
        name="transfer",
    )(slot, coords, *near_core(turned), *in_hbm(blocks, precond))


def times(matrices, vectors, put):
    rows = vectors[0].shape[0]

    def body(step, carry):
        for k in range(8):
            row = step * 8 + k
            total = None
            for matrix, vector in zip(matrices, vectors):
                term = matrix[row] * vector
                total = term if total is None else total + term
            put(row, jnp.sum(total, axis=0, keepdims=True))
        return carry

    lax.fori_loop(0, rows // 8, body, 0)


def precondition(precond_ref, listed_ref, vector, out_ref, send_ref):
    def put(row, value):
        out_ref[pl.ds(row, 1), :] = value

    times([precond_ref], [vector], put)
    send_ref[...] = pick_from(listed_ref[...], pad_rows(out_ref[...], LANES))


def start_kernel(
    mapped_ref, onehot_ref, precond_ref, listed_ref, load_ref, pre_ref, send_ref, wide
):
    unpack(mapped_ref, wide)
    load = pick(wide[...], onehot_ref[...], TN)[: load_ref.shape[0]]
    load_ref[...] = load
    precondition(precond_ref, listed_ref, load, pre_ref, send_ref)


def start(mapped, onehot, precond, listed):
    shape = pltpu.VMEM((precond.shape[0], LANES), F32)
    return pl.pallas_call(
        start_kernel,
        out_shape=(shape, shape, pltpu.VMEM(listed.shape, F32)),
        in_specs=[VMEM] * 4,
        out_specs=[VMEM] * 3,
        scratch_shapes=[pltpu.VMEM(onehot.shape, F32)],
        compiler_params=limit(6),
        name="start",
    )(mapped, onehot, *near_core(precond, listed))


def inside_kernel(
    blocks_ref, local_ref, outer_ref, old_ref, pre_ref, near_ref, *refs
):
    earlier, (part_ref, taken_ref, *more) = refs[:-3], refs[-3:]
    pre = pre_ref[...]
    size = pre.shape[0]
    count = near_ref.shape[0]

    def put(row, value):
        part_ref[pl.ds(row, 1), :] = value - old_ref[pl.ds(row, 1), :]

    times([blocks_ref.at[0]], [pre], put)
    for neighbor in range(2):
        taken = pick(pre, local_ref[neighbor], NN)
        taken_ref[neighbor] = taken + pick(near_ref[...], outer_ref[neighbor, :count, :], TN)[:size]
    if not earlier:
        more[0][...] = old_ref[...]
    else:
        vectors = [ref[...] for ref in earlier] + [old_ref[...]]
        sums = [jnp.sum(vectors[i] * vectors[j], axis=0, keepdims=True) for i, j in KNOWN]
        more[0][...] = pad_rows(jnp.concatenate(sums, axis=0), HELD)


def inside(blocks, local, outer, old, pre, near, earlier):
    size = old.shape[0]
    more = pltpu.VMEM((HELD, LANES), F32) if earlier else jax.ShapeDtypeStruct(old.shape, F32)
    return pl.pallas_call(
        inside_kernel,
        out_shape=(pltpu.VMEM(old.shape, F32), pltpu.VMEM((2, size, LANES), F32), more),
        in_specs=[VMEM] * (6 + len(earlier)),
        out_specs=[VMEM] * 3,
        compiler_params=limit(6),
        cost_estimate=pl.CostEstimate(flops=0, bytes_accessed=2 * MIB, transcendentals=0),
        name="inside",
    )(*near_core(blocks, local, outer, old, pre, near, *earlier))


def outside(blocks_ref, outer_ref, part_ref, taken_ref, far_ref, new_ref):
    size = part_ref.shape[0]
    count = far_ref.shape[0]
    vectors = [
        taken_ref[neighbor] + pick(far_ref[...], outer_ref[neighbor, count:, :], TN)[:size]
        for neighbor in range(2)
    ]

    def put(row, value):
        new_ref[pl.ds(row, 1), :] = value + part_ref[pl.ds(row, 1), :]

    times([blocks_ref.at[1], blocks_ref.at[2]], vectors, put)


def step_kernel(
    blocks_ref, precond_ref, outer_ref, listed_ref, part_ref, taken_ref, far_ref,
    new_ref, new_pre_ref, send_ref,
):
    outside(blocks_ref, outer_ref, part_ref, taken_ref, far_ref, new_ref)
    precondition(precond_ref, listed_ref, new_ref[...], new_pre_ref, send_ref)


def step(blocks, precond, outer, listed, part, taken, far):
    shape = pltpu.VMEM(part.shape, F32)
    return pl.pallas_call(
        step_kernel,
        out_shape=(shape, shape, pltpu.VMEM(far.shape, F32)),
        in_specs=[VMEM] * 7,
        out_specs=[VMEM] * 3,
        compiler_params=limit(6),
        name="step",
    )(*near_core(blocks, precond, outer, listed, part, taken, far))


def last_kernel(
    blocks_ref, outer_ref, part_ref, taken_ref, far_ref, known_ref, b0_ref, b1_ref, b2_ref, b3_ref,
    new_ref, sums_ref,
):
    outside(blocks_ref, outer_ref, part_ref, taken_ref, far_ref, new_ref)
    new = new_ref[...]
    vectors = [ref[...] for ref in (b0_ref, b1_ref, b2_ref, b3_ref)] + [new]
    sums = [known_ref[...]] + [jnp.sum(v * new, axis=0, keepdims=True) for v in vectors]
    ones = jnp.ones((sums_ref.shape[0], LANES), BF16)
    sums_ref[...] = pick_from(ones, pad_rows(jnp.concatenate(sums, axis=0), LANES))


def last(blocks, outer, part, taken, far, known, basis, parts):
    return pl.pallas_call(
        last_kernel,
        out_shape=(pltpu.VMEM(part.shape, F32), pltpu.VMEM((parts, LANES), F32)),
        in_specs=[VMEM] * 10,
        out_specs=[VMEM] * 2,
        compiler_params=limit(6),
        name="last",
    )(*near_core(blocks, outer, part, taken, far, known, *basis))


def plus(x, y):
    return [a + b for a, b in zip(x, y)]


def tree(terms):
    while len(terms) > 1:
        terms = [sum(terms[k : k + 2]) for k in range(0, len(terms), 2)]
    return terms[0]


def scaled(scale, x):
    return [scale * a for a in x]


def recurrences(product):
    def inner(x, y):
        return tree(
            [a * b * product[min(i, j), max(i, j)] for i, a in enumerate(x) for j, b in enumerate(y)]
        )

    def image_of(x):
        return plus([x[0] * 0.0] + x, x + [x[0] * 0.0])

    one = product[0, 0] * 0.0 + 1.0
    residual = search = shadow = [one]
    answer = []
    alignment = product[0, 0]

    def add(x, y):
        size = max(len(x), len(y))
        zero = one * 0.0
        return plus(x + [zero] * (size - len(x)), y + [zero] * (size - len(y)))

    for iteration in range(2):
        image = image_of(search)
        step_size = alignment / inner(shadow, image)
        middle = add(residual, scaled(-step_size, image))
        middle_image = image_of(middle)
        smoothing = inner(middle_image, middle) / inner(middle_image, middle_image)
        answer = add(answer, add(scaled(step_size, search), scaled(smoothing, middle)))
        residual = add(middle, scaled(-smoothing, middle_image))
        if iteration == 0:
            new_alignment = inner(shadow, residual)
            momentum = new_alignment / alignment * (step_size / smoothing)
            search = add(residual, scaled(momentum, add(search, scaled(-smoothing, image))))
            alignment = new_alignment
    return answer, residual


def finish_kernel(sums_ref, *refs):
    basis, pres, (solution_ref, residual_ref) = refs[:5], refs[5:9], refs[9:]
    totals = jnp.sum(sums_ref[...], axis=0, keepdims=True)
    lane = dict(zip(KNOWN, range(len(KNOWN))))
    lane.update({(i, STEPS): HELD + i for i in range(STEPS + 1)})
    product = {pair: totals[:, k : k + 1] for pair, k in lane.items()}
    answer, residual = recurrences(product)
    solution_ref[...] = sum(a * ref[...] for a, ref in zip(answer, pres))
    residual_ref[...] = sum(a * ref[...] for a, ref in zip(residual, basis))


def finish(sums, basis, pres):
    shape = jax.ShapeDtypeStruct(pres[0].shape, F32)
    return pl.pallas_call(
        finish_kernel,
        out_shape=(shape, shape),
        in_specs=[VMEM] * 10,
        compiler_params=limit(4),
        name="finish",
    )(*near_core(sums, *basis, *pres))


def to_near(send):
    devices = lax.axis_size(DOM)
    return lax.ppermute(send, DOM, [(i, i ^ 1) for i in range(devices)])


def to_far(send, closed):
    devices = lax.axis_size(DOM)
    pairs = [(i, (i + 1) % devices) for i in range(1, devices if closed else devices - 1, 2)]
    return lax.ppermute(send, DOM, pairs + [(j, i) for i, j in pairs])


def to_all(x):
    return lax.all_to_all(x, DOM, split_axis=0, concat_axis=0, tiled=True)


def on_device(
    traction, fluid_coords, struct_coords, dest, target, blocks, columns, halo_list, precond
):
    parts = lax.axis_size(DOM)
    place = lax.axis_index(DOM).astype(jnp.int32).reshape(1)
    force = jnp.transpose(traction, (1, 0, 2))
    fluid = jnp.transpose(fluid_coords, (1, 0, 2))
    coords = struct_coords.reshape(-1, struct_coords.shape[2])
    wanted, slot = slots(dest.reshape(1, -1), target.reshape(1, -1), parts)
    turned, coords, local, outer, listed = prepare(
        halo_list, place, columns, coords, wanted, fluid, force
    )
    onehot, answered = answer(to_all(wanted), coords)
    answered = to_all(answered.reshape(parts, 1, -1)).reshape(answered.shape)
    mapped, blocks, precond = transfer(slot, answered, turned, blocks, precond)
    mapped = to_all(mapped.reshape(parts, 1, -1)).reshape(mapped.shape)
    load, pre, send = start(mapped, onehot, precond, listed)
    basis, pres = [load], [pre]
    for j in range(STEPS):
        far = to_far(send, j > 0)
        near = to_near(send)
        earlier = basis[:-1] if j == STEPS - 1 else []
        part, taken, more = inside(blocks, local, outer, basis[-1], pres[-1], near, earlier)
        load_field = more if j == 0 else load_field
        if j < STEPS - 1:
            new, pre, send = step(blocks, precond, outer, listed, part, taken, far)
            pres.append(pre)
        else:
            new, sums = last(blocks, outer, part, taken, far, more, basis, parts)
        basis.append(new)
    solution, residual = finish(to_all(sums), basis, pres)
    return load_field, solution, residual


def solution(mesh):
    in_specs = (
        P(DOM, None, None),
        P(DOM, None, None),
        P(None, None, DOM),
        P(DOM, None),
        P(DOM),
        P(None, None, None, DOM),
        P(None, DOM),
        P(DOM),
        P(None, None, DOM),
    )
    out_specs = (P(None, DOM), P(None, DOM), P(None, DOM))
    return jax.shard_map(
        on_device, mesh=mesh, in_specs=in_specs, out_specs=out_specs, check_vma=False
    )
```

```python
import functools

import jax
import jax.numpy as jnp
from jax import lax
from jax.experimental import pallas as pl
from jax.experimental.pallas import tpu as pltpu
from jax.sharding import PartitionSpec as P

DOM = "dom"
SUPPORT = 0.9
CAP = 8
LANES = 128
STEPS = 4
KNOWN = [(i, j) for j in range(STEPS) for i in range(j + 1)]
HELD = 16
F32 = jnp.float32
BF16 = jnp.bfloat16
NN = (((1,), (0,)), ((), ()))
NT = (((1,), (1,)), ((), ()))
TN = (((0,), (0,)), ((), ()))


SMEM = pl.BlockSpec(memory_space=pltpu.SMEM)
VMEM = pl.BlockSpec(memory_space=pltpu.VMEM)
ANY = pl.BlockSpec(memory_space=pl.ANY)
MIB = 1 << 20


def limit(mib):
    return pltpu.CompilerParams(vmem_limit_bytes=mib * MIB)


def near_core(*arrays):
    return [pltpu.with_memory_space_constraint(x, pltpu.VMEM) for x in arrays]


def in_hbm(*arrays):
    return [pltpu.with_memory_space_constraint(x, pltpu.HBM) for x in arrays]


def iota(shape, dim):
    return lax.broadcasted_iota(jnp.int32, shape, dim)


def flag(mask):
    return jnp.where(mask, 1.0, 0.0).astype(BF16)


def split3(x):
    high = x.astype(BF16)
    rest = x - high.astype(F32)
    mid = rest.astype(BF16)
    low = (rest - mid.astype(F32)).astype(BF16)
    return high, mid, low


def dot(a, b, dims):
    return lax.dot_general(a, b, dims, preferred_element_type=F32)


def three(product, size, axis):
    parts = [lax.slice_in_dim(product, k * size, (k + 1) * size, axis=axis) for k in range(3)]
    return parts[0] + (parts[1] + parts[2])


def pick(x, onehot, dims):
    free = 0 if dims == NN else 1
    stacked = jnp.concatenate(split3(x), axis=free)
    return three(dot(stacked, onehot, dims), x.shape[free], 0)


def pick_from(onehot, x):
    return three(dot(onehot, jnp.concatenate(split3(x), axis=0), NT), x.shape[0], 1)


def pad_rows(x, rows):
    if x.shape[0] == rows:
        return x
    return jnp.concatenate([x, jnp.zeros((rows - x.shape[0], x.shape[1]), x.dtype)], axis=0)


def pack(wide_ref, out_ref):
    parts = wide_ref.shape[0] // CAP
    free = iota((parts, LANES), 1) >= 96
    spare = [wide_ref[pl.ds(6 + k, parts, CAP), :] for k in range(2)]
    for r in range(6):
        own = wide_ref[pl.ds(r, parts, CAP), :]
        extra = pltpu.roll(spare[r // 3], 96 - 32 * (r % 3), axis=1)
        out_ref[pl.ds(r, parts, 6), :] = jnp.where(free, extra, own)


def unpack(packed_ref, wide_ref):
    parts = wide_ref.shape[0] // CAP
    lane = iota((parts, LANES), 1)
    rows = [packed_ref[pl.ds(r, parts, 6), :] for r in range(6)]
    for r in range(6):
        wide_ref[pl.ds(r, parts, CAP), :] = rows[r]
    for k in range(2):
        first, second, third = [pltpu.roll(rows[3 * k + c], 32 * c + 32, axis=1) for c in range(3)]
        value = jnp.where(lane < 32, first, jnp.where(lane < 64, second, third))
        wide_ref[pl.ds(6 + k, parts, CAP), :] = value


def slots_kernel(dest_ref, target_ref, labels_ref, slot_ref):
    dest = dest_ref[...]
    count = dest.shape[1]
    parts = labels_ref.shape[0]
    hits = flag(iota((parts, count), 0) == dest)
    earlier = flag(iota((count, count), 0) < iota((count, count), 1))
    running = dot(hits, earlier, NN)
    before = jnp.sum(running * hits.astype(F32), axis=0, keepdims=True)
    slot_ref[...] = dest * CAP + before.astype(jnp.int32)
    place = iota((LANES, count), 0).astype(F32)
    wanted = jnp.where(place == before, (target_ref[...] + 1).astype(F32), 0.0)
    labels_ref[...] = dot(hits, wanted.astype(BF16), NT)


def slots(dest, target, parts):
    count = dest.shape[1]
    return pl.pallas_call(
        slots_kernel,
        out_shape=(
            jax.ShapeDtypeStruct((parts, LANES), F32),
            jax.ShapeDtypeStruct((1, count), jnp.int32),
        ),
        compiler_params=limit(2),
        name="slots",
    )(*in_hbm(dest, target))


def prepare_kernel(
    parts, halo_ref, place_ref, columns_ref, coords_ref, slot_ref, after_ref, fluid_ref, force_ref,
    turned_ref, chosen_ref, coords_out, local_ref, outer_ref, listed_ref,
    points, sems,
):
    copies = [
        pltpu.make_async_copy(ref, points.at[k], sems.at[k])
        for k, ref in enumerate((fluid_ref, force_ref))
    ]
    for copy in copies:
        copy.start()
    chosen_ref[...] = flag(iota(chosen_ref.shape, 0) == slot_ref[...])
    coords_out[...] = pad_rows(coords_ref[...], LANES)
    halo = listed_ref.shape[0]
    core = place_ref[0] % 2
    at_end = jnp.logical_or(place_ref[0] == 0, place_ref[0] == parts - 1)
    held = jnp.where(at_end, halo, 2 * halo)
    for neighbor in range(2):
        column = columns_ref[pl.ds(neighbor, 1), :]
        lanes = pl.ds(neighbor * LANES, LANES)
        local_ref[:, lanes] = flag(iota((LANES, LANES), 0) == column)
        outer = (column - LANES) ^ ((1 - core) * halo)
        outer = jnp.where(outer < held, outer, -1)
        outer_ref[:, lanes] = flag(iota((2 * halo, LANES), 0) == outer)
    rows = iota(listed_ref.shape, 0)
    column = jnp.zeros(listed_ref.shape, jnp.int32)
    for h in range(listed_ref.shape[0]):
        column = jnp.where(rows == h, halo_ref[h], column)
    listed_ref[...] = flag(column == iota(listed_ref.shape, 1))
    for copy in copies:
        copy.wait()
    for group in range(points.shape[2] // LANES):
        lanes = pl.ds(group * LANES, LANES)
        length = jnp.zeros(turned_ref.shape[2:], F32)
        for c in range(3):
            position = points[0, c, lanes, :].T * (1.0 / SUPPORT)
            length = length + position * position
            turned_ref[group, c] = position * -2.0
            turned_ref[group, 3 + c] = points[1, c, lanes, :].T * 4.0
        turned_ref[group, 6] = length


def prepare(halo_list, place, columns, coords, slot, after, fluid, force):
    count, nodes = fluid.shape[1:]
    halo = halo_list.shape[0]
    return pl.pallas_call(
        functools.partial(prepare_kernel, after.shape[0]),
        out_shape=(
            pltpu.VMEM((count // LANES, 7, nodes, LANES), F32),
            pltpu.VMEM((after.shape[0] * CAP, count), BF16),
            pltpu.VMEM((LANES, LANES), F32),
            pltpu.VMEM((LANES, 2 * LANES), BF16),
            pltpu.VMEM((2 * halo, 2 * LANES), BF16),
            pltpu.VMEM((halo, LANES), BF16),
        ),
        in_specs=[SMEM, SMEM, VMEM, VMEM, VMEM] + [ANY] * 3,
        out_specs=[VMEM] * 6,
        scratch_shapes=[pltpu.VMEM((2, 3, count, nodes), F32), pltpu.SemaphoreType.DMA((2,))],
        compiler_params=limit(4),
        cost_estimate=pl.CostEstimate(flops=0, bytes_accessed=3 * MIB, transcendentals=0),
        name="prepare",
    )(*in_hbm(halo_list, place, columns, coords), slot, *in_hbm(after, fluid, force))


def answer_kernel(labels_ref, coords_ref, onehot_ref, out_ref, wide):
    rows = onehot_ref.shape[0]
    parts = labels_ref.shape[0]
    repeat = flag(iota((rows, parts), 0) // CAP == iota((rows, parts), 1))
    spread = dot(repeat, labels_ref[...].astype(BF16), NN)
    own = iota((rows, LANES), 0) % CAP == iota((rows, LANES), 1)
    own_label = jnp.where(own, spread, 0.0).astype(BF16)
    label = dot(own_label, jnp.ones((LANES, LANES), BF16), NN)
    onehot = flag(label == (iota((rows, LANES), 1) + 1).astype(F32))
    onehot_ref[...] = onehot
    wide[...] = pick_from(onehot, coords_ref[...])
    pack(wide, out_ref)


def answer(labels, coords):
    rows = labels.shape[0] * CAP
    return pl.pallas_call(
        answer_kernel,
        out_shape=(
            jax.ShapeDtypeStruct((rows, LANES), BF16),
            jax.ShapeDtypeStruct((rows * 3 // 4, LANES), F32),
        ),
        in_specs=[VMEM, VMEM],
        scratch_shapes=[pltpu.VMEM((rows, LANES), F32)],
        compiler_params=limit(6),
        name="answer",
    )(labels, *near_core(coords))


def transfer_kernel(
    chosen_ref, coords_ref, turned_ref, blocks_ref, precond_ref, out_ref, blocks_out, precond_out,
    wide, struct, mapped, sems,
):
    tables = [
        pltpu.make_async_copy(precond_ref, precond_out, sems.at[0]),
        pltpu.make_async_copy(blocks_ref, blocks_out, sems.at[1]),
    ]
    for copy in tables:
        copy.start()
    count = chosen_ref.shape[1]
    unpack(coords_ref, wide)
    struct[...] = pick(wide[...], chosen_ref[...], TN) * (1.0 / SUPPORT)
    nodes = turned_ref.shape[2]
    for group in range(count // LANES):
        lanes = pl.ds(group * LANES, LANES)
        where = [struct[pl.ds(c * 32, 32), lanes] for c in range(3)]
        length = where[0] * where[0] + where[1] * where[1] + where[2] * where[2]

        def body(step, sums):
            sums = list(sums)
            for k in range(8):
                n = pl.ds(step * 8 + k, 1)
                square = length + turned_ref[group, 6, n, :]
                for c in range(3):
                    square = square + where[c] * turned_ref[group, c, n, :]
                square = jnp.maximum(square, 1e-30)
                left = jnp.maximum(1.0 - square * lax.rsqrt(square), 0.0)
                twice = left * left
                quarter = twice * twice * (1.25 - left)
                for c in range(3):
                    sums[c] = sums[c] + quarter * turned_ref[group, 3 + c, n, :]
            return tuple(sums)

        zero = jnp.zeros((32, LANES), F32)
        sums = lax.fori_loop(0, nodes // 8, body, (zero, zero, zero))
        for c in range(3):
            mapped[pl.ds(c * 32, 32), lanes] = sums[c]
    mapped[pl.ds(96, 32), :] = jnp.zeros((32, count), F32)
    wide[...] = pick_from(chosen_ref[...], mapped[...])
    pack(wide, out_ref)
    for copy in tables:
        copy.wait()


def transfer(chosen, coords, turned, blocks, precond):
    count = chosen.shape[1]
    return pl.pallas_call(
        transfer_kernel,
        out_shape=(
            jax.ShapeDtypeStruct(coords.shape, F32),
            pltpu.VMEM(blocks.shape, F32),
            pltpu.VMEM(precond.shape, F32),
        ),
        in_specs=[VMEM] * 3 + [ANY] * 2,
        out_specs=[VMEM] * 3,
        scratch_shapes=[
            pltpu.VMEM((coords.shape[0] * 4 // 3, LANES), F32),
            pltpu.VMEM((LANES, count), F32),
            pltpu.VMEM((LANES, count), F32),
            pltpu.SemaphoreType.DMA((2,)),
        ],
        compiler_params=limit(10),
        name="transfer",
    )(*near_core(chosen), coords, *near_core(turned), *in_hbm(blocks, precond))


def times(matrices, vectors, put):
    rows = vectors[0].shape[0]

    def body(step, carry):
        for k in range(8):
            row = step * 8 + k
            total = None
            for matrix, vector in zip(matrices, vectors):
                term = matrix[row] * vector
                total = term if total is None else total + term
            put(row, jnp.sum(total, axis=0, keepdims=True))
        return carry

    lax.fori_loop(0, rows // 8, body, 0)


def precondition(precond_ref, listed_ref, vector, out_ref, send_ref):
    def put(row, value):
        out_ref[pl.ds(row, 1), :] = value

    times([precond_ref], [vector], put)
    send_ref[...] = pick_from(listed_ref[...], pad_rows(out_ref[...], LANES))


def start_kernel(
    mapped_ref, onehot_ref, precond_ref, listed_ref, load_ref, pre_ref, send_ref, wide
):
    unpack(mapped_ref, wide)
    load = pick(wide[...], onehot_ref[...], TN)[: load_ref.shape[0]]
    load_ref[...] = load
    precondition(precond_ref, listed_ref, load, pre_ref, send_ref)


def start(mapped, onehot, precond, listed):
    shape = pltpu.VMEM((precond.shape[0], LANES), F32)
    return pl.pallas_call(
        start_kernel,
        out_shape=(shape, shape, pltpu.VMEM(listed.shape, F32)),
        in_specs=[VMEM] * 4,
        out_specs=[VMEM] * 3,
        scratch_shapes=[pltpu.VMEM(onehot.shape, F32)],
        compiler_params=limit(6),
        name="start",
    )(mapped, onehot, *near_core(precond, listed))


def inside_kernel(
    blocks_ref, local_ref, outer_ref, old_ref, pre_ref, near_ref, *refs
):
    earlier, (part_ref, taken_ref, *more) = refs[:-3], refs[-3:]
    pre = pre_ref[...]
    size = pre.shape[0]
    count = near_ref.shape[0]

    def put(row, value):
        part_ref[pl.ds(row, 1), :] = value - old_ref[pl.ds(row, 1), :]

    times([blocks_ref.at[0]], [pre], put)
    taken = pick(near_ref[...], outer_ref[:count, :], TN)[:size]
    taken_ref[...] = taken + pick(pre, local_ref[...], NN)
    if not earlier:
        more[0][...] = old_ref[...]
    else:
        vectors = [ref[...] for ref in earlier] + [old_ref[...]]
        sums = [jnp.sum(vectors[i] * vectors[j], axis=0, keepdims=True) for i, j in KNOWN]
        more[0][...] = pad_rows(jnp.concatenate(sums, axis=0), HELD)


def inside(blocks, local, outer, old, pre, near, earlier):
    size = old.shape[0]
    more = pltpu.VMEM((HELD, LANES), F32) if earlier else jax.ShapeDtypeStruct(old.shape, F32)
    return pl.pallas_call(
        inside_kernel,
        out_shape=(pltpu.VMEM(old.shape, F32), pltpu.VMEM((size, 2 * LANES), F32), more),
        in_specs=[VMEM] * (6 + len(earlier)),
        out_specs=[VMEM] * 3,
        compiler_params=limit(6),
        cost_estimate=pl.CostEstimate(flops=0, bytes_accessed=2 * MIB, transcendentals=0),
        name="inside",
    )(*near_core(blocks, local, outer, old, pre, near, *earlier))


def outside(blocks_ref, outer_ref, part_ref, taken_ref, far_ref, new_ref):
    size = part_ref.shape[0]
    count = far_ref.shape[0]
    taken = taken_ref[...] + pick(far_ref[...], outer_ref[count:, :], TN)[:size]
    vectors = [taken[:, :LANES], taken[:, LANES:]]

    def put(row, value):
        new_ref[pl.ds(row, 1), :] = value + part_ref[pl.ds(row, 1), :]

    times([blocks_ref.at[1], blocks_ref.at[2]], vectors, put)


def step_kernel(
    blocks_ref, precond_ref, outer_ref, listed_ref, part_ref, taken_ref, far_ref,
    new_ref, new_pre_ref, send_ref,
):
    outside(blocks_ref, outer_ref, part_ref, taken_ref, far_ref, new_ref)
    precondition(precond_ref, listed_ref, new_ref[...], new_pre_ref, send_ref)


def step(blocks, precond, outer, listed, part, taken, far):
    shape = pltpu.VMEM(part.shape, F32)
    return pl.pallas_call(
        step_kernel,
        out_shape=(shape, shape, pltpu.VMEM(far.shape, F32)),
        in_specs=[VMEM] * 7,
        out_specs=[VMEM] * 3,
        compiler_params=limit(6),
        name="step",
    )(*near_core(blocks, precond, outer, listed, part, taken, far))


def last_kernel(
    blocks_ref, outer_ref, part_ref, taken_ref, far_ref, known_ref, b0_ref, b1_ref, b2_ref, b3_ref,
    new_ref, sums_ref,
):
    outside(blocks_ref, outer_ref, part_ref, taken_ref, far_ref, new_ref)
    new = new_ref[...]
    vectors = [ref[...] for ref in (b0_ref, b1_ref, b2_ref, b3_ref)] + [new]
    sums = [known_ref[...]] + [jnp.sum(v * new, axis=0, keepdims=True) for v in vectors]
    ones = jnp.ones((sums_ref.shape[0], LANES), BF16)
    sums_ref[...] = pick_from(ones, pad_rows(jnp.concatenate(sums, axis=0), LANES))


def last(blocks, outer, part, taken, far, known, basis, parts):
    return pl.pallas_call(
        last_kernel,
        out_shape=(pltpu.VMEM(part.shape, F32), pltpu.VMEM((parts, LANES), F32)),
        in_specs=[VMEM] * 10,
        out_specs=[VMEM] * 2,
        compiler_params=limit(6),
        name="last",
    )(*near_core(blocks, outer, part, taken, far, known, *basis))


def plus(x, y):
    return [a + b for a, b in zip(x, y)]


def tree(terms):
    while len(terms) > 1:
        terms = [sum(terms[k : k + 2]) for k in range(0, len(terms), 2)]
    return terms[0]


def scaled(scale, x):
    return [scale * a for a in x]


def recurrences(product):
    def inner(x, y):
        return tree(
            [a * b * product[min(i, j), max(i, j)] for i, a in enumerate(x) for j, b in enumerate(y)]
        )

    def image_of(x):
        return plus([x[0] * 0.0] + x, x + [x[0] * 0.0])

    one = product[0, 0] * 0.0 + 1.0
    residual = search = shadow = [one]
    answer = []
    alignment = product[0, 0]

    def add(x, y):
        size = max(len(x), len(y))
        zero = one * 0.0
        return plus(x + [zero] * (size - len(x)), y + [zero] * (size - len(y)))

    for iteration in range(2):
        image = image_of(search)
        step_size = alignment / inner(shadow, image)
        middle = add(residual, scaled(-step_size, image))
        middle_image = image_of(middle)
        smoothing = inner(middle_image, middle) / inner(middle_image, middle_image)
        answer = add(answer, add(scaled(step_size, search), scaled(smoothing, middle)))
        residual = add(middle, scaled(-smoothing, middle_image))
        if iteration == 0:
            new_alignment = inner(shadow, residual)
            momentum = new_alignment / alignment * (step_size / smoothing)
            search = add(residual, scaled(momentum, add(search, scaled(-smoothing, image))))
            alignment = new_alignment
    return answer, residual


def finish_kernel(sums_ref, *refs):
    basis, pres, (solution_ref, residual_ref) = refs[:5], refs[5:9], refs[9:]
    totals = jnp.sum(sums_ref[...], axis=0, keepdims=True)
    lane = dict(zip(KNOWN, range(len(KNOWN))))
    lane.update({(i, STEPS): HELD + i for i in range(STEPS + 1)})
    product = {pair: totals[:, k : k + 1] for pair, k in lane.items()}
    answer, residual = recurrences(product)
    solution_ref[...] = sum(a * ref[...] for a, ref in zip(answer, pres))
    residual_ref[...] = sum(a * ref[...] for a, ref in zip(residual, basis))


def finish(sums, basis, pres):
    shape = jax.ShapeDtypeStruct(pres[0].shape, F32)
    return pl.pallas_call(
        finish_kernel,
        out_shape=(shape, shape),
        in_specs=[VMEM] * 10,
        compiler_params=limit(4),
        name="finish",
    )(*near_core(sums, *basis, *pres))


def to_near(send):
    devices = lax.axis_size(DOM)
    return lax.ppermute(send, DOM, [(i, i ^ 1) for i in range(devices)])


def to_far(send, closed):
    devices = lax.axis_size(DOM)
    pairs = [(i, (i + 1) % devices) for i in range(1, devices if closed else devices - 1, 2)]
    return lax.ppermute(send, DOM, pairs + [(j, i) for i, j in pairs])


def to_all(x):
    return lax.all_to_all(x, DOM, split_axis=0, concat_axis=0, tiled=True)


def on_device(
    traction, fluid_coords, struct_coords, dest, target, blocks, columns, halo_list, precond
):
    parts = lax.axis_size(DOM)
    place = lax.axis_index(DOM).astype(jnp.int32).reshape(1)
    force = jnp.transpose(traction, (1, 0, 2))
    fluid = jnp.transpose(fluid_coords, (1, 0, 2))
    coords = struct_coords.reshape(-1, struct_coords.shape[2])
    wanted, slot = slots(dest.reshape(1, -1), target.reshape(1, -1), parts)
    turned, chosen, coords, local, outer, listed = prepare(
        halo_list, place, columns, coords, slot, wanted, fluid, force
    )
    onehot, answered = answer(to_all(wanted), coords)
    answered = to_all(answered.reshape(parts, 1, -1)).reshape(answered.shape)
    mapped, blocks, precond = transfer(chosen, answered, turned, blocks, precond)
    mapped = to_all(mapped.reshape(parts, 1, -1)).reshape(mapped.shape)
    load, pre, send = start(mapped, onehot, precond, listed)
    basis, pres = [load], [pre]
    for j in range(STEPS):
        far = to_far(send, j > 0)
        near = to_near(send)
        earlier = basis[:-1] if j == STEPS - 1 else []
        part, taken, more = inside(blocks, local, outer, basis[-1], pres[-1], near, earlier)
        load_field = more if j == 0 else load_field
        if j < STEPS - 1:
            new, pre, send = step(blocks, precond, outer, listed, part, taken, far)
            pres.append(pre)
        else:
            new, sums = last(blocks, outer, part, taken, far, more, basis, parts)
        basis.append(new)
    solution, residual = finish(to_all(sums), basis, pres)
    return load_field, solution, residual


def solution(mesh):
    in_specs = (
        P(DOM, None, None),
        P(DOM, None, None),
        P(None, None, DOM),
        P(DOM, None),
        P(DOM),
        P(None, None, None, DOM),
        P(None, DOM),
        P(DOM),
        P(None, None, DOM),
    )
    out_specs = (P(None, DOM), P(None, DOM), P(None, DOM))
    return jax.shard_map(
        on_device, mesh=mesh, in_specs=in_specs, out_specs=out_specs, check_vma=False
    )
```

```python
import functools

import jax
import jax.numpy as jnp
from jax import lax
from jax.experimental import pallas as pl
from jax.experimental.pallas import tpu as pltpu
from jax.sharding import PartitionSpec as P

DOM = "dom"
SUPPORT = 0.9
CAP = 8
LANES = 128
STEPS = 4
KNOWN = [(i, j) for j in range(STEPS) for i in range(j + 1)]
HELD = 16
UNROLL = 24
F32 = jnp.float32
BF16 = jnp.bfloat16
NN = (((1,), (0,)), ((), ()))
NT = (((1,), (1,)), ((), ()))
TN = (((0,), (0,)), ((), ()))


SMEM = pl.BlockSpec(memory_space=pltpu.SMEM)
VMEM = pl.BlockSpec(memory_space=pltpu.VMEM)
ANY = pl.BlockSpec(memory_space=pl.ANY)
MIB = 1 << 20


def limit(mib):
    return pltpu.CompilerParams(vmem_limit_bytes=mib * MIB)


def near_core(*arrays):
    return [pltpu.with_memory_space_constraint(x, pltpu.VMEM) for x in arrays]


def in_hbm(*arrays):
    return [pltpu.with_memory_space_constraint(x, pltpu.HBM) for x in arrays]


def iota(shape, dim):
    return lax.broadcasted_iota(jnp.int32, shape, dim)


def flag(mask):
    return jnp.where(mask, 1.0, 0.0).astype(BF16)


def split3(x):
    high = x.astype(BF16)
    rest = x - high.astype(F32)
    mid = rest.astype(BF16)
    low = (rest - mid.astype(F32)).astype(BF16)
    return high, mid, low


def dot(a, b, dims):
    return lax.dot_general(a, b, dims, preferred_element_type=F32)


def three(product, size, axis):
    parts = [lax.slice_in_dim(product, k * size, (k + 1) * size, axis=axis) for k in range(3)]
    return parts[0] + (parts[1] + parts[2])


def pick(x, onehot, dims):
    free = 0 if dims == NN else 1
    stacked = jnp.concatenate(split3(x), axis=free)
    return three(dot(stacked, onehot, dims), x.shape[free], 0)


def pick_from(onehot, x):
    return three(dot(onehot, jnp.concatenate(split3(x), axis=0), NT), x.shape[0], 1)


def pad_rows(x, rows):
    if x.shape[0] == rows:
        return x
    return jnp.concatenate([x, jnp.zeros((rows - x.shape[0], x.shape[1]), x.dtype)], axis=0)


def pack(wide_ref, out_ref):
    parts = wide_ref.shape[0] // CAP
    free = iota((parts, LANES), 1) >= 96
    spare = [wide_ref[pl.ds(6 + k, parts, CAP), :] for k in range(2)]
    for r in range(6):
        own = wide_ref[pl.ds(r, parts, CAP), :]
        extra = pltpu.roll(spare[r // 3], 96 - 32 * (r % 3), axis=1)
        out_ref[pl.ds(r, parts, 6), :] = jnp.where(free, extra, own)


def unpack(packed_ref, wide_ref):
    parts = wide_ref.shape[0] // CAP
    lane = iota((parts, LANES), 1)
    rows = [packed_ref[pl.ds(r, parts, 6), :] for r in range(6)]
    for r in range(6):
        wide_ref[pl.ds(r, parts, CAP), :] = rows[r]
    for k in range(2):
        first, second, third = [pltpu.roll(rows[3 * k + c], 32 * c + 32, axis=1) for c in range(3)]
        value = jnp.where(lane < 32, first, jnp.where(lane < 64, second, third))
        wide_ref[pl.ds(6 + k, parts, CAP), :] = value


def slots_kernel(dest_ref, target_ref, labels_ref, slot_ref):
    dest = dest_ref[...]
    count = dest.shape[1]
    parts = labels_ref.shape[0]
    hits = flag(iota((parts, count), 0) == dest)
    earlier = flag(iota((LANES, LANES), 0) < iota((LANES, LANES), 1))
    passed = jnp.zeros((parts, LANES), F32)
    before = []
    for chunk in range(count // LANES):
        own = hits[:, chunk * LANES : (chunk + 1) * LANES]
        running = dot(own, earlier, NN) + passed
        before.append(jnp.sum(running * own.astype(F32), axis=0, keepdims=True))
        passed = passed + dot(own, jnp.ones((LANES, LANES), BF16), NN)
    before = jnp.concatenate(before, axis=1)
    slot_ref[...] = dest * CAP + before.astype(jnp.int32)
    place = iota((LANES, count), 0).astype(F32)
    wanted = jnp.where(place == before, (target_ref[...] + 1).astype(F32), 0.0)
    labels_ref[...] = dot(hits, wanted.astype(BF16), NT)


def slots(dest, target, parts):
    count = dest.shape[1]
    return pl.pallas_call(
        slots_kernel,
        out_shape=(
            jax.ShapeDtypeStruct((parts, LANES), F32),
            jax.ShapeDtypeStruct((1, count), jnp.int32),
        ),
        compiler_params=limit(2),
        name="slots",
    )(*in_hbm(dest, target))


def prepare_kernel(
    parts, halo_ref, place_ref, columns_ref, coords_ref, after_ref, fluid_ref, force_ref,
    turned_ref, coords_out, local_ref, outer_ref, listed_ref,
    points, sems,
):
    copies = [
        pltpu.make_async_copy(ref, points.at[k], sems.at[k])
        for k, ref in enumerate((fluid_ref, force_ref))
    ]
    for copy in copies:
        copy.start()
    coords_out[...] = pad_rows(coords_ref[...], LANES)
    halo = listed_ref.shape[0]
    core = place_ref[0] % 2
    at_end = jnp.logical_or(place_ref[0] == 0, place_ref[0] == parts - 1)
    held = jnp.where(at_end, halo, 2 * halo)
    for neighbor in range(2):
        column = columns_ref[pl.ds(neighbor, 1), :]
        local_ref[neighbor] = flag(iota((LANES, LANES), 0) == column)
        outer = (column - LANES) ^ ((1 - core) * halo)
        outer = jnp.where(outer < held, outer, -1)
        outer_ref[neighbor] = flag(iota(outer_ref.shape[1:], 0) == outer)
    rows = iota(listed_ref.shape, 0)
    column = jnp.zeros(listed_ref.shape, jnp.int32)
    for h in range(listed_ref.shape[0]):
        column = jnp.where(rows == h, halo_ref[h], column)
    listed_ref[...] = flag(column == iota(listed_ref.shape, 1))
    for copy in copies:
        copy.wait()
    for group in range(points.shape[2] // LANES):
        lanes = pl.ds(group * LANES, LANES)
        length = jnp.zeros(turned_ref.shape[2:], F32)
        for c in range(3):
            position = points[0, c, lanes, :].T * (1.0 / SUPPORT)
            length = length + position * position
            turned_ref[group, c] = position * -2.0
            turned_ref[group, 3 + c] = points[1, c, lanes, :].T * 4.0
        turned_ref[group, 6] = length


def prepare(halo_list, place, columns, coords, after, fluid, force):
    count, nodes = fluid.shape[1:]
    halo = halo_list.shape[0]
    return pl.pallas_call(
        functools.partial(prepare_kernel, after.shape[0]),
        out_shape=(
            pltpu.VMEM((count // LANES, 7, nodes, LANES), F32),
            pltpu.VMEM((LANES, LANES), F32),
            pltpu.VMEM((2, LANES, LANES), BF16),
            pltpu.VMEM((2, 2 * halo, LANES), BF16),
            pltpu.VMEM((halo, LANES), BF16),
        ),
        in_specs=[SMEM, SMEM, VMEM, VMEM] + [ANY] * 3,
        out_specs=[VMEM] * 5,
        scratch_shapes=[pltpu.VMEM((2, 3, count, nodes), F32), pltpu.SemaphoreType.DMA((2,))],
        compiler_params=limit(4),
        cost_estimate=pl.CostEstimate(flops=0, bytes_accessed=3 * MIB, transcendentals=0),
        name="prepare",
    )(*in_hbm(halo_list, place, columns, coords, after, fluid, force))


def answer_kernel(labels_ref, coords_ref, onehot_ref, out_ref, wide):
    rows = onehot_ref.shape[0]
    parts = labels_ref.shape[0]
    repeat = flag(iota((rows, parts), 0) // CAP == iota((rows, parts), 1))
    spread = dot(repeat, labels_ref[...].astype(BF16), NN)
    own = iota((rows, LANES), 0) % CAP == iota((rows, LANES), 1)
    own_label = jnp.where(own, spread, 0.0).astype(BF16)
    label = dot(own_label, jnp.ones((LANES, LANES), BF16), NN)
    onehot = flag(label == (iota((rows, LANES), 1) + 1).astype(F32))
    onehot_ref[...] = onehot
    wide[...] = pick_from(onehot, coords_ref[...])
    pack(wide, out_ref)


def answer(labels, coords):
    rows = labels.shape[0] * CAP
    return pl.pallas_call(
        answer_kernel,
        out_shape=(
            jax.ShapeDtypeStruct((rows, LANES), BF16),
            jax.ShapeDtypeStruct((rows * 3 // 4, LANES), F32),
        ),
        in_specs=[VMEM, VMEM],
        scratch_shapes=[pltpu.VMEM((rows, LANES), F32)],
        compiler_params=limit(6),
        name="answer",
    )(labels, *near_core(coords))


def transfer_kernel(
    slot_ref, coords_ref, turned_ref, blocks_ref, precond_ref, out_ref, blocks_out, precond_out,
    wide, struct, mapped, sems,
):
    tables = [
        pltpu.make_async_copy(precond_ref, precond_out, sems.at[0]),
        pltpu.make_async_copy(blocks_ref, blocks_out, sems.at[1]),
    ]
    for copy in tables:
        copy.start()
    rows = wide.shape[0]
    count = slot_ref.shape[1]
    unpack(coords_ref, wide)
    chosen = flag(iota((rows, count), 0) == slot_ref[...])
    struct[...] = pick(wide[...], chosen, TN) * (1.0 / SUPPORT)
    nodes = turned_ref.shape[2]
    for group in range(count // LANES):
        lanes = pl.ds(group * LANES, LANES)
        where = [struct[pl.ds(c * 32, 32), lanes] for c in range(3)]
        length = where[0] * where[0] + where[1] * where[1] + where[2] * where[2]

        def body(step, sums):
            sums = list(sums)
            for k in range(8):
                n = pl.ds(step * 8 + k, 1)
                square = length + turned_ref[group, 6, n, :]
                for c in range(3):
                    square = square + where[c] * turned_ref[group, c, n, :]
                square = jnp.maximum(square, 1e-30)
                left = jnp.maximum(1.0 - square * lax.rsqrt(square), 0.0)
                twice = left * left
                quarter = twice * twice * (1.25 - left)
                for c in range(3):
                    sums[c] = sums[c] + quarter * turned_ref[group, 3 + c, n, :]
            return tuple(sums)

        zero = jnp.zeros((32, LANES), F32)
        sums = lax.fori_loop(0, nodes // 8, body, (zero, zero, zero))
        for c in range(3):
            mapped[pl.ds(c * 32, 32), lanes] = sums[c]
    mapped[pl.ds(96, 32), :] = jnp.zeros((32, count), F32)
    wide[...] = pick_from(chosen, mapped[...])
    pack(wide, out_ref)
    for copy in tables:
        copy.wait()


def transfer(slot, coords, turned, blocks, precond):
    count = slot.shape[1]
    return pl.pallas_call(
        transfer_kernel,
        out_shape=(
            jax.ShapeDtypeStruct(coords.shape, F32),
            pltpu.VMEM(blocks.shape, F32),
            pltpu.VMEM(precond.shape, F32),
        ),
        in_specs=[VMEM] * 3 + [ANY] * 2,
        out_specs=[VMEM] * 3,
        scratch_shapes=[
            pltpu.VMEM((coords.shape[0] * 4 // 3, LANES), F32),
            pltpu.VMEM((LANES, count), F32),
            pltpu.VMEM((LANES, count), F32),
            pltpu.SemaphoreType.DMA((2,)),
        ],
        compiler_params=limit(10),
        name="transfer",
    )(slot, coords, *near_core(turned), *in_hbm(blocks, precond))


def times(matrices, vectors, put):
    rows = vectors[0].shape[0]

    def body(step, carry):
        for k in range(UNROLL):
            row = step * UNROLL + k
            total = None
            for matrix, vector in zip(matrices, vectors):
                term = matrix[row] * vector
                total = term if total is None else total + term
            put(row, jnp.sum(total, axis=0, keepdims=True))
        return carry

    lax.fori_loop(0, rows // UNROLL, body, 0)


def precondition(precond_ref, listed_ref, vector, out_ref, send_ref):
    def put(row, value):
        out_ref[pl.ds(row, 1), :] = value

    times([precond_ref], [vector], put)
    send_ref[...] = pick_from(listed_ref[...], pad_rows(out_ref[...], LANES))


def start_kernel(
    mapped_ref, onehot_ref, precond_ref, listed_ref, load_ref, pre_ref, send_ref, wide
):
    unpack(mapped_ref, wide)
    load = pick(wide[...], onehot_ref[...], TN)[: load_ref.shape[0]]
    load_ref[...] = load
    precondition(precond_ref, listed_ref, load, pre_ref, send_ref)


def start(mapped, onehot, precond, listed):
    shape = pltpu.VMEM((precond.shape[0], LANES), F32)
    return pl.pallas_call(
        start_kernel,
        out_shape=(shape, shape, pltpu.VMEM(listed.shape, F32)),
        in_specs=[VMEM] * 4,
        out_specs=[VMEM] * 3,
        scratch_shapes=[pltpu.VMEM(onehot.shape, F32)],
        compiler_params=limit(6),
        name="start",
    )(mapped, onehot, *near_core(precond, listed))


def inside_kernel(
    blocks_ref, local_ref, outer_ref, old_ref, pre_ref, near_ref, *refs
):
    earlier, (part_ref, taken_ref, *more) = refs[:-3], refs[-3:]
    pre = pre_ref[...]
    size = pre.shape[0]
    count = near_ref.shape[0]

    def put(row, value):
        part_ref[pl.ds(row, 1), :] = value - old_ref[pl.ds(row, 1), :]

    times([blocks_ref.at[0]], [pre], put)
    for neighbor in range(2):
        taken = pick(pre, local_ref[neighbor], NN)
        taken_ref[neighbor] = taken + pick(near_ref[...], outer_ref[neighbor, :count, :], TN)[:size]
    if not earlier:
        more[0][...] = old_ref[...]
    else:
        vectors = [ref[...] for ref in earlier] + [old_ref[...]]
        sums = [jnp.sum(vectors[i] * vectors[j], axis=0, keepdims=True) for i, j in KNOWN]
        more[0][...] = pad_rows(jnp.concatenate(sums, axis=0), HELD)


def inside(blocks, local, outer, old, pre, near, earlier):
    size = old.shape[0]
    more = pltpu.VMEM((HELD, LANES), F32) if earlier else jax.ShapeDtypeStruct(old.shape, F32)
    return pl.pallas_call(
        inside_kernel,
        out_shape=(pltpu.VMEM(old.shape, F32), pltpu.VMEM((2, size, LANES), F32), more),
        in_specs=[VMEM] * (6 + len(earlier)),
        out_specs=[VMEM] * 3,
        compiler_params=limit(6),
        cost_estimate=pl.CostEstimate(flops=0, bytes_accessed=2 * MIB, transcendentals=0),
        name="inside",
    )(*near_core(blocks, local, outer, old, pre, near, *earlier))


def outside(blocks_ref, outer_ref, part_ref, taken_ref, far_ref, new_ref):
    size = part_ref.shape[0]
    count = far_ref.shape[0]
    vectors = [
        taken_ref[neighbor] + pick(far_ref[...], outer_ref[neighbor, count:, :], TN)[:size]
        for neighbor in range(2)
    ]

    def put(row, value):
        new_ref[pl.ds(row, 1), :] = value + part_ref[pl.ds(row, 1), :]

    times([blocks_ref.at[1], blocks_ref.at[2]], vectors, put)


def step_kernel(
    blocks_ref, precond_ref, outer_ref, listed_ref, part_ref, taken_ref, far_ref,
    new_ref, new_pre_ref, send_ref,
):
    outside(blocks_ref, outer_ref, part_ref, taken_ref, far_ref, new_ref)
    precondition(precond_ref, listed_ref, new_ref[...], new_pre_ref, send_ref)


def step(blocks, precond, outer, listed, part, taken, far):
    shape = pltpu.VMEM(part.shape, F32)
    return pl.pallas_call(
        step_kernel,
        out_shape=(shape, shape, pltpu.VMEM(far.shape, F32)),
        in_specs=[VMEM] * 7,
        out_specs=[VMEM] * 3,
        compiler_params=limit(6),
        name="step",
    )(*near_core(blocks, precond, outer, listed, part, taken, far))


def last_kernel(
    blocks_ref, outer_ref, part_ref, taken_ref, far_ref, known_ref, b0_ref, b1_ref, b2_ref, b3_ref,
    new_ref, sums_ref,
):
    outside(blocks_ref, outer_ref, part_ref, taken_ref, far_ref, new_ref)
    new = new_ref[...]
    vectors = [ref[...] for ref in (b0_ref, b1_ref, b2_ref, b3_ref)] + [new]
    sums = [known_ref[...]] + [jnp.sum(v * new, axis=0, keepdims=True) for v in vectors]
    ones = jnp.ones((sums_ref.shape[0], LANES), BF16)
    sums_ref[...] = pick_from(ones, pad_rows(jnp.concatenate(sums, axis=0), LANES))


def last(blocks, outer, part, taken, far, known, basis, parts):
    return pl.pallas_call(
        last_kernel,
        out_shape=(pltpu.VMEM(part.shape, F32), pltpu.VMEM((parts, LANES), F32)),
        in_specs=[VMEM] * 10,
        out_specs=[VMEM] * 2,
        compiler_params=limit(6),
        name="last",
    )(*near_core(blocks, outer, part, taken, far, known, *basis))


def plus(x, y):
    return [a + b for a, b in zip(x, y)]


def tree(terms):
    while len(terms) > 1:
        terms = [sum(terms[k : k + 2]) for k in range(0, len(terms), 2)]
    return terms[0]


def scaled(scale, x):
    return [scale * a for a in x]


def recurrences(product):
    def inner(x, y):
        return tree(
            [a * b * product[min(i, j), max(i, j)] for i, a in enumerate(x) for j, b in enumerate(y)]
        )

    def image_of(x):
        return plus([x[0] * 0.0] + x, x + [x[0] * 0.0])

    one = product[0, 0] * 0.0 + 1.0
    residual = search = shadow = [one]
    answer = []
    alignment = product[0, 0]

    def add(x, y):
        size = max(len(x), len(y))
        zero = one * 0.0
        return plus(x + [zero] * (size - len(x)), y + [zero] * (size - len(y)))

    for iteration in range(2):
        image = image_of(search)
        step_size = alignment / inner(shadow, image)
        middle = add(residual, scaled(-step_size, image))
        middle_image = image_of(middle)
        smoothing = inner(middle_image, middle) / inner(middle_image, middle_image)
        answer = add(answer, add(scaled(step_size, search), scaled(smoothing, middle)))
        residual = add(middle, scaled(-smoothing, middle_image))
        if iteration == 0:
            new_alignment = inner(shadow, residual)
            momentum = new_alignment / alignment * (step_size / smoothing)
            search = add(residual, scaled(momentum, add(search, scaled(-smoothing, image))))
            alignment = new_alignment
    return answer, residual


def finish_kernel(sums_ref, *refs):
    basis, pres, (solution_ref, residual_ref) = refs[:5], refs[5:9], refs[9:]
    totals = jnp.sum(sums_ref[...], axis=0, keepdims=True)
    lane = dict(zip(KNOWN, range(len(KNOWN))))
    lane.update({(i, STEPS): HELD + i for i in range(STEPS + 1)})
    product = {pair: totals[:, k : k + 1] for pair, k in lane.items()}
    answer, residual = recurrences(product)
    solution_ref[...] = sum(a * ref[...] for a, ref in zip(answer, pres))
    residual_ref[...] = sum(a * ref[...] for a, ref in zip(residual, basis))


def finish(sums, basis, pres):
    shape = jax.ShapeDtypeStruct(pres[0].shape, F32)
    return pl.pallas_call(
        finish_kernel,
        out_shape=(shape, shape),
        in_specs=[VMEM] * 10,
        compiler_params=limit(4),
        name="finish",
    )(*near_core(sums, *basis, *pres))


def to_near(send):
    devices = lax.axis_size(DOM)
    return lax.ppermute(send, DOM, [(i, i ^ 1) for i in range(devices)])


def to_far(send, closed):
    devices = lax.axis_size(DOM)
    pairs = [(i, (i + 1) % devices) for i in range(1, devices if closed else devices - 1, 2)]
    return lax.ppermute(send, DOM, pairs + [(j, i) for i, j in pairs])


def to_all(x):
    return lax.all_to_all(x, DOM, split_axis=0, concat_axis=0, tiled=True)


def on_device(
    traction, fluid_coords, struct_coords, dest, target, blocks, columns, halo_list, precond
):
    parts = lax.axis_size(DOM)
    place = lax.axis_index(DOM).astype(jnp.int32).reshape(1)
    force = jnp.transpose(traction, (1, 0, 2))
    fluid = jnp.transpose(fluid_coords, (1, 0, 2))
    coords = struct_coords.reshape(-1, struct_coords.shape[2])
    wanted, slot = slots(dest.reshape(1, -1), target.reshape(1, -1), parts)
    turned, coords, local, outer, listed = prepare(
        halo_list, place, columns, coords, wanted, fluid, force
    )
    onehot, answered = answer(to_all(wanted), coords)
    answered = to_all(answered.reshape(parts, 1, -1)).reshape(answered.shape)
    mapped, blocks, precond = transfer(slot, answered, turned, blocks, precond)
    mapped = to_all(mapped.reshape(parts, 1, -1)).reshape(mapped.shape)
    load, pre, send = start(mapped, onehot, precond, listed)
    basis, pres = [load], [pre]
    for j in range(STEPS):
        far = to_far(send, j > 0)
        near = to_near(send)
        earlier = basis[:-1] if j == STEPS - 1 else []
        part, taken, more = inside(blocks, local, outer, basis[-1], pres[-1], near, earlier)
        load_field = more if j == 0 else load_field
        if j < STEPS - 1:
            new, pre, send = step(blocks, precond, outer, listed, part, taken, far)
            pres.append(pre)
        else:
            new, sums = last(blocks, outer, part, taken, far, more, basis, parts)
        basis.append(new)
    solution, residual = finish(to_all(sums), basis, pres)
    return load_field, solution, residual


def solution(mesh):
    in_specs = (
        P(DOM, None, None),
        P(DOM, None, None),
        P(None, None, DOM),
        P(DOM, None),
        P(DOM),
        P(None, None, None, DOM),
        P(None, DOM),
        P(DOM),
        P(None, None, DOM),
    )
    out_specs = (P(None, DOM), P(None, DOM), P(None, DOM))
    return jax.shard_map(
        on_device, mesh=mesh, in_specs=in_specs, out_specs=out_specs, check_vma=False
    )
```

```python
import functools

import jax
import jax.numpy as jnp
from jax import lax
from jax.experimental import pallas as pl
from jax.experimental.pallas import tpu as pltpu
from jax.sharding import PartitionSpec as P

DOM = "dom"
SUPPORT = 0.9
CAP = 8
LANES = 128
STEPS = 4
KNOWN = [(i, j) for j in range(STEPS) for i in range(j + 1)]
HELD = 16
UNROLL = 48
F32 = jnp.float32
BF16 = jnp.bfloat16
NN = (((1,), (0,)), ((), ()))
NT = (((1,), (1,)), ((), ()))
TN = (((0,), (0,)), ((), ()))


SMEM = pl.BlockSpec(memory_space=pltpu.SMEM)
VMEM = pl.BlockSpec(memory_space=pltpu.VMEM)
ANY = pl.BlockSpec(memory_space=pl.ANY)
MIB = 1 << 20


def limit(mib):
    return pltpu.CompilerParams(vmem_limit_bytes=mib * MIB)


def near_core(*arrays):
    return [pltpu.with_memory_space_constraint(x, pltpu.VMEM) for x in arrays]


def in_hbm(*arrays):
    return [pltpu.with_memory_space_constraint(x, pltpu.HBM) for x in arrays]


def iota(shape, dim):
    return lax.broadcasted_iota(jnp.int32, shape, dim)


def flag(mask):
    return jnp.where(mask, 1.0, 0.0).astype(BF16)


def split3(x):
    high = x.astype(BF16)
    rest = x - high.astype(F32)
    mid = rest.astype(BF16)
    low = (rest - mid.astype(F32)).astype(BF16)
    return high, mid, low


def dot(a, b, dims):
    return lax.dot_general(a, b, dims, preferred_element_type=F32)


def three(product, size, axis):
    parts = [lax.slice_in_dim(product, k * size, (k + 1) * size, axis=axis) for k in range(3)]
    return parts[0] + (parts[1] + parts[2])


def pick(x, onehot, dims):
    free = 0 if dims == NN else 1
    stacked = jnp.concatenate(split3(x), axis=free)
    return three(dot(stacked, onehot, dims), x.shape[free], 0)


def pick_from(onehot, x):
    return three(dot(onehot, jnp.concatenate(split3(x), axis=0), NT), x.shape[0], 1)


def pad_rows(x, rows):
    if x.shape[0] == rows:
        return x
    return jnp.concatenate([x, jnp.zeros((rows - x.shape[0], x.shape[1]), x.dtype)], axis=0)


def pack(wide_ref, out_ref):
    parts = wide_ref.shape[0] // CAP
    free = iota((parts, LANES), 1) >= 96
    spare = [wide_ref[pl.ds(6 + k, parts, CAP), :] for k in range(2)]
    for r in range(6):
        own = wide_ref[pl.ds(r, parts, CAP), :]
        extra = pltpu.roll(spare[r // 3], 96 - 32 * (r % 3), axis=1)
        out_ref[pl.ds(r, parts, 6), :] = jnp.where(free, extra, own)


def unpack(packed_ref, wide_ref):
    parts = wide_ref.shape[0] // CAP
    lane = iota((parts, LANES), 1)
    rows = [packed_ref[pl.ds(r, parts, 6), :] for r in range(6)]
    for r in range(6):
        wide_ref[pl.ds(r, parts, CAP), :] = rows[r]
    for k in range(2):
        first, second, third = [pltpu.roll(rows[3 * k + c], 32 * c + 32, axis=1) for c in range(3)]
        value = jnp.where(lane < 32, first, jnp.where(lane < 64, second, third))
        wide_ref[pl.ds(6 + k, parts, CAP), :] = value


def slots_kernel(dest_ref, target_ref, labels_ref, slot_ref):
    dest = dest_ref[...]
    count = dest.shape[1]
    parts = labels_ref.shape[0]
    hits = flag(iota((parts, count), 0) == dest)
    earlier = flag(iota((LANES, LANES), 0) < iota((LANES, LANES), 1))
    passed = jnp.zeros((parts, LANES), F32)
    before = []
    for chunk in range(count // LANES):
        own = hits[:, chunk * LANES : (chunk + 1) * LANES]
        running = dot(own, earlier, NN) + passed
        before.append(jnp.sum(running * own.astype(F32), axis=0, keepdims=True))
        passed = passed + dot(own, jnp.ones((LANES, LANES), BF16), NN)
    before = jnp.concatenate(before, axis=1)
    slot_ref[...] = dest * CAP + before.astype(jnp.int32)
    place = iota((LANES, count), 0).astype(F32)
    wanted = jnp.where(place == before, (target_ref[...] + 1).astype(F32), 0.0)
    labels_ref[...] = dot(hits, wanted.astype(BF16), NT)


def slots(dest, target, parts):
    count = dest.shape[1]
    return pl.pallas_call(
        slots_kernel,
        out_shape=(
            jax.ShapeDtypeStruct((parts, LANES), F32),
            jax.ShapeDtypeStruct((1, count), jnp.int32),
        ),
        compiler_params=limit(2),
        name="slots",
    )(*in_hbm(dest, target))


def prepare_kernel(
    parts, halo_ref, place_ref, columns_ref, coords_ref, after_ref, fluid_ref, force_ref,
    turned_ref, coords_out, local_ref, outer_ref, listed_ref,
    points, sems,
):
    copies = [
        pltpu.make_async_copy(ref, points.at[k], sems.at[k])
        for k, ref in enumerate((fluid_ref, force_ref))
    ]
    for copy in copies:
        copy.start()
    coords_out[...] = pad_rows(coords_ref[...], LANES)
    halo = listed_ref.shape[0]
    core = place_ref[0] % 2
    at_end = jnp.logical_or(place_ref[0] == 0, place_ref[0] == parts - 1)
    held = jnp.where(at_end, halo, 2 * halo)
    for neighbor in range(2):
        column = columns_ref[pl.ds(neighbor, 1), :]
        local_ref[neighbor] = flag(iota((LANES, LANES), 0) == column)
        outer = (column - LANES) ^ ((1 - core) * halo)
        outer = jnp.where(outer < held, outer, -1)
        outer_ref[neighbor] = flag(iota(outer_ref.shape[1:], 0) == outer)
    rows = iota(listed_ref.shape, 0)
    column = jnp.zeros(listed_ref.shape, jnp.int32)
    for h in range(listed_ref.shape[0]):
        column = jnp.where(rows == h, halo_ref[h], column)
    listed_ref[...] = flag(column == iota(listed_ref.shape, 1))
    for copy in copies:
        copy.wait()
    for group in range(points.shape[2] // LANES):
        lanes = pl.ds(group * LANES, LANES)
        length = jnp.zeros(turned_ref.shape[2:], F32)
        for c in range(3):
            position = points[0, c, lanes, :].T * (1.0 / SUPPORT)
            length = length + position * position
            turned_ref[group, c] = position * -2.0
            turned_ref[group, 3 + c] = points[1, c, lanes, :].T * 4.0
        turned_ref[group, 6] = length


def prepare(halo_list, place, columns, coords, after, fluid, force):
    count, nodes = fluid.shape[1:]
    halo = halo_list.shape[0]
    return pl.pallas_call(
        functools.partial(prepare_kernel, after.shape[0]),
        out_shape=(
            pltpu.VMEM((count // LANES, 7, nodes, LANES), F32),
            pltpu.VMEM((LANES, LANES), F32),
            pltpu.VMEM((2, LANES, LANES), BF16),
            pltpu.VMEM((2, 2 * halo, LANES), BF16),
            pltpu.VMEM((halo, LANES), BF16),
        ),
        in_specs=[SMEM, SMEM, VMEM, VMEM] + [ANY] * 3,
        out_specs=[VMEM] * 5,
        scratch_shapes=[pltpu.VMEM((2, 3, count, nodes), F32), pltpu.SemaphoreType.DMA((2,))],
        compiler_params=limit(4),
        cost_estimate=pl.CostEstimate(flops=0, bytes_accessed=3 * MIB, transcendentals=0),
        name="prepare",
    )(*in_hbm(halo_list, place, columns, coords, after, fluid, force))


def answer_kernel(labels_ref, coords_ref, onehot_ref, out_ref, wide):
    rows = onehot_ref.shape[0]
    parts = labels_ref.shape[0]
    repeat = flag(iota((rows, parts), 0) // CAP == iota((rows, parts), 1))
    spread = dot(repeat, labels_ref[...].astype(BF16), NN)
    own = iota((rows, LANES), 0) % CAP == iota((rows, LANES), 1)
    own_label = jnp.where(own, spread, 0.0).astype(BF16)
    label = dot(own_label, jnp.ones((LANES, LANES), BF16), NN)
    onehot = flag(label == (iota((rows, LANES), 1) + 1).astype(F32))
    onehot_ref[...] = onehot
    wide[...] = pick_from(onehot, coords_ref[...])
    pack(wide, out_ref)


def answer(labels, coords):
    rows = labels.shape[0] * CAP
    return pl.pallas_call(
        answer_kernel,
        out_shape=(
            jax.ShapeDtypeStruct((rows, LANES), BF16),
            jax.ShapeDtypeStruct((rows * 3 // 4, LANES), F32),
        ),
        in_specs=[VMEM, VMEM],
        scratch_shapes=[pltpu.VMEM((rows, LANES), F32)],
        compiler_params=limit(6),
        name="answer",
    )(labels, *near_core(coords))


def transfer_kernel(
    slot_ref, coords_ref, turned_ref, blocks_ref, precond_ref, out_ref, blocks_out, precond_out,
    wide, struct, mapped, sems,
):
    tables = [
        pltpu.make_async_copy(precond_ref, precond_out, sems.at[0]),
        pltpu.make_async_copy(blocks_ref, blocks_out, sems.at[1]),
    ]
    for copy in tables:
        copy.start()
    rows = wide.shape[0]
    count = slot_ref.shape[1]
    unpack(coords_ref, wide)
    chosen = flag(iota((rows, count), 0) == slot_ref[...])
    struct[...] = pick(wide[...], chosen, TN) * (1.0 / SUPPORT)
    nodes = turned_ref.shape[2]
    for group in range(count // LANES):
        lanes = pl.ds(group * LANES, LANES)
        where = [struct[pl.ds(c * 32, 32), lanes] for c in range(3)]
        length = where[0] * where[0] + where[1] * where[1] + where[2] * where[2]

        def body(step, sums):
            sums = list(sums)
            for k in range(8):
                n = pl.ds(step * 8 + k, 1)
                square = length + turned_ref[group, 6, n, :]
                for c in range(3):
                    square = square + where[c] * turned_ref[group, c, n, :]
                square = jnp.maximum(square, 1e-30)
                left = jnp.maximum(1.0 - square * lax.rsqrt(square), 0.0)
                twice = left * left
                quarter = twice * twice * (1.25 - left)
                for c in range(3):
                    sums[c] = sums[c] + quarter * turned_ref[group, 3 + c, n, :]
            return tuple(sums)

        zero = jnp.zeros((32, LANES), F32)
        sums = lax.fori_loop(0, nodes // 8, body, (zero, zero, zero))
        for c in range(3):
            mapped[pl.ds(c * 32, 32), lanes] = sums[c]
    mapped[pl.ds(96, 32), :] = jnp.zeros((32, count), F32)
    wide[...] = pick_from(chosen, mapped[...])
    pack(wide, out_ref)
    for copy in tables:
        copy.wait()


def transfer(slot, coords, turned, blocks, precond):
    count = slot.shape[1]
    return pl.pallas_call(
        transfer_kernel,
        out_shape=(
            jax.ShapeDtypeStruct(coords.shape, F32),
            pltpu.VMEM(blocks.shape, F32),
            pltpu.VMEM(precond.shape, F32),
        ),
        in_specs=[VMEM] * 3 + [ANY] * 2,
        out_specs=[VMEM] * 3,
        scratch_shapes=[
            pltpu.VMEM((coords.shape[0] * 4 // 3, LANES), F32),
            pltpu.VMEM((LANES, count), F32),
            pltpu.VMEM((LANES, count), F32),
            pltpu.SemaphoreType.DMA((2,)),
        ],
        compiler_params=limit(10),
        name="transfer",
    )(slot, coords, *near_core(turned), *in_hbm(blocks, precond))


def times(matrices, vectors, put):
    rows = vectors[0].shape[0]

    def body(step, carry):
        for k in range(UNROLL):
            row = step * UNROLL + k
            total = None
            for matrix, vector in zip(matrices, vectors):
                term = matrix[row] * vector
                total = term if total is None else total + term
            put(row, jnp.sum(total, axis=0, keepdims=True))
        return carry

    lax.fori_loop(0, rows // UNROLL, body, 0)


def precondition(precond_ref, listed_ref, vector, out_ref, send_ref):
    def put(row, value):
        out_ref[pl.ds(row, 1), :] = value

    times([precond_ref], [vector], put)
    send_ref[...] = pick_from(listed_ref[...], pad_rows(out_ref[...], LANES))


def start_kernel(
    mapped_ref, onehot_ref, precond_ref, listed_ref, load_ref, pre_ref, send_ref, wide
):
    unpack(mapped_ref, wide)
    load = pick(wide[...], onehot_ref[...], TN)[: load_ref.shape[0]]
    load_ref[...] = load
    precondition(precond_ref, listed_ref, load, pre_ref, send_ref)


def start(mapped, onehot, precond, listed):
    shape = pltpu.VMEM((precond.shape[0], LANES), F32)
    return pl.pallas_call(
        start_kernel,
        out_shape=(shape, shape, pltpu.VMEM(listed.shape, F32)),
        in_specs=[VMEM] * 4,
        out_specs=[VMEM] * 3,
        scratch_shapes=[pltpu.VMEM(onehot.shape, F32)],
        compiler_params=limit(6),
        name="start",
    )(mapped, onehot, *near_core(precond, listed))


def inside_kernel(
    blocks_ref, local_ref, outer_ref, old_ref, pre_ref, near_ref, *refs
):
    earlier, (part_ref, taken_ref, *more) = refs[:-3], refs[-3:]
    pre = pre_ref[...]
    size = pre.shape[0]
    count = near_ref.shape[0]

    def put(row, value):
        part_ref[pl.ds(row, 1), :] = value - old_ref[pl.ds(row, 1), :]

    times([blocks_ref.at[0]], [pre], put)
    for neighbor in range(2):
        taken = pick(pre, local_ref[neighbor], NN)
        taken_ref[neighbor] = taken + pick(near_ref[...], outer_ref[neighbor, :count, :], TN)[:size]
    if not earlier:
        more[0][...] = old_ref[...]
    else:
        vectors = [ref[...] for ref in earlier] + [old_ref[...]]
        sums = [jnp.sum(vectors[i] * vectors[j], axis=0, keepdims=True) for i, j in KNOWN]
        more[0][...] = pad_rows(jnp.concatenate(sums, axis=0), HELD)


def inside(blocks, local, outer, old, pre, near, earlier):
    size = old.shape[0]
    more = pltpu.VMEM((HELD, LANES), F32) if earlier else jax.ShapeDtypeStruct(old.shape, F32)
    return pl.pallas_call(
        inside_kernel,
        out_shape=(pltpu.VMEM(old.shape, F32), pltpu.VMEM((2, size, LANES), F32), more),
        in_specs=[VMEM] * (6 + len(earlier)),
        out_specs=[VMEM] * 3,
        compiler_params=limit(6),
        cost_estimate=pl.CostEstimate(flops=0, bytes_accessed=2 * MIB, transcendentals=0),
        name="inside",
    )(*near_core(blocks, local, outer, old, pre, near, *earlier))


def outside(blocks_ref, outer_ref, part_ref, taken_ref, far_ref, new_ref):
    size = part_ref.shape[0]
    count = far_ref.shape[0]
    vectors = [
        taken_ref[neighbor] + pick(far_ref[...], outer_ref[neighbor, count:, :], TN)[:size]
        for neighbor in range(2)
    ]

    def put(row, value):
        new_ref[pl.ds(row, 1), :] = value + part_ref[pl.ds(row, 1), :]

    times([blocks_ref.at[1], blocks_ref.at[2]], vectors, put)


def step_kernel(
    blocks_ref, precond_ref, outer_ref, listed_ref, part_ref, taken_ref, far_ref,
    new_ref, new_pre_ref, send_ref,
):
    outside(blocks_ref, outer_ref, part_ref, taken_ref, far_ref, new_ref)
    precondition(precond_ref, listed_ref, new_ref[...], new_pre_ref, send_ref)


def step(blocks, precond, outer, listed, part, taken, far):
    shape = pltpu.VMEM(part.shape, F32)
    return pl.pallas_call(
        step_kernel,
        out_shape=(shape, shape, pltpu.VMEM(far.shape, F32)),
        in_specs=[VMEM] * 7,
        out_specs=[VMEM] * 3,
        compiler_params=limit(6),
        name="step",
    )(*near_core(blocks, precond, outer, listed, part, taken, far))


def last_kernel(
    blocks_ref, outer_ref, part_ref, taken_ref, far_ref, known_ref, b0_ref, b1_ref, b2_ref, b3_ref,
    new_ref, sums_ref,
):
    outside(blocks_ref, outer_ref, part_ref, taken_ref, far_ref, new_ref)
    new = new_ref[...]
    vectors = [ref[...] for ref in (b0_ref, b1_ref, b2_ref, b3_ref)] + [new]
    sums = [known_ref[...]] + [jnp.sum(v * new, axis=0, keepdims=True) for v in vectors]
    ones = jnp.ones((sums_ref.shape[0], LANES), BF16)
    sums_ref[...] = pick_from(ones, pad_rows(jnp.concatenate(sums, axis=0), LANES))


def last(blocks, outer, part, taken, far, known, basis, parts):
    return pl.pallas_call(
        last_kernel,
        out_shape=(pltpu.VMEM(part.shape, F32), pltpu.VMEM((parts, LANES), F32)),
        in_specs=[VMEM] * 10,
        out_specs=[VMEM] * 2,
        compiler_params=limit(6),
        name="last",
    )(*near_core(blocks, outer, part, taken, far, known, *basis))


def plus(x, y):
    return [a + b for a, b in zip(x, y)]


def tree(terms):
    while len(terms) > 1:
        terms = [sum(terms[k : k + 2]) for k in range(0, len(terms), 2)]
    return terms[0]


def scaled(scale, x):
    return [scale * a for a in x]


def recurrences(product):
    def inner(x, y):
        return tree(
            [a * b * product[min(i, j), max(i, j)] for i, a in enumerate(x) for j, b in enumerate(y)]
        )

    def image_of(x):
        return plus([x[0] * 0.0] + x, x + [x[0] * 0.0])

    one = product[0, 0] * 0.0 + 1.0
    residual = search = shadow = [one]
    answer = []
    alignment = product[0, 0]

    def add(x, y):
        size = max(len(x), len(y))
        zero = one * 0.0
        return plus(x + [zero] * (size - len(x)), y + [zero] * (size - len(y)))

    for iteration in range(2):
        image = image_of(search)
        step_size = alignment / inner(shadow, image)
        middle = add(residual, scaled(-step_size, image))
        middle_image = image_of(middle)
        smoothing = inner(middle_image, middle) / inner(middle_image, middle_image)
        answer = add(answer, add(scaled(step_size, search), scaled(smoothing, middle)))
        residual = add(middle, scaled(-smoothing, middle_image))
        if iteration == 0:
            new_alignment = inner(shadow, residual)
            momentum = new_alignment / alignment * (step_size / smoothing)
            search = add(residual, scaled(momentum, add(search, scaled(-smoothing, image))))
            alignment = new_alignment
    return answer, residual


def finish_kernel(sums_ref, *refs):
    basis, pres, (solution_ref, residual_ref) = refs[:5], refs[5:9], refs[9:]
    totals = jnp.sum(sums_ref[...], axis=0, keepdims=True)
    lane = dict(zip(KNOWN, range(len(KNOWN))))
    lane.update({(i, STEPS): HELD + i for i in range(STEPS + 1)})
    product = {pair: totals[:, k : k + 1] for pair, k in lane.items()}
    answer, residual = recurrences(product)
    solution_ref[...] = sum(a * ref[...] for a, ref in zip(answer, pres))
    residual_ref[...] = sum(a * ref[...] for a, ref in zip(residual, basis))


def finish(sums, basis, pres):
    shape = jax.ShapeDtypeStruct(pres[0].shape, F32)
    return pl.pallas_call(
        finish_kernel,
        out_shape=(shape, shape),
        in_specs=[VMEM] * 10,
        compiler_params=limit(4),
        name="finish",
    )(*near_core(sums, *basis, *pres))


def to_near(send):
    devices = lax.axis_size(DOM)
    return lax.ppermute(send, DOM, [(i, i ^ 1) for i in range(devices)])


def to_far(send, closed):
    devices = lax.axis_size(DOM)
    pairs = [(i, (i + 1) % devices) for i in range(1, devices if closed else devices - 1, 2)]
    return lax.ppermute(send, DOM, pairs + [(j, i) for i, j in pairs])


def to_all(x):
    return lax.all_to_all(x, DOM, split_axis=0, concat_axis=0, tiled=True)


def on_device(
    traction, fluid_coords, struct_coords, dest, target, blocks, columns, halo_list, precond
):
    parts = lax.axis_size(DOM)
    place = lax.axis_index(DOM).astype(jnp.int32).reshape(1)
    force = jnp.transpose(traction, (1, 0, 2))
    fluid = jnp.transpose(fluid_coords, (1, 0, 2))
    coords = struct_coords.reshape(-1, struct_coords.shape[2])
    wanted, slot = slots(dest.reshape(1, -1), target.reshape(1, -1), parts)
    turned, coords, local, outer, listed = prepare(
        halo_list, place, columns, coords, wanted, fluid, force
    )
    onehot, answered = answer(to_all(wanted), coords)
    answered = to_all(answered.reshape(parts, 1, -1)).reshape(answered.shape)
    mapped, blocks, precond = transfer(slot, answered, turned, blocks, precond)
    mapped = to_all(mapped.reshape(parts, 1, -1)).reshape(mapped.shape)
    load, pre, send = start(mapped, onehot, precond, listed)
    basis, pres = [load], [pre]
    for j in range(STEPS):
        far = to_far(send, j < STEPS - 1)
        near = to_near(send)
        earlier = basis[:-1] if j == STEPS - 1 else []
        part, taken, more = inside(blocks, local, outer, basis[-1], pres[-1], near, earlier)
        load_field = more if j == 0 else load_field
        if j < STEPS - 1:
            new, pre, send = step(blocks, precond, outer, listed, part, taken, far)
            pres.append(pre)
        else:
            new, sums = last(blocks, outer, part, taken, far, more, basis, parts)
        basis.append(new)
    solution, residual = finish(to_all(sums), basis, pres)
    return load_field, solution, residual


def solution(mesh):
    in_specs = (
        P(DOM, None, None),
        P(DOM, None, None),
        P(None, None, DOM),
        P(DOM, None),
        P(DOM),
        P(None, None, None, DOM),
        P(None, DOM),
        P(DOM),
        P(None, None, DOM),
    )
    out_specs = (P(None, DOM), P(None, DOM), P(None, DOM))
    return jax.shard_map(
        on_device, mesh=mesh, in_specs=in_specs, out_specs=out_specs, check_vma=False
    )
```
